256 devices in a mesh: seq: 16 (over y_lo, z), tp: 8 (over y_hi, x), dp: 2 (over core).
Axes of the slice: x: 4, y: 4 (y_hi: 2, y_lo: 2; y = y_hi * 2 + y_lo), z: 8, core: 2. Of those that a mesh axis runs over, the one named last changes fastest.
Arguments:
- img_query: bfloat16 [16384, 3072], P(('dp', 'seq'), 'tp'), parts along dimension 0, may hold values from -6 to 6
- img_key: bfloat16 [16384, 3072], P(('dp', 'seq'), 'tp'), parts along dimension 0, may hold values from -6 to 6
- img_value: bfloat16 [16384, 3072], P(('dp', 'seq'), 'tp'), parts along dimension 0, may hold values from -12 to 12
- text_key: bfloat16 [512, 3072], P(('dp', 'seq'), 'tp'), parts along dimension 0, may hold values from -6 to 6
- text_value: bfloat16 [512, 3072], P(('dp', 'seq'), 'tp'), parts along dimension 0, may hold values from -12 to 12
- residual_in: bfloat16 [16384, 3072], P(('dp', 'seq', 'tp')), parts along dimension 0, may hold values from -12 to 12
- mod_shift: float32 [6144], P('dp'), parts along dimension 0, may hold values from -3 to 3
- mod_scale: float32 [6144], P('dp'), parts along dimension 0, may hold values from -0.5 to 0.5
- gate_attn: float32 [6144], P('dp'), parts along dimension 0, may hold values from 0.5 to 1.5
- gate_mlp: float32 [6144], P('dp'), parts along dimension 0, may hold values from 0.5 to 1.5
- out_weight: bfloat16 [3072, 3072], P('tp'), may hold values from -0.109375 to 0.109375
- out_bias: float32 [3072], replicated, may hold values from -3 to 3
- up_weight: bfloat16 [3072, 6144], P(None, 'tp'), may hold values from -0.109375 to 0.109375
- up_bias: float32 [6144], P('tp'), may hold values from -3 to 3
- down_weight: bfloat16 [6144, 3072], P('tp'), may hold values from -0.078125 to 0.078125
- down_bias: float32 [3072], replicated, may hold values from -3 to 3
Outputs:
- stream_out: bfloat16 [16384, 3072], P(('dp', 'seq', 'tp')), parts along dimension 0
The draws below stay inside these ranges and needn't reach their ends.
There are 2 independent parts, one for each index of `dp`. The reference program is written for one: setup_inputs(seed, part) draws one part's arguments, and reference() takes and returns one part's arrays. A program takes and returns all parts, laid end to end along the dimension named above; an argument that names none is the same for every part. Nothing has to cross between parts.
All inputs are finite; a program needn't handle non-finite values.
Results may differ from the reference program's by a relative error of at most 0.015.
Values may be sent and summed in bfloat16 or wider, within the bound.
No kernel may reach another device: no remote copies, remote signals or barrier semaphores. Data moves between devices by JAX's collectives and lax.ppermute only.
A program may use at most 192 MiB of HBM per device.

```python
import math
import jax
import jax.numpy as jnp
from jax import lax

HEADS = 24
HD = 128
D = 3072
FFW = 6144
IMG = 8192
TEXT = 256
N_TP = 8


def draw_img_query(key, part):
    values_drawn = jnp.clip(1.4 * jax.random.normal(jax.random.fold_in(key, 11), (IMG, D), jnp.float32), -6.0, 6.0)
    return values_drawn.astype(jnp.bfloat16)


def draw_img_key(key, part):
    values_drawn = jnp.clip(1.4 * jax.random.normal(jax.random.fold_in(key, 13), (IMG, D), jnp.float32), -6.0, 6.0)
    return values_drawn.astype(jnp.bfloat16)


def draw_residual_in(key, part):
    first, second, third = jax.random.split(jax.random.fold_in(key, 17), 3)
    noise = jnp.clip(jax.random.normal(first, (IMG, D), jnp.float32), -4.0, 4.0)
    column_scale = jnp.exp(jax.random.uniform(second, (D,), jnp.float32) * math.log(10.0))
    row_scale = jnp.exp(jax.random.uniform(third, (IMG, 1), jnp.float32) * math.log(3.0))
    return (0.1 * noise * column_scale[None, :] * row_scale).astype(jnp.bfloat16)


def level_of(key, dims, shards, low, largest):
    def one(position, blocks):
        draws = jax.random.uniform(jax.random.fold_in(jax.random.fold_in(key, 6), position), (blocks,), jnp.float32, low / len(shards), largest / len(shards))
        return jnp.repeat(jnp.exp(draws), dims[position] // blocks).reshape((-1,) + (1,) * (len(dims) - position - 1))

    loudness = one(*shards[0])
    for cut in shards[1:]:
        loudness = loudness * one(*cut)
    return loudness


def normal_values(own_key, extent, deviation, bound, pieces=(), held_as=jnp.bfloat16):
    gain = level_of(own_key, extent, pieces, -0.22, 0.18) if pieces else 1.0
    drawn = jax.random.normal(own_key, extent, jnp.float32) * deviation * gain
    return jnp.minimum(jnp.maximum(drawn, -bound), bound).astype(held_as)


def setup_inputs(seed: int = 0, part: int = 0) -> dict:
    keys = jax.random.split(jax.random.key(seed), 17)
    part_splits = jax.random.split(jax.random.fold_in(keys[16], part), 17)
    img_query = draw_img_query(jax.random.fold_in(jax.random.fold_in(keys[16], part), 71), part)
    img_key = draw_img_key(jax.random.fold_in(jax.random.fold_in(keys[16], part), 71), part)
    img_value = normal_values(part_splits[2], (IMG, D), 3.0, 12.0, ((0, 16), (1, 8)))
    text_key = normal_values(part_splits[3], (TEXT, D), 1.4, 6.0, ((0, 16), (1, 8)))
    text_value = normal_values(part_splits[4], (TEXT, D), 3.0, 12.0, ((0, 16), (1, 8)))
    residual_in = draw_residual_in(jax.random.fold_in(jax.random.fold_in(keys[16], part), 71), part)
    mod_shift = normal_values(part_splits[6], (D,), 0.5, 3.0, (), jnp.float32)
    mod_scale = jnp.clip(jax.random.uniform(part_splits[7], (D,), jnp.float32, -0.5, 0.5), -0.5, 0.5)
    gate_attn = jnp.clip(jax.random.uniform(part_splits[8], (D,), jnp.float32, 0.5, 1.5), 0.5, 1.5)
    gate_mlp = jnp.clip(jax.random.uniform(part_splits[9], (D,), jnp.float32, 0.5, 1.5), 0.5, 1.5)
    out_weight = normal_values(keys[10], (D, D), D ** -0.5, 0.109375, ((0, 8),))
    out_bias = normal_values(keys[11], (D,), 0.5, 3.0, (), jnp.float32)
    up_weight = normal_values(keys[12], (D, FFW), D ** -0.5, 0.109375, ((1, 8),))
    up_bias = normal_values(keys[13], (FFW,), 0.5, 3.0, ((0, 8),), jnp.float32)
    down_weight = normal_values(keys[14], (FFW, D), FFW ** -0.5, 0.078125, ((0, 8),))
    down_bias = normal_values(keys[15], (D,), 0.5, 3.0, (), jnp.float32)
    return dict(img_query=img_query, img_key=img_key, img_value=img_value, text_key=text_key, text_value=text_value, residual_in=residual_in, mod_shift=mod_shift, mod_scale=mod_scale, gate_attn=gate_attn, gate_mlp=gate_mlp, out_weight=out_weight, out_bias=out_bias, up_weight=up_weight, up_bias=up_bias, down_weight=down_weight, down_bias=down_bias)


def attend(img_query, key_rows, value_rows):
    block = math.gcd(IMG, 512)
    queries = img_query.reshape(IMG // block, block, HEADS, HD)
    key_all = key_rows.reshape(-1, HEADS, HD).astype(jnp.float32)
    value_all = value_rows.reshape(-1, HEADS, HD).astype(jnp.float32)

    def one_block(query_block):
        scores = jnp.einsum('bhd,khd->hbk', query_block.astype(jnp.float32), key_all) / math.sqrt(HD)
        top_score = lax.optimization_barrier(jnp.max(scores, axis=-1, keepdims=True))
        expd = jnp.exp(scores - top_score)
        denom = lax.optimization_barrier(jnp.sum(expd, axis=-1))
        rounded = lax.optimization_barrier(expd.astype(jnp.bfloat16)).astype(jnp.float32)
        mixed = jnp.einsum('hbk,khd->bhd', rounded, value_all)
        return mixed / jnp.transpose(denom)[:, :, None]
    result = lax.map(one_block, queries)
    return result.reshape(IMG, D).astype(jnp.bfloat16)

def grouped_sum(left, right):
    width = left.shape[1] // N_TP
    accum = jnp.zeros((left.shape[0], right.shape[1]), jnp.float32)
    for group in range(N_TP):
        partial_term = jnp.dot(left[:, group * width:(group + 1) * width], right[group * width:(group + 1) * width, :], preferred_element_type=jnp.float32)
        accum = accum + lax.optimization_barrier(partial_term.astype(jnp.bfloat16)).astype(jnp.float32)
    return accum

def reference(img_query, img_key, img_value, text_key, text_value, residual_in, mod_shift, mod_scale, gate_attn, gate_mlp, out_weight, out_bias, up_weight, up_bias, down_weight, down_bias):
    key_rows = jnp.concatenate([img_key, text_key], axis=0)
    value_rows = jnp.concatenate([img_value, text_value], axis=0)
    attended = attend(img_query, key_rows, value_rows)
    proj = grouped_sum(attended, out_weight)
    stream = residual_in.astype(jnp.float32) + gate_attn * (proj + out_bias)
    center = lax.optimization_barrier(jnp.mean(stream, axis=-1, keepdims=True))
    spread = lax.optimization_barrier(jnp.mean((stream - center) ** 2, axis=-1, keepdims=True))
    normed = ((stream - center) * lax.rsqrt(spread + 1e-06) * (1.0 + mod_scale) + mod_shift).astype(jnp.bfloat16)
    hidden = jax.nn.gelu(jnp.dot(normed, up_weight, preferred_element_type=jnp.float32) + up_bias, approximate=True).astype(jnp.bfloat16)
    mlp = grouped_sum(hidden, down_weight)
    return (stream + gate_mlp * (mlp + down_bias)).astype(jnp.bfloat16)
```

```python
import functools
import math

import jax
import jax.numpy as jnp
from jax import lax
from jax.experimental import pallas as pl
from jax.experimental.pallas import tpu as pltpu
from jax.sharding import Mesh, PartitionSpec as P

HD = 128
LOG2E = math.log2(math.e)
SCORE_TO_LOG2 = LOG2E / math.sqrt(HD)

FINE = (("yl", 2), ("z", 8), ("yh", 2), ("x", 4), ("dp", 2))


def attend_body(pieces, first, last, *refs):
    q_ref = refs[0]
    k_refs = refs[1 : 1 + pieces]
    v_refs = refs[1 + pieces : 1 + 2 * pieces]
    at = 1 + 2 * pieces
    if not first:
        m_in, l_in, acc_in = refs[at : at + 3]
        at += 3
    outs = refs[at:]
    q = q_ref[...]
    scores = [
        lax.dot_general(k[...], q, (((1,), (1,)), ((), ())), preferred_element_type=jnp.float32)
        for k in k_refs
    ]
    m = functools.reduce(jnp.maximum, [jnp.max(s, axis=0, keepdims=True) for s in scores])
    if not first:
        m_old = m_in[0]
        m = jnp.maximum(m, m_old)
    den = None
    acc = None
    for s, v in zip(scores, v_refs):
        e = jnp.exp2((s - m) * SCORE_TO_LOG2)
        part = jnp.sum(e, axis=0, keepdims=True)
        den = part if den is None else den + part
        mixed = lax.dot_general(
            v[...],
            e.astype(jnp.bfloat16),
            (((0,), (0,)), ((), ())),
            preferred_element_type=jnp.float32,
        )
        acc = mixed if acc is None else acc + mixed
    if not first:
        factor = jnp.exp2((m_old - m) * SCORE_TO_LOG2)
        den = den + factor * l_in[0]
        acc = acc + factor * acc_in[...]
    if last:
        o_ref, lse_ref = outs
        o_ref[...] = (acc / den).T.astype(jnp.bfloat16)
        lse_ref[0] = m * SCORE_TO_LOG2 + jnp.log2(den)
    else:
        m_out, l_out, acc_out = outs
        m_out[0] = m
        l_out[0] = den
        acc_out[...] = acc


def attend(q, ks, vs, state, last, block=512):
    rows, width = q.shape
    heads = width // HD
    first = state is None
    q_spec = pl.BlockSpec((block, HD), lambda h, j: (j, h))
    kv_specs = [pl.BlockSpec((k.shape[0], HD), lambda h, j: (0, h)) for k in ks]
    stat = pl.BlockSpec((1, 1, block), lambda h, j: (h, 0, j))
    acc = pl.BlockSpec((HD, block), lambda h, j: (h, j))
    stat_shape = jax.ShapeDtypeStruct((heads, 1, rows), jnp.float32)
    if last:
        out_specs = [q_spec, stat]
        out_shape = [jax.ShapeDtypeStruct((rows, width), jnp.bfloat16), stat_shape]
    else:
        out_specs = [stat, stat, acc]
        out_shape = [stat_shape, stat_shape, jax.ShapeDtypeStruct((width, rows), jnp.float32)]
    keys = sum(k.shape[0] for k in ks)
    return pl.pallas_call(
        functools.partial(attend_body, len(ks), first, last),
        grid=(heads, rows // block),
        in_specs=[q_spec, *kv_specs, *kv_specs, *(() if first else (stat, stat, acc))],
        out_specs=out_specs,
        out_shape=out_shape,
        cost_estimate=pl.CostEstimate(
            flops=4 * rows * keys * width,
            transcendentals=rows * keys * heads,
            bytes_accessed=2 * (rows + 2 * keys) * width,
        ),
        compiler_params=pltpu.CompilerParams(vmem_limit_bytes=48 << 20),
    )(q, *ks, *vs, *(() if first else state))


def shift(array, axis, size, by):
    return lax.ppermute(array, axis, [(i, (i + by) % size) for i in range(size)])


def cross(array):
    return lax.ppermute(array, ("yl", "yh"), [(0, 3), (3, 0), (1, 2), (2, 1)])


def half_of(array, index, axis):
    n = array.shape[axis] // 2
    return lax.dynamic_slice_in_dim(array, index * n, n, axis)


def gather_x(rows):
    n = rows.shape[0] // 2
    left = shift(rows, "x", 4, 1)
    right = shift(rows, "x", 4, 3)
    far = jnp.concatenate([shift(left[:n], "x", 4, 1), shift(right[n:], "x", 4, 3)], axis=0)
    return rows, left, right, far


def shards(
    img_query,
    img_key,
    img_value,
    text_key,
    text_value,
    residual_in,
    mod_shift,
    mod_scale,
    gate_attn,
    gate_mlp,
    out_weight,
    out_bias,
    up_weight,
    up_bias,
    down_weight,
    down_bias,
):
    core = lax.axis_index("dp")
    x_at = lax.axis_index("x")
    rows_own, width = img_query.shape
    row_block = residual_in.shape[0]
    d_model = residual_in.shape[1]

    up_mine = cross(half_of(up_weight, core, 0))
    down_mine = cross(half_of(down_weight, core, 0))
    bias_other = cross(up_bias)
    up_mate = shift(up_mine, "dp", 2, 1)
    down_mate = shift(down_mine, "dp", 2, 1)

    queries = jnp.concatenate([img_query, shift(img_query, "yl", 2, 1)], axis=0)
    keys = jnp.concatenate([img_key, text_key], axis=0)
    values = jnp.concatenate([img_value, text_value], axis=0)
    cut = -(-keys.shape[0] // 32) * 16
    state = attend(queries, [keys], [values], None, False)
    k_up = k_down = keys
    v_up = v_down = values
    for _ in range(3):
        k_up, k_down = shift(k_up, "z", 8, 1), shift(k_down, "z", 8, 7)
        v_up, v_down = shift(v_up, "z", 8, 1), shift(v_down, "z", 8, 7)
        state = attend(queries, [k_up, k_down], [v_up, v_down], state, False)
    k_up, k_down = shift(k_up[:cut], "z", 8, 1), shift(k_down[cut:], "z", 8, 7)
    v_up, v_down = shift(v_up[:cut], "z", 8, 1), shift(v_down[cut:], "z", 8, 7)
    part, lse = attend(queries, [k_up, k_down], [v_up, v_down], state, True)

    part_other = shift(part[rows_own:], "yl", 2, 1)
    lse_other = shift(lse[:, :, rows_own:], "yl", 2, 1)
    share = 1.0 / (1.0 + jnp.exp2(lse_other - lse[:, :, :rows_own]))
    share = jnp.repeat(share[:, 0, :].T, HD, axis=1)
    part_own = part[:rows_own].astype(jnp.float32)
    part_other = part_other.astype(jnp.float32)
    attended = (part_other + share * (part_own - part_other)).astype(jnp.bfloat16)

    terms = jnp.dot(attended, out_weight, preferred_element_type=jnp.float32).astype(jnp.bfloat16)
    terms = lax.all_to_all(
        terms.reshape(8, row_block, d_model), ("yh", "x"), split_axis=0, concat_axis=0, tiled=True
    )
    proj = jnp.sum(terms.astype(jnp.float32), axis=0)
    stream = residual_in.astype(jnp.float32) + gate_attn * (proj + out_bias)
    center = jnp.mean(stream, axis=-1, keepdims=True)
    spread = jnp.mean((stream - center) ** 2, axis=-1, keepdims=True)
    normed = ((stream - center) * lax.rsqrt(spread + 1e-06) * (1.0 + mod_scale) + mod_shift).astype(
        jnp.bfloat16
    )

    everyone = jnp.concatenate(gather_x(normed), axis=0)
    half = d_model // 2
    near = jnp.dot(everyone, up_weight, preferred_element_type=jnp.float32) + up_bias
    cols_mine = lax.dynamic_slice_in_dim(everyone, core * half, half, 1)
    cols_mate = lax.dynamic_slice_in_dim(everyone, (1 - core) * half, half, 1)
    away = (
        jnp.dot(cols_mine, up_mine, preferred_element_type=jnp.float32)
        + jnp.dot(cols_mate, up_mate, preferred_element_type=jnp.float32)
        + bias_other
    )
    near = jax.nn.gelu(near, approximate=True).astype(jnp.bfloat16)
    away = jax.nn.gelu(away, approximate=True).astype(jnp.bfloat16)
    half = away.shape[1] // 2
    away_mine = lax.dynamic_slice_in_dim(away, core * half, half, 1)
    away_mate = lax.dynamic_slice_in_dim(away, (1 - core) * half, half, 1)
    out = (
        jnp.dot(near, down_weight, preferred_element_type=jnp.float32)
        + jnp.dot(away_mine, down_mine, preferred_element_type=jnp.float32)
        + jnp.dot(away_mate, down_mate, preferred_element_type=jnp.float32)
    ).astype(jnp.bfloat16)
    blocks = out.reshape(4, row_block, d_model)
    mlp = blocks[0].astype(jnp.float32)
    mlp = mlp + shift(blocks[1], "x", 4, 3).astype(jnp.float32)
    mlp = mlp + shift(blocks[2], "x", 4, 1).astype(jnp.float32)
    mlp = mlp + shift(blocks[3], "x", 4, 2).astype(jnp.float32)
    return (stream + gate_mlp * (mlp + down_bias)).astype(jnp.bfloat16)


def solution(mesh):
    fine = Mesh(mesh.devices.reshape([n for _, n in FINE]), [name for name, _ in FINE])
    seq, tp = ("yl", "z"), ("yh", "x")
    tokens = P(("dp", *seq), tp)
    rows = P(("dp", *seq, *tp), None)
    in_specs = (
        tokens,
        tokens,
        tokens,
        tokens,
        tokens,
        rows,
        P("dp"),
        P("dp"),
        P("dp"),
        P("dp"),
        P(tp, None),
        P(),
        P(None, tp),
        P(tp),
        P(tp, None),
        P(),
    )
    return jax.shard_map(shards, mesh=fine, in_specs=in_specs, out_specs=rows, check_vma=False)
```

```python
import functools
import math

import jax
import jax.numpy as jnp
from jax import lax
from jax.experimental import pallas as pl
from jax.experimental.pallas import tpu as pltpu
from jax.sharding import Mesh, PartitionSpec as P

HD = 128
LOG2E = math.log2(math.e)
SCORE_TO_LOG2 = LOG2E / math.sqrt(HD)

FINE = (("yl", 2), ("z", 8), ("yh", 2), ("x", 4), ("dp", 2))


def attend_body(pieces, first, last, *refs):
    q_ref = refs[0]
    k_refs = refs[1 : 1 + pieces]
    v_refs = refs[1 + pieces : 1 + 2 * pieces]
    at = 1 + 2 * pieces
    if not first:
        m_in, l_in, acc_in = refs[at : at + 3]
        at += 3
    outs = refs[at:]
    q = q_ref[...]
    scores = [
        lax.dot_general(k[...], q, (((1,), (1,)), ((), ())), preferred_element_type=jnp.float32)
        for k in k_refs
    ]
    m = functools.reduce(jnp.maximum, [jnp.max(s, axis=0, keepdims=True) for s in scores])
    if not first:
        m_old = m_in[0]
        m = jnp.maximum(m, m_old)
    den = None
    acc = None
    for s, v in zip(scores, v_refs):
        e = jnp.exp2((s - m) * SCORE_TO_LOG2)
        part = jnp.sum(e, axis=0, keepdims=True)
        den = part if den is None else den + part
        mixed = lax.dot_general(
            v[...],
            e.astype(jnp.bfloat16),
            (((0,), (0,)), ((), ())),
            preferred_element_type=jnp.float32,
        )
        acc = mixed if acc is None else acc + mixed
    if not first:
        factor = jnp.exp2((m_old - m) * SCORE_TO_LOG2)
        den = den + factor * l_in[0]
        acc = acc + factor * acc_in[...]
    if last:
        o_ref, lse_ref = outs
        o_ref[...] = (acc / den).T.astype(jnp.bfloat16)
        lse_ref[0] = m * SCORE_TO_LOG2 + jnp.log2(den)
    else:
        m_out, l_out, acc_out = outs
        m_out[0] = m
        l_out[0] = den
        acc_out[...] = acc


def attend(q, pairs, state, last, block=512):
    rows, width = q.shape
    heads = width // HD
    ks = vs = pairs
    first = state is None
    q_spec = pl.BlockSpec((block, HD), lambda h, j: (j, h))
    k_specs = [pl.BlockSpec((k.shape[0], HD), lambda h, j: (0, h)) for k in ks]
    v_specs = [pl.BlockSpec((v.shape[0], HD), lambda h, j: (0, heads + h)) for v in vs]
    stat = pl.BlockSpec((1, 1, block), lambda h, j: (h, 0, j))
    acc = pl.BlockSpec((HD, block), lambda h, j: (h, j))
    stat_shape = jax.ShapeDtypeStruct((heads, 1, rows), jnp.float32)
    if last:
        out_specs = [q_spec, stat]
        out_shape = [jax.ShapeDtypeStruct((rows, width), jnp.bfloat16), stat_shape]
    else:
        out_specs = [stat, stat, acc]
        out_shape = [stat_shape, stat_shape, jax.ShapeDtypeStruct((width, rows), jnp.float32)]
    keys = sum(k.shape[0] for k in ks)
    return pl.pallas_call(
        functools.partial(attend_body, len(ks), first, last),
        grid=(heads, rows // block),
        in_specs=[q_spec, *k_specs, *v_specs, *(() if first else (stat, stat, acc))],
        out_specs=out_specs,
        out_shape=out_shape,
        cost_estimate=pl.CostEstimate(
            flops=4 * rows * keys * width,
            transcendentals=rows * keys * heads,
            bytes_accessed=2 * (rows + 2 * keys) * width,
        ),
        compiler_params=pltpu.CompilerParams(vmem_limit_bytes=48 << 20),
    )(q, *ks, *vs, *(() if first else state))


def join_project_body(part_ref, other_ref, lse_ref, lse_other_ref, weight_ref, out_ref):
    pieces = []
    for h in range(part_ref.shape[1] // HD):
        cols = slice(h * HD, (h + 1) * HD)
        share = 1.0 / (1.0 + jnp.exp2(lse_other_ref[h] - lse_ref[h]))
        share = jnp.broadcast_to(share, (HD, share.shape[1])).T
        own = part_ref[:, cols].astype(jnp.float32)
        other = other_ref[:, cols].astype(jnp.float32)
        pieces.append((other + share * (own - other)).astype(jnp.bfloat16))
    attended = jnp.concatenate(pieces, axis=1)
    out_ref[...] = jnp.dot(
        attended, weight_ref[...], preferred_element_type=jnp.float32
    ).astype(jnp.bfloat16)


def join_project(part, other, lse, lse_other, weight, block=768):
    rows, width = other.shape
    cols = weight.shape[1]
    first = pl.BlockSpec((rows, width), lambda j: (0, 0))
    stat = pl.BlockSpec((lse.shape[0], 1, rows), lambda j: (0, 0, 0))
    return pl.pallas_call(
        join_project_body,
        grid=(cols // block,),
        in_specs=[first, first, stat, stat, pl.BlockSpec((width, block), lambda j: (0, j))],
        out_specs=pl.BlockSpec((rows, block), lambda j: (0, j)),
        out_shape=jax.ShapeDtypeStruct((rows, cols), jnp.bfloat16),
        cost_estimate=pl.CostEstimate(
            flops=2 * rows * width * cols, transcendentals=0, bytes_accessed=2 * width * cols
        ),
        compiler_params=pltpu.CompilerParams(vmem_limit_bytes=32 << 20),
    )(part, other, lse, lse_other, weight)


def stream_norm_body(
    terms_ref, residual_ref, gate_ref, bias_ref, scale_ref, shift_ref, stream_ref, normed_ref
):
    proj = terms_ref[0].astype(jnp.float32)
    for g in range(1, terms_ref.shape[0]):
        proj = proj + terms_ref[g].astype(jnp.float32)
    stream = residual_ref[...].astype(jnp.float32) + gate_ref[...] * (proj + bias_ref[...])
    center = jnp.mean(stream, axis=-1, keepdims=True)
    off = stream - center
    spread = jnp.mean(off * off, axis=-1, keepdims=True)
    normed = off * lax.rsqrt(spread + 1e-06) * (1.0 + scale_ref[...]) + shift_ref[...]
    stream_ref[...] = stream
    normed_ref[...] = normed.astype(jnp.bfloat16)


def stream_norm(terms, residual, gate, bias, scale, shift_by, block=16):
    groups, rows, d_model = terms.shape
    row = pl.BlockSpec((block, d_model), lambda i: (i, 0))
    vec = pl.BlockSpec((1, d_model), lambda i: (0, 0))
    return pl.pallas_call(
        stream_norm_body,
        grid=(rows // block,),
        in_specs=[pl.BlockSpec((groups, block, d_model), lambda i: (0, i, 0)), row, vec, vec, vec, vec],
        out_specs=[row, row],
        out_shape=[
            jax.ShapeDtypeStruct((rows, d_model), jnp.float32),
            jax.ShapeDtypeStruct((rows, d_model), jnp.bfloat16),
        ],
        cost_estimate=pl.CostEstimate(
            flops=20 * rows * d_model, transcendentals=0, bytes_accessed=24 * rows * d_model
        ),
        compiler_params=pltpu.CompilerParams(vmem_limit_bytes=32 << 20),
    )(terms, residual, *(v.reshape(1, -1) for v in (gate, bias, scale, shift_by)))


def mlp_body(order, x_ref, up_ref, down_ref, bias_ref, bias_far_ref, *refs):
    n = 4
    up_far, down_far, out_ref = refs[:n], refs[n : n + 2], refs[n + 2]
    near, far, hid_near, hid_far, up_buf, down_buf, sems = refs[n + 3 :]
    i = pl.program_id(0)
    quarter = up_ref.shape[0]

    def copies():
        for j in range(n):
            yield pltpu.make_async_copy(up_far[j], up_buf.at[j], sems.at[j])
        for j in range(n):
            cols = pl.ds((j % 2) * quarter, quarter)
            yield pltpu.make_async_copy(down_far[j // 2].at[:, cols], down_buf.at[j], sems.at[n + j])

    @pl.when(i == 0)
    def _():
        for copy in copies():
            copy.start()
        near[...] = jnp.broadcast_to(bias_ref[...], near.shape)
        far[...] = jnp.broadcast_to(bias_far_ref[...], far.shape)

    for j, copy in enumerate(copies()):

        @pl.when(i == j)
        def _(copy=copy):
            copy.wait()

    @pl.when(i < n)
    def _():
        at = pl.multiple_of(i * quarter, quarter)
        near[...] += jnp.dot(
            x_ref[:, pl.ds(at, quarter)], up_ref[...], preferred_element_type=jnp.float32
        )
        at = pl.multiple_of(order[i] * quarter, quarter)
        far[...] += jnp.dot(
            x_ref[:, pl.ds(at, quarter)], up_buf[i], preferred_element_type=jnp.float32
        )

    @pl.when(i == n - 1)
    def _():
        hid_near[...] = jax.nn.gelu(near[...], approximate=True).astype(jnp.bfloat16)
        hid_far[...] = jax.nn.gelu(far[...], approximate=True).astype(jnp.bfloat16)

    @pl.when(i >= n)
    def _():
        out_ref[...] = (
            jnp.dot(hid_near[...], down_ref[...], preferred_element_type=jnp.float32)
            + jnp.dot(hid_far[...], down_buf[i - n], preferred_element_type=jnp.float32)
        ).astype(jnp.bfloat16)


def mlp(x, up, down, bias, bias_far, up_far, down_far, order):
    rows, d_model = x.shape
    hidden = up.shape[1]
    n = len(up_far)
    quarter = d_model // n
    whole = lambda i, order: (0, 0)
    column = lambda i, order: (0, order[jnp.maximum(i, n)])
    far_spec = pl.BlockSpec(memory_space=pltpu.MemorySpace.HBM)
    return pl.pallas_call(
        mlp_body,
        grid_spec=pltpu.PrefetchScalarGridSpec(
            num_scalar_prefetch=1,
            grid=(2 * n,),
            in_specs=[
                pl.BlockSpec((rows, d_model), whole),
                pl.BlockSpec((quarter, hidden), lambda i, order: (jnp.minimum(i, n - 1), 0)),
                pl.BlockSpec((hidden, quarter), column),
                pl.BlockSpec((1, hidden), whole),
                pl.BlockSpec((1, hidden), whole),
                *[far_spec] * (n + 2),
            ],
            out_specs=pl.BlockSpec((rows, quarter), column),
            scratch_shapes=[
                pltpu.VMEM((rows, hidden), jnp.float32),
                pltpu.VMEM((rows, hidden), jnp.float32),
                pltpu.VMEM((rows, hidden), jnp.bfloat16),
                pltpu.VMEM((rows, hidden), jnp.bfloat16),
                pltpu.VMEM((n, quarter, hidden), jnp.bfloat16),
                pltpu.VMEM((n, hidden, quarter), jnp.bfloat16),
                pltpu.SemaphoreType.DMA((2 * n,)),
            ],
        ),
        out_shape=jax.ShapeDtypeStruct((rows, d_model), jnp.bfloat16),
        cost_estimate=pl.CostEstimate(
            flops=8 * rows * d_model * hidden,
            transcendentals=rows * hidden * 2,
            bytes_accessed=8 * d_model * hidden,
        ),
        compiler_params=pltpu.CompilerParams(vmem_limit_bytes=40 << 20),
    )(order, x, up, down, bias.reshape(1, -1), bias_far.reshape(1, -1), *up_far, *down_far)


def shift(array, axis, size, by):
    return lax.ppermute(array, axis, [(i, (i + by) % size) for i in range(size)])


def cross(array):
    return lax.ppermute(array, ("yl", "yh"), [(0, 3), (3, 0), (1, 2), (2, 1)])


def part_of(array, parts, index, axis):
    n = array.shape[axis] // parts
    return lax.dynamic_slice_in_dim(array, index * n, n, axis)


tie = lax.optimization_barrier


def gather_x(rows):
    n = rows.shape[0] // 2
    left = shift(rows, "x", 4, 1)
    right = shift(rows, "x", 4, 3)
    far = jnp.concatenate([shift(left[:n], "x", 4, 1), shift(right[n:], "x", 4, 3)], axis=0)
    return rows, left, right, far


def shards(
    img_query,
    img_key,
    img_value,
    text_key,
    text_value,
    residual_in,
    mod_shift,
    mod_scale,
    gate_attn,
    gate_mlp,
    out_weight,
    out_bias,
    up_weight,
    up_bias,
    down_weight,
    down_bias,
):
    yl_at, core = lax.axis_index("yl"), lax.axis_index("dp")
    rows_own = img_query.shape[0]
    row_block, d_model = residual_in.shape

    up_a = cross(part_of(up_weight, 4, yl_at * 2 + core, 0))
    down_a = cross(part_of(down_weight, 2, core, 1))
    order = jnp.bitwise_xor(
        jnp.array([2, 2, 2, 2, 0, 0, 0, 0], jnp.int32) * (1 - yl_at)
        + core * jnp.array([1, 1, 1, 1, 2, 2, 2, 2], jnp.int32),
        jnp.array([0, 2, 1, 3, 0, 1, 2, 3], jnp.int32),
    )

    q_other = shift(img_query, "yl", 2, 1)
    own = jnp.concatenate(
        [
            jnp.concatenate([img_key, text_key], axis=0),
            jnp.concatenate([img_value, text_value], axis=0),
        ],
        axis=1,
    )
    cut = -(-own.shape[0] // 32) * 16

    def around(up, down):
        return [shift(up, "z", 8, 1), shift(down, "z", 8, 7)]

    one = around(own, own)
    one, q_other = tie((one, q_other))
    queries = jnp.concatenate([img_query, q_other], axis=0)
    two = around(*one)
    state = attend(queries, [own], None, False)
    state = attend(queries, one, state, False)
    two, state, up_a = tie((two, state, up_a))
    three = around(*two)
    up_b = shift(up_a, "yl", 2, 1)
    state = attend(queries, two, state, False)
    three, state = tie((three, state))
    four = around(three[0][:cut], three[1][cut:])
    state = attend(queries, three, state, False)
    four, state = tie((four, state))
    part, lse = attend(queries, four, state, True)
    part, up_b, down_a = tie((part, up_b, down_a))

    part_other = shift(part[rows_own:], "yl", 2, 1)
    lse_other = shift(lse[:, :, rows_own:], "yl", 2, 1)
    terms = join_project(part, part_other, lse, lse_other, out_weight)
    terms = lax.all_to_all(
        terms.reshape(8, row_block, d_model), ("yh", "x"), split_axis=0, concat_axis=0, tiled=True
    )
    up_far = [up_a, up_b, shift(up_a, "dp", 2, 1), shift(up_b, "dp", 2, 1)]
    down_far = [down_a, shift(down_a, "dp", 2, 1)]
    bias_far = cross(up_bias)
    terms, up_far, down_far, bias_far = tie((terms, up_far, down_far, bias_far))
    stream, normed = stream_norm(terms, residual_in, gate_attn, out_bias, mod_scale, mod_shift)
    everyone = jnp.concatenate(gather_x(normed), axis=0)
    out = mlp(everyone, up_weight, down_weight, up_bias, bias_far, up_far, down_far, order)
    blocks = out.reshape(4, row_block, d_model)
    total = blocks[0].astype(jnp.float32)
    total = total + shift(blocks[1], "x", 4, 3).astype(jnp.float32)
    total = total + shift(blocks[2], "x", 4, 1).astype(jnp.float32)
    total = total + shift(blocks[3], "x", 4, 2).astype(jnp.float32)
    return (stream + gate_mlp * (total + down_bias)).astype(jnp.bfloat16)


def solution(mesh):
    fine = Mesh(mesh.devices.reshape([n for _, n in FINE]), [name for name, _ in FINE])
    seq, tp = ("yl", "z"), ("yh", "x")
    tokens = P(("dp", *seq), tp)
    rows = P(("dp", *seq, *tp), None)
    in_specs = (
        tokens,
        tokens,
        tokens,
        tokens,
        tokens,
        rows,
        P("dp"),
        P("dp"),
        P("dp"),
        P("dp"),
        P(tp, None),
        P(),
        P(None, tp),
        P(tp),
        P(tp, None),
        P(),
    )
    return jax.shard_map(shards, mesh=fine, in_specs=in_specs, out_specs=rows, check_vma=False)
```

```python
import functools
import math

import jax
import jax.numpy as jnp
from jax import lax
from jax.experimental import pallas as pl
from jax.experimental.pallas import tpu as pltpu
from jax.sharding import Mesh, PartitionSpec as P

HD = 128
LOG2E = math.log2(math.e)
SCORE_TO_LOG2 = LOG2E / math.sqrt(HD)

FINE = (("yl", 2), ("z", 8), ("yh", 2), ("x", 4), ("dp", 2))


def store_part(o_ref, part, lse):
    h = pl.program_id(1)
    terms = []
    rest = lse
    for _ in range(3):
        terms.append(rest.astype(jnp.bfloat16).astype(jnp.float32))
        rest = rest - terms[-1]
    row = lax.broadcasted_iota(jnp.int32, (HD, lse.shape[1]), 0) - 3 * h
    stats = jnp.zeros((HD, lse.shape[1]), jnp.float32)
    for k, term in enumerate(terms):
        stats = jnp.where(row == k, term, stats)
    stats = stats.T.astype(jnp.bfloat16)
    _, x_size, yh_size, rows, width = o_ref.shape
    for x in range(x_size):
        for yh in range(yh_size):
            at = slice((yh * x_size + x) * rows, (yh * x_size + x + 1) * rows)
            o_ref[0, x, yh, :, pl.ds(pl.multiple_of(h * HD, HD), HD)] = part[at]

            @pl.when(h == 0)
            def _(x=x, yh=yh, at=at):
                o_ref[0, x, yh, :, width - HD :] = stats[at]

            @pl.when(h > 0)
            def _(x=x, yh=yh, at=at):
                o_ref[0, x, yh, :, width - HD :] += stats[at]


def attend_body(pieces, first, last, *refs):
    q_ref = refs[0]
    k_refs = refs[1 : 1 + pieces]
    v_refs = refs[1 + pieces : 1 + 2 * pieces]
    at = 1 + 2 * pieces
    if not first:
        m_in, l_in, acc_in = refs[at : at + 3]
        at += 3
    outs = refs[at:]
    q = q_ref[...]
    scores = [
        lax.dot_general(k[...], q, (((1,), (1,)), ((), ())), preferred_element_type=jnp.float32)
        for k in k_refs
    ]
    m = functools.reduce(jnp.maximum, [jnp.max(s, axis=0, keepdims=True) for s in scores])
    if not first:
        m_old = m_in[0]
        m = jnp.maximum(m, m_old)
    den = None
    acc = None
    for s, v in zip(scores, v_refs):
        e = jnp.exp2((s - m) * SCORE_TO_LOG2)
        part = jnp.sum(e, axis=0, keepdims=True)
        den = part if den is None else den + part
        mixed = lax.dot_general(
            v[...],
            e.astype(jnp.bfloat16),
            (((0,), (0,)), ((), ())),
            preferred_element_type=jnp.float32,
        )
        acc = mixed if acc is None else acc + mixed
    if not first:
        factor = jnp.exp2((m_old - m) * SCORE_TO_LOG2)
        den = den + factor * l_in[0]
        acc = acc + factor * acc_in[...]
    if last:
        store_part(outs[0], (acc / den).T.astype(jnp.bfloat16), m * SCORE_TO_LOG2 + jnp.log2(den))
    else:
        m_out, l_out, acc_out = outs
        m_out[0] = m
        l_out[0] = den
        acc_out[...] = acc


def attend(q, pairs, state, last=None, block=512):
    rows, width = q.shape
    heads = width // HD
    ks = vs = pairs
    first = state is None
    if last:
        grid, at = (rows // block, heads), lambda f: lambda j, h: f(h, j)
    else:
        grid, at = (heads, rows // block), lambda f: f
    q_spec = pl.BlockSpec((block, HD), at(lambda h, j: (j, h)))
    k_specs = [pl.BlockSpec((k.shape[0], HD), at(lambda h, j: (0, h))) for k in ks]
    v_specs = [pl.BlockSpec((v.shape[0], HD), at(lambda h, j: (0, heads + h))) for v in vs]
    stat = pl.BlockSpec((1, 1, block), at(lambda h, j: (h, 0, j)))
    acc = pl.BlockSpec((HD, block), at(lambda h, j: (h, j)))
    if last:
        out_specs = [pl.BlockSpec((1, *last[1:]), at(lambda h, j: (j, 0, 0, 0, 0)))]
        out_shape = [jax.ShapeDtypeStruct(last, jnp.bfloat16)]
    else:
        stat_shape = jax.ShapeDtypeStruct((heads, 1, rows), jnp.float32)
        out_specs = [stat, stat, acc]
        out_shape = [stat_shape, stat_shape, jax.ShapeDtypeStruct((width, rows), jnp.float32)]
    keys = sum(k.shape[0] for k in ks)
    return pl.pallas_call(
        functools.partial(attend_body, len(ks), first, bool(last)),
        grid=grid,
        in_specs=[q_spec, *k_specs, *v_specs, *(() if first else (stat, stat, acc))],
        out_specs=out_specs,
        out_shape=out_shape,
        cost_estimate=pl.CostEstimate(
            flops=4 * rows * keys * width,
            transcendentals=rows * keys * heads,
            bytes_accessed=2 * (rows + 2 * keys) * width,
        ),
        compiler_params=pltpu.CompilerParams(vmem_limit_bytes=48 << 20),
    )(q, *ks, *vs, *(() if first else state))


def join_project_body(order, yh, part_ref, mine_ref, mate_ref, own_ref, away_ref, attended):
    i = pl.program_id(0)
    x_size = part_ref.shape[0] // 2
    rows = part_ref.shape[1] // 2
    width = part_ref.shape[2] - HD

    @pl.when(i == 0)
    def _():
        for side in range(2):
            at = pl.ds(pl.multiple_of((yh[0] if side == 0 else 1 - yh[0]) * rows, rows), rows)
            for x in range(x_size):
                a = part_ref[x, at, :].astype(jnp.float32)
                b = part_ref[x_size + x, at, :].astype(jnp.float32)
                for h in range(width // HD):
                    k = width + 3 * h
                    lse_a = a[:, k : k + 1] + a[:, k + 1 : k + 2] + a[:, k + 2 : k + 3]
                    lse_b = b[:, k : k + 1] + b[:, k + 1 : k + 2] + b[:, k + 2 : k + 3]
                    share = 1.0 / (1.0 + jnp.exp2(lse_b - lse_a))
                    cols = slice(h * HD, (h + 1) * HD)
                    joined = b[:, cols] + share * (a[:, cols] - b[:, cols])
                    attended[
                        side * rows : (side + 1) * rows, x * width + h * HD : x * width + (h + 1) * HD
                    ] = joined.astype(jnp.bfloat16)

    def project(weight_ref):
        out = jnp.dot(attended[...], weight_ref[...], preferred_element_type=jnp.float32)
        own_ref[...] = out[:rows]
        away_ref[...] = out[rows:].astype(jnp.bfloat16)

    @pl.when(i < 2)
    def _():
        project(mine_ref)

    @pl.when(i >= 2)
    def _():
        project(mate_ref)


def join_project(parts, mine, mate, order, yh):
    n, both, wide = parts.shape
    k, half = mine.shape
    block, rows = half // 2, both // 2
    out = pl.BlockSpec((rows, block), lambda i, order, yh: (0, order[i]))
    return pl.pallas_call(
        join_project_body,
        grid_spec=pltpu.PrefetchScalarGridSpec(
            num_scalar_prefetch=2,
            grid=(4,),
            in_specs=[
                pl.BlockSpec((n, both, wide), lambda i, order, yh: (0, 0, 0)),
                pl.BlockSpec((k, block), lambda i, order, yh: (0, jnp.minimum(i, 1))),
                pl.BlockSpec((k, block), lambda i, order, yh: (0, jnp.maximum(i - 2, 0))),
            ],
            out_specs=[out, out],
            scratch_shapes=[pltpu.VMEM((both, k), jnp.bfloat16)],
        ),
        out_shape=[
            jax.ShapeDtypeStruct((rows, 2 * half), jnp.float32),
            jax.ShapeDtypeStruct((rows, 2 * half), jnp.bfloat16),
        ],
        cost_estimate=pl.CostEstimate(
            flops=4 * both * k * half, transcendentals=0, bytes_accessed=4 * k * half
        ),
        compiler_params=pltpu.CompilerParams(vmem_limit_bytes=40 << 20),
    )(order, yh, parts, mine, mate)


def stream_norm_body(own_ref, other_ref, residual_ref, vectors_ref, stream_ref, normed_ref):
    gate, bias, scale, shift_by = (vectors_ref[i : i + 1, :] for i in range(4))
    proj = own_ref[...] + other_ref[...].astype(jnp.float32)
    stream = residual_ref[...].astype(jnp.float32) + gate * (proj + bias)
    center = jnp.mean(stream, axis=-1, keepdims=True)
    off = stream - center
    spread = jnp.mean(off * off, axis=-1, keepdims=True)
    normed = off * lax.rsqrt(spread + 1e-06) * (1.0 + scale) + shift_by
    stream_ref[...] = stream
    normed_ref[...] = normed.astype(jnp.bfloat16)


def stream_norm(own, other, residual, vectors, block=16):
    rows, d_model = own.shape
    row = pl.BlockSpec((block, d_model), lambda i: (i, 0))
    return pl.pallas_call(
        stream_norm_body,
        grid=(rows // block,),
        in_specs=[row, row, row, pl.BlockSpec(vectors.shape, lambda i: (0, 0))],
        out_specs=[row, row],
        out_shape=[
            jax.ShapeDtypeStruct((rows, d_model), jnp.float32),
            jax.ShapeDtypeStruct((rows, d_model), jnp.bfloat16),
        ],
        cost_estimate=pl.CostEstimate(
            flops=20 * rows * d_model, transcendentals=0, bytes_accessed=14 * rows * d_model
        ),
        compiler_params=pltpu.CompilerParams(vmem_limit_bytes=32 << 20),
    )(own, other, residual, vectors)


def mlp_body(order, x_ref, up_ref, down_ref, bias_ref, bias_far_ref, *refs):
    n = 4
    up_far, down_far, out_ref = refs[:n], refs[n : n + 2], refs[n + 2]
    near, far, hid_near, hid_far, up_buf, down_buf, sems = refs[n + 3 :]
    i = pl.program_id(0)
    quarter = up_ref.shape[0]

    def copies():
        for j in range(n):
            yield pltpu.make_async_copy(up_far[j], up_buf.at[j], sems.at[j])
        for j in range(n):
            cols = pl.ds((j % 2) * quarter, quarter)
            yield pltpu.make_async_copy(down_far[j // 2].at[:, cols], down_buf.at[j], sems.at[n + j])

    @pl.when(i == 0)
    def _():
        for copy in copies():
            copy.start()
        near[...] = jnp.broadcast_to(bias_ref[...], near.shape)
        far[...] = jnp.broadcast_to(bias_far_ref[...], far.shape)

    for j, copy in enumerate(copies()):

        @pl.when(i == j)
        def _(copy=copy):
            copy.wait()

    @pl.when(i < n)
    def _():
        at = pl.multiple_of(i * quarter, quarter)
        near[...] += jnp.dot(
            x_ref[:, pl.ds(at, quarter)], up_ref[...], preferred_element_type=jnp.float32
        )
        at = pl.multiple_of(order[i] * quarter, quarter)
        far[...] += jnp.dot(
            x_ref[:, pl.ds(at, quarter)], up_buf[i], preferred_element_type=jnp.float32
        )

    @pl.when(i == n - 1)
    def _():
        hid_near[...] = jax.nn.gelu(near[...], approximate=True).astype(jnp.bfloat16)
        hid_far[...] = jax.nn.gelu(far[...], approximate=True).astype(jnp.bfloat16)

    @pl.when(i >= n)
    def _():
        out_ref[...] = (
            jnp.dot(hid_near[...], down_ref[...], preferred_element_type=jnp.float32)
            + jnp.dot(hid_far[...], down_buf[i - n], preferred_element_type=jnp.float32)
        ).astype(jnp.bfloat16)


def mlp(x, up, down, bias, bias_far, up_far, down_far, order):
    rows, d_model = x.shape
    hidden = up.shape[1]
    n = len(up_far)
    quarter = d_model // n
    whole = lambda i, order: (0, 0)
    column = lambda i, order: (0, order[jnp.maximum(i, n)])
    far_spec = pl.BlockSpec(memory_space=pltpu.MemorySpace.HBM)
    return pl.pallas_call(
        mlp_body,
        grid_spec=pltpu.PrefetchScalarGridSpec(
            num_scalar_prefetch=1,
            grid=(2 * n,),
            in_specs=[
                pl.BlockSpec((rows, d_model), whole),
                pl.BlockSpec((quarter, hidden), lambda i, order: (jnp.minimum(i, n - 1), 0)),
                pl.BlockSpec((hidden, quarter), column),
                pl.BlockSpec((1, hidden), whole),
                pl.BlockSpec((1, hidden), whole),
                *[far_spec] * (n + 2),
            ],
            out_specs=pl.BlockSpec((rows, quarter), column),
            scratch_shapes=[
                pltpu.VMEM((rows, hidden), jnp.float32),
                pltpu.VMEM((rows, hidden), jnp.float32),
                pltpu.VMEM((rows, hidden), jnp.bfloat16),
                pltpu.VMEM((rows, hidden), jnp.bfloat16),
                pltpu.VMEM((n, quarter, hidden), jnp.bfloat16),
                pltpu.VMEM((n, hidden, quarter), jnp.bfloat16),
                pltpu.SemaphoreType.DMA((2 * n,)),
            ],
        ),
        out_shape=jax.ShapeDtypeStruct((rows, d_model), jnp.bfloat16),
        cost_estimate=pl.CostEstimate(
            flops=8 * rows * d_model * hidden,
            transcendentals=rows * hidden * 2,
            bytes_accessed=8 * d_model * hidden,
        ),
        compiler_params=pltpu.CompilerParams(vmem_limit_bytes=40 << 20),
    )(order, x, up, down, bias.reshape(1, -1), bias_far.reshape(1, -1), *up_far, *down_far)


def shift(array, axis, size, by):
    return lax.ppermute(array, axis, [(i, (i + by) % size) for i in range(size)])


def cross(array):
    return lax.ppermute(array, ("yl", "yh"), [(0, 3), (3, 0), (1, 2), (2, 1)])


def part_of(array, parts, index, axis):
    n = array.shape[axis] // parts
    return lax.dynamic_slice_in_dim(array, index * n, n, axis)


tie = lax.optimization_barrier


def gather_x(rows):
    n = rows.shape[0] // 2
    left = shift(rows, "x", 4, 1)
    right = shift(rows, "x", 4, 3)
    far = jnp.concatenate([shift(left[:n], "x", 4, 1), shift(right[n:], "x", 4, 3)], axis=0)
    return rows, left, right, far


def shards(
    img_query,
    img_key,
    img_value,
    text_key,
    text_value,
    residual_in,
    mod_shift,
    mod_scale,
    gate_attn,
    gate_mlp,
    out_weight,
    out_bias,
    up_weight,
    up_bias,
    down_weight,
    down_bias,
):
    yl_at, yh_at, core = lax.axis_index("yl"), lax.axis_index("yh"), lax.axis_index("dp")
    rows_own, width = img_query.shape
    row_block, d_model = residual_in.shape

    up_a = cross(part_of(up_weight, 4, yl_at * 2 + core, 0))
    down_a = cross(part_of(down_weight, 2, core, 1))
    out_mine = lax.all_gather(part_of(out_weight, 2, core, 1), "x", axis=0, tiled=True)
    vectors = jnp.stack([gate_attn, out_bias, mod_scale, mod_shift])
    order = jnp.bitwise_xor(
        jnp.array([2, 2, 2, 2, 0, 0, 0, 0], jnp.int32) * (1 - yl_at)
        + core * jnp.array([1, 1, 1, 1, 2, 2, 2, 2], jnp.int32),
        jnp.array([0, 2, 1, 3, 0, 1, 2, 3], jnp.int32),
    )

    q_other = shift(img_query, "yl", 2, 1)
    own = jnp.concatenate(
        [
            jnp.concatenate([img_key, text_key], axis=0),
            jnp.concatenate([img_value, text_value], axis=0),
        ],
        axis=1,
    )
    cut = -(-own.shape[0] // 32) * 16

    def around(up, down):
        return [shift(up, "z", 8, 1), shift(down, "z", 8, 7)]

    one = around(own, own)
    one, q_other = tie((one, q_other))
    queries = jnp.where(
        yl_at == 0,
        jnp.concatenate([img_query, q_other], axis=0),
        jnp.concatenate([q_other, img_query], axis=0),
    )
    two = around(*one)
    state = attend(queries, [own], None)
    state = attend(queries, one, state)
    two, state, up_a = tie((two, state, up_a))
    three = around(*two)
    up_b = shift(up_a, "yl", 2, 1)
    state = attend(queries, two, state)
    three, state = tie((three, state))
    four = around(three[0][:cut], three[1][cut:])
    state = attend(queries, three, state)
    four, state = tie((four, state))
    shape = (2, 4, 2, row_block, width + HD)
    (part,) = attend(queries, four, state, shape)
    part, up_b, out_mine, down_a = tie((part, up_b, out_mine, down_a))
    out_mate = shift(out_mine, "dp", 2, 1)

    parts = lax.all_to_all(
        part.reshape(8, 2 * row_block, width + HD), ("yl", "x"), split_axis=0, concat_axis=0, tiled=True
    )
    proj_own, proj_away = join_project(parts, out_mine, out_mate, order[4:], yh_at.reshape(1))
    proj_other = shift(proj_away, "yh", 2, 1)
    up_far = [up_a, up_b, shift(up_a, "dp", 2, 1), shift(up_b, "dp", 2, 1)]
    down_far = [down_a, shift(down_a, "dp", 2, 1)]
    bias_far = cross(up_bias)
    proj_other, up_far, down_far, bias_far = tie((proj_other, up_far, down_far, bias_far))
    stream, normed = stream_norm(proj_own, proj_other, residual_in, vectors)
    everyone = jnp.concatenate(gather_x(normed), axis=0)
    out = mlp(everyone, up_weight, down_weight, up_bias, bias_far, up_far, down_far, order)
    blocks = out.reshape(4, row_block, d_model)
    total = blocks[0].astype(jnp.float32)
    total = total + shift(blocks[1], "x", 4, 3).astype(jnp.float32)
    total = total + shift(blocks[2], "x", 4, 1).astype(jnp.float32)
    total = total + shift(blocks[3], "x", 4, 2).astype(jnp.float32)
    return (stream + gate_mlp * (total + down_bias)).astype(jnp.bfloat16)


def solution(mesh):
    fine = Mesh(mesh.devices.reshape([n for _, n in FINE]), [name for name, _ in FINE])
    seq, tp = ("yl", "z"), ("yh", "x")
    tokens = P(("dp", *seq), tp)
    rows = P(("dp", *seq, *tp), None)
    in_specs = (
        tokens,
        tokens,
        tokens,
        tokens,
        tokens,
        rows,
        P("dp"),
        P("dp"),
        P("dp"),
        P("dp"),
        P(tp, None),
        P(),
        P(None, tp),
        P(tp),
        P(tp, None),
        P(),
    )
    return jax.shard_map(shards, mesh=fine, in_specs=in_specs, out_specs=rows, check_vma=False)
```

```python
import functools
import math

import jax
import jax.numpy as jnp
from jax import lax
from jax.experimental import pallas as pl
from jax.experimental.pallas import tpu as pltpu
from jax.sharding import Mesh, PartitionSpec as P

HD = 128
LOG2E = math.log2(math.e)
SCORE_TO_LOG2 = LOG2E / math.sqrt(HD)

FINE = (("yl", 2), ("z", 8), ("yh", 2), ("x", 4), ("dp", 2))


def store_part(o_ref, part, lse):
    h = pl.program_id(1)
    terms = []
    rest = lse
    for _ in range(3):
        terms.append(rest.astype(jnp.bfloat16).astype(jnp.float32))
        rest = rest - terms[-1]
    row = lax.broadcasted_iota(jnp.int32, (HD, lse.shape[1]), 0) - 3 * h
    stats = jnp.zeros((HD, lse.shape[1]), jnp.float32)
    for k, term in enumerate(terms):
        stats = jnp.where(row == k, term, stats)
    stats = stats.T.astype(jnp.bfloat16)
    _, x_size, yh_size, rows, width = o_ref.shape
    for x in range(x_size):
        for yh in range(yh_size):
            at = slice((yh * x_size + x) * rows, (yh * x_size + x + 1) * rows)
            o_ref[0, x, yh, :, pl.ds(pl.multiple_of(h * HD, HD), HD)] = part[at]

            @pl.when(h == 0)
            def _(x=x, yh=yh, at=at):
                o_ref[0, x, yh, :, width - HD :] = stats[at]

            @pl.when(h > 0)
            def _(x=x, yh=yh, at=at):
                o_ref[0, x, yh, :, width - HD :] += stats[at]


def attend_body(pieces, first, last, *refs):
    q_ref = refs[0]
    k_refs = refs[1 : 1 + pieces]
    v_refs = refs[1 + pieces : 1 + 2 * pieces]
    at = 1 + 2 * pieces
    if not first:
        m_in, l_in, acc_in = refs[at : at + 3]
        at += 3
    outs = refs[at:]
    q = q_ref[...]
    scores = [
        lax.dot_general(k[...], q, (((1,), (1,)), ((), ())), preferred_element_type=jnp.float32)
        for k in k_refs
    ]
    m = functools.reduce(jnp.maximum, [jnp.max(s, axis=0, keepdims=True) for s in scores])
    if not first:
        m_old = m_in[0]
        m = jnp.maximum(m, m_old)
    den = None
    acc = None
    for s, v in zip(scores, v_refs):
        e = jnp.exp2((s - m) * SCORE_TO_LOG2)
        part = jnp.sum(e, axis=0, keepdims=True)
        den = part if den is None else den + part
        mixed = lax.dot_general(
            v[...],
            e.astype(jnp.bfloat16),
            (((0,), (0,)), ((), ())),
            preferred_element_type=jnp.float32,
        )
        acc = mixed if acc is None else acc + mixed
    if not first:
        factor = jnp.exp2((m_old - m) * SCORE_TO_LOG2)
        den = den + factor * l_in[0]
        acc = acc + factor * acc_in[...]
    if last:
        store_part(outs[0], (acc / den).T.astype(jnp.bfloat16), m * SCORE_TO_LOG2 + jnp.log2(den))
    else:
        m_out, l_out, acc_out = outs
        m_out[0] = m
        l_out[0] = den
        acc_out[...] = acc


def attend(q, pairs, state, last=None, block=512):
    rows, width = q.shape
    heads = width // HD
    ks = vs = pairs
    first = state is None
    if last:
        grid, at = (rows // block, heads), lambda f: lambda j, h: f(h, j)
    else:
        grid, at = (heads, rows // block), lambda f: f
    q_spec = pl.BlockSpec((block, HD), at(lambda h, j: (j, h)))
    k_specs = [pl.BlockSpec((k.shape[0], HD), at(lambda h, j: (0, h))) for k in ks]
    v_specs = [pl.BlockSpec((v.shape[0], HD), at(lambda h, j: (0, heads + h))) for v in vs]
    stat = pl.BlockSpec((1, 1, block), at(lambda h, j: (h, 0, j)))
    acc = pl.BlockSpec((HD, block), at(lambda h, j: (h, j)))
    if last:
        out_specs = [pl.BlockSpec((1, *last[1:]), at(lambda h, j: (j, 0, 0, 0, 0)))]
        out_shape = [jax.ShapeDtypeStruct(last, jnp.bfloat16)]
    else:
        stat_shape = jax.ShapeDtypeStruct((heads, 1, rows), jnp.float32)
        out_specs = [stat, stat, acc]
        out_shape = [stat_shape, stat_shape, jax.ShapeDtypeStruct((width, rows), jnp.float32)]
    keys = sum(k.shape[0] for k in ks)
    return pl.pallas_call(
        functools.partial(attend_body, len(ks), first, bool(last)),
        grid=grid,
        in_specs=[q_spec, *k_specs, *v_specs, *(() if first else (stat, stat, acc))],
        out_specs=out_specs,
        out_shape=out_shape,
        cost_estimate=pl.CostEstimate(
            flops=4 * rows * keys * width,
            transcendentals=rows * keys * heads,
            bytes_accessed=2 * (rows + 2 * keys) * width,
        ),
        compiler_params=pltpu.CompilerParams(vmem_limit_bytes=48 << 20),
    )(q, *ks, *vs, *(() if first else state))


def join_project_body(order, place, part_ref, own_w, *refs):
    mine, mate = refs[:3], refs[3:6]
    own_ref, away_ref, attended, weights, sems = refs[6:]
    i = pl.program_id(0)
    x_size = part_ref.shape[0] // 2
    rows = part_ref.shape[1] // 2
    width = part_ref.shape[2] - HD
    block = weights.shape[2]

    def copies(n):
        at = pl.multiple_of(order[n] * block, block)
        yield pltpu.make_async_copy(
            own_w.at[:, pl.ds(at, block)], weights.at[n, pl.ds(0, width)], sems.at[n, 0]
        )
        for p, piece in enumerate(mine if n < 2 else mate):
            yield pltpu.make_async_copy(
                piece.at[:, pl.ds(n % 2 * block, block)],
                weights.at[n, pl.ds((p + 1) * width, width)],
                sems.at[n, p + 1],
            )

    @pl.when(i == 0)
    def _():
        for n in range(4):
            for copy in copies(n):
                copy.start()
        for side in range(2):
            yh = place[4] if side == 0 else 1 - place[4]
            at = pl.ds(pl.multiple_of(yh * rows, rows), rows)
            for p in range(x_size):
                a = part_ref[place[p], at, :].astype(jnp.float32)
                b = part_ref[x_size + place[p], at, :].astype(jnp.float32)
                for h in range(width // HD):
                    k = width + 3 * h
                    lse_a = a[:, k : k + 1] + a[:, k + 1 : k + 2] + a[:, k + 2 : k + 3]
                    lse_b = b[:, k : k + 1] + b[:, k + 1 : k + 2] + b[:, k + 2 : k + 3]
                    share = 1.0 / (1.0 + jnp.exp2(lse_b - lse_a))
                    cols = slice(h * HD, (h + 1) * HD)
                    joined = b[:, cols] + share * (a[:, cols] - b[:, cols])
                    to = slice(p * width + h * HD, p * width + (h + 1) * HD)
                    attended[side * rows : (side + 1) * rows, to] = joined.astype(jnp.bfloat16)

    for n in range(4):

        @pl.when(i == n)
        def _(n=n):
            for copy in copies(n):
                copy.wait()
            out = jnp.dot(attended[...], weights[n], preferred_element_type=jnp.float32)
            own_ref[...] = out[:rows]
            away_ref[...] = out[rows:].astype(jnp.bfloat16)


def join_project(parts, own_w, mine, mate, order, place):
    n, both, wide = parts.shape
    width, d_model = own_w.shape
    block, rows = d_model // 4, both // 2
    out = pl.BlockSpec((rows, block), lambda i, order, place: (0, order[i]))
    far_spec = pl.BlockSpec(memory_space=pltpu.MemorySpace.HBM)
    return pl.pallas_call(
        join_project_body,
        grid_spec=pltpu.PrefetchScalarGridSpec(
            num_scalar_prefetch=2,
            grid=(4,),
            in_specs=[
                pl.BlockSpec((n, both, wide), lambda i, order, place: (0, 0, 0)),
                *[far_spec] * 7,
            ],
            out_specs=[out, out],
            scratch_shapes=[
                pltpu.VMEM((both, 4 * width), jnp.bfloat16),
                pltpu.VMEM((4, 4 * width, block), jnp.bfloat16),
                pltpu.SemaphoreType.DMA((4, 4)),
            ],
        ),
        out_shape=[
            jax.ShapeDtypeStruct((rows, d_model), jnp.float32),
            jax.ShapeDtypeStruct((rows, d_model), jnp.bfloat16),
        ],
        cost_estimate=pl.CostEstimate(
            flops=8 * both * width * d_model, transcendentals=0, bytes_accessed=8 * width * d_model
        ),
        compiler_params=pltpu.CompilerParams(vmem_limit_bytes=40 << 20),
    )(order, place, parts, own_w, *mine, *mate)


def stream_norm_body(own_ref, other_ref, residual_ref, vectors_ref, stream_ref, normed_ref):
    gate, bias, scale, shift_by = (vectors_ref[i : i + 1, :] for i in range(4))
    proj = own_ref[...] + other_ref[...].astype(jnp.float32)
    stream = residual_ref[...].astype(jnp.float32) + gate * (proj + bias)
    center = jnp.mean(stream, axis=-1, keepdims=True)
    off = stream - center
    spread = jnp.mean(off * off, axis=-1, keepdims=True)
    normed = off * lax.rsqrt(spread + 1e-06) * (1.0 + scale) + shift_by
    stream_ref[...] = stream
    normed_ref[...] = normed.astype(jnp.bfloat16)


def stream_norm(own, other, residual, vectors, block=16):
    rows, d_model = own.shape
    row = pl.BlockSpec((block, d_model), lambda i: (i, 0))
    return pl.pallas_call(
        stream_norm_body,
        grid=(rows // block,),
        in_specs=[row, row, row, pl.BlockSpec(vectors.shape, lambda i: (0, 0))],
        out_specs=[row, row],
        out_shape=[
            jax.ShapeDtypeStruct((rows, d_model), jnp.float32),
            jax.ShapeDtypeStruct((rows, d_model), jnp.bfloat16),
        ],
        cost_estimate=pl.CostEstimate(
            flops=20 * rows * d_model, transcendentals=0, bytes_accessed=14 * rows * d_model
        ),
        compiler_params=pltpu.CompilerParams(vmem_limit_bytes=32 << 20),
    )(own, other, residual, vectors)


def mlp_body(order, x_ref, up_ref, down_ref, bias_ref, bias_far_ref, *refs):
    n = 4
    up_far, down_far, out_ref = refs[:n], refs[n : 2 * n], refs[2 * n]
    near, far, hid_near, hid_far, up_buf, down_buf, sems = refs[2 * n + 1 :]
    i = pl.program_id(0)
    quarter = up_ref.shape[0]

    def copies(j):
        down = j >= n
        a, b = (down_far if down else up_far)[j % n // 2 * 2 : j % n // 2 * 2 + 2]
        to = (down_buf if down else up_buf).at[j % n]

        def part(ref, start, size):
            return ref.at[:, pl.ds(start, size)] if down else ref.at[pl.ds(start, size)]

        if j % 2 == 0:
            yield pltpu.make_async_copy(part(a, 0, quarter), to, sems.at[j, 0])
            return
        rest = a.shape[1 if down else 0] - quarter
        yield pltpu.make_async_copy(part(a, quarter, rest), part(to, 0, rest), sems.at[j, 0])
        yield pltpu.make_async_copy(b, part(to, rest, quarter - rest), sems.at[j, 1])

    @pl.when(i == 0)
    def _():
        for j in range(2 * n):
            for copy in copies(j):
                copy.start()
        near[...] = jnp.broadcast_to(bias_ref[...], near.shape)
        far[...] = jnp.broadcast_to(bias_far_ref[...], far.shape)

    for j in range(2 * n):

        @pl.when(i == j)
        def _(j=j):
            for copy in copies(j):
                copy.wait()

    @pl.when(i < n)
    def _():
        at = pl.multiple_of(order[i] * quarter, quarter)
        x = x_ref[:, pl.ds(at, quarter)]
        near[...] += jnp.dot(x, up_ref[...], preferred_element_type=jnp.float32)
        far[...] += jnp.dot(x, up_buf[i], preferred_element_type=jnp.float32)

    @pl.when(i == n - 1)
    def _():
        hid_near[...] = jax.nn.gelu(near[...], approximate=True).astype(jnp.bfloat16)
        hid_far[...] = jax.nn.gelu(far[...], approximate=True).astype(jnp.bfloat16)

    @pl.when(i >= n)
    def _():
        out_ref[...] = (
            jnp.dot(hid_near[...], down_ref[...], preferred_element_type=jnp.float32)
            + jnp.dot(hid_far[...], down_buf[i - n], preferred_element_type=jnp.float32)
        ).astype(jnp.bfloat16)


def mlp(x, up, down, bias, bias_far, up_far, down_far, order):
    rows, d_model = x.shape
    hidden = up.shape[1]
    n = 4
    quarter = d_model // n
    whole = lambda i, order: (0, 0)
    column = lambda i, order: (0, order[jnp.maximum(i - n, 0)])
    far_spec = pl.BlockSpec(memory_space=pltpu.MemorySpace.HBM)
    return pl.pallas_call(
        mlp_body,
        grid_spec=pltpu.PrefetchScalarGridSpec(
            num_scalar_prefetch=1,
            grid=(2 * n,),
            in_specs=[
                pl.BlockSpec((rows, d_model), whole),
                pl.BlockSpec((quarter, hidden), lambda i, order: (order[jnp.minimum(i, n - 1)], 0)),
                pl.BlockSpec((hidden, quarter), column),
                pl.BlockSpec((1, hidden), whole),
                pl.BlockSpec((1, hidden), whole),
                *[far_spec] * (2 * n),
            ],
            out_specs=pl.BlockSpec((rows, quarter), column),
            scratch_shapes=[
                pltpu.VMEM((rows, hidden), jnp.float32),
                pltpu.VMEM((rows, hidden), jnp.float32),
                pltpu.VMEM((rows, hidden), jnp.bfloat16),
                pltpu.VMEM((rows, hidden), jnp.bfloat16),
                pltpu.VMEM((n, quarter, hidden), jnp.bfloat16),
                pltpu.VMEM((n, hidden, quarter), jnp.bfloat16),
                pltpu.SemaphoreType.DMA((2 * n, 2)),
            ],
        ),
        out_shape=jax.ShapeDtypeStruct((rows, d_model), jnp.bfloat16),
        cost_estimate=pl.CostEstimate(
            flops=8 * rows * d_model * hidden,
            transcendentals=rows * hidden * 2,
            bytes_accessed=8 * d_model * hidden,
        ),
        compiler_params=pltpu.CompilerParams(vmem_limit_bytes=40 << 20),
    )(order, x, up, down, bias.reshape(1, -1), bias_far.reshape(1, -1), *up_far, *down_far)


def shift(array, axis, size, by):
    return lax.ppermute(array, axis, [(i, (i + by) % size) for i in range(size)])


def cross(array):
    return lax.ppermute(array, ("yl", "yh"), [(0, 3), (3, 0), (1, 2), (2, 1)])


def part_of(array, parts, index, axis):
    n = array.shape[axis] // parts
    return lax.dynamic_slice_in_dim(array, index * n, n, axis)


def half_of(array, index, axis, start, stop):
    n = array.shape[axis] // 2
    return lax.dynamic_slice_in_dim(array, index * n + start, stop - start, axis)


tie = lax.optimization_barrier


def gather_x(rows):
    n = rows.shape[0] // 2
    left = shift(rows, "x", 4, 1)
    right = shift(rows, "x", 4, 3)
    far = jnp.concatenate([shift(left[:n], "x", 4, 1), shift(right[n:], "x", 4, 3)], axis=0)
    return rows, left, right, far


def shards(
    img_query,
    img_key,
    img_value,
    text_key,
    text_value,
    residual_in,
    mod_shift,
    mod_scale,
    gate_attn,
    gate_mlp,
    out_weight,
    out_bias,
    up_weight,
    up_bias,
    down_weight,
    down_bias,
):
    yl_at, yh_at, core = lax.axis_index("yl"), lax.axis_index("yh"), lax.axis_index("dp")
    rows_own, width = img_query.shape
    row_block, d_model = residual_in.shape

    vectors = jnp.stack([gate_attn, out_bias, mod_scale, mod_shift])
    order = jnp.bitwise_xor(2 * core, jnp.arange(4, dtype=jnp.int32))
    x_at = lax.axis_index("x")
    place = jnp.concatenate(
        [(x_at + jnp.array([0, 3, 1, 2], jnp.int32)) % 4, yh_at.reshape(1).astype(jnp.int32)]
    )
    out_half = part_of(out_weight, 2, core, 1)
    up_most, down_most = d_model // 3, d_model // 8 * 3

    q_other = shift(img_query, "yl", 2, 1)
    own = jnp.concatenate(
        [
            jnp.concatenate([img_key, text_key], axis=0),
            jnp.concatenate([img_value, text_value], axis=0),
        ],
        axis=1,
    )
    cut = -(-own.shape[0] // 32) * 16

    def around(up, down):
        return [shift(up, "z", 8, 1), shift(down, "z", 8, 7)]

    one = around(own, own)
    up_a = cross(half_of(up_weight, core, 0, 0, up_most))
    out_l = shift(out_half, "x", 4, 1)
    out_r = shift(out_half, "x", 4, 3)
    one, q_other = tie((one, q_other))
    queries = jnp.where(
        yl_at == 0,
        jnp.concatenate([img_query, q_other], axis=0),
        jnp.concatenate([q_other, img_query], axis=0),
    )
    two = around(*one)
    state = attend(queries, [own], None)
    state = attend(queries, one, state)
    two, state, up_a, out_l, out_r, core, out_half = tie(
        (two, state, up_a, out_l, out_r, core, out_half)
    )
    three = around(*two)
    down_a = cross(half_of(down_weight, core, 1, 0, down_most))
    out_f = shift(out_half, "x", 4, 2)
    state = attend(queries, two, state)
    three, state, core = tie((three, state, core))
    up_late = half_of(up_weight, core, 0, up_most, d_model // 2)
    down_late = half_of(down_weight, core, 1, down_most, d_model // 2)
    four = around(three[0][:cut], three[1][cut:])
    state = attend(queries, three, state)
    four, state = tie((four, state))
    shape = (2, 4, 2, row_block, width + HD)
    (part,) = attend(queries, four, state, shape)
    out_mine = [out_l, out_r, out_f]
    part, down_a, up_a, out_mine, up_late, down_late = tie(
        (part, down_a, up_a, out_mine, up_late, down_late)
    )
    out_mate = [shift(piece, "dp", 2, 1) for piece in out_mine]
    up_b = cross(up_late)
    down_b = cross(down_late)

    parts = lax.all_to_all(
        part.reshape(8, 2 * row_block, width + HD), ("yl", "x"), split_axis=0, concat_axis=0, tiled=True
    )
    parts, out_mate, up_b, down_b = tie((parts, out_mate, up_b, down_b))
    proj_own, proj_away = join_project(parts, out_weight, out_mine, out_mate, order, place)
    proj_other = shift(proj_away, "yh", 2, 1)
    up_far = [up_a, up_b, shift(up_a, "dp", 2, 1), shift(up_b, "dp", 2, 1)]
    down_far = [down_a, down_b, shift(down_a, "dp", 2, 1), shift(down_b, "dp", 2, 1)]
    bias_far = cross(up_bias)
    proj_other, up_far, down_far, bias_far = tie((proj_other, up_far, down_far, bias_far))
    stream, normed = stream_norm(proj_own, proj_other, residual_in, vectors)
    everyone = jnp.concatenate(gather_x(normed), axis=0)
    out = mlp(everyone, up_weight, down_weight, up_bias, bias_far, up_far, down_far, order)
    blocks = out.reshape(4, row_block, d_model)
    total = blocks[0].astype(jnp.float32)
    total = total + shift(blocks[1], "x", 4, 3).astype(jnp.float32)
    total = total + shift(blocks[2], "x", 4, 1).astype(jnp.float32)
    total = total + shift(blocks[3], "x", 4, 2).astype(jnp.float32)
    return (stream + gate_mlp * (total + down_bias)).astype(jnp.bfloat16)


def solution(mesh):
    fine = Mesh(mesh.devices.reshape([n for _, n in FINE]), [name for name, _ in FINE])
    seq, tp = ("yl", "z"), ("yh", "x")
    tokens = P(("dp", *seq), tp)
    rows = P(("dp", *seq, *tp), None)
    in_specs = (
        tokens,
        tokens,
        tokens,
        tokens,
        tokens,
        rows,
        P("dp"),
        P("dp"),
        P("dp"),
        P("dp"),
        P(tp, None),
        P(),
        P(None, tp),
        P(tp),
        P(tp, None),
        P(),
    )
    return jax.shard_map(shards, mesh=fine, in_specs=in_specs, out_specs=rows, check_vma=False)
```

```python
import functools
import math

import jax
import jax.numpy as jnp
from jax import lax
from jax.experimental import pallas as pl
from jax.experimental.pallas import tpu as pltpu
from jax.sharding import Mesh, PartitionSpec as P

HD = 128
LOG2E = math.log2(math.e)
SCORE_TO_LOG2 = LOG2E / math.sqrt(HD)

FINE = (("yl", 2), ("z", 8), ("yh", 2), ("x", 4), ("dp", 2))


def store_part(o_ref, part, lse):
    h = pl.program_id(1)
    terms = []
    rest = lse
    for _ in range(3):
        terms.append(rest.astype(jnp.bfloat16).astype(jnp.float32))
        rest = rest - terms[-1]
    row = lax.broadcasted_iota(jnp.int32, (HD, lse.shape[1]), 0) - 3 * h
    stats = jnp.zeros((HD, lse.shape[1]), jnp.float32)
    for k, term in enumerate(terms):
        stats = jnp.where(row == k, term, stats)
    stats = stats.T.astype(jnp.bfloat16)
    _, x_size, yh_size, rows, width = o_ref.shape
    for x in range(x_size):
        for yh in range(yh_size):
            at = slice((yh * x_size + x) * rows, (yh * x_size + x + 1) * rows)
            o_ref[0, x, yh, :, pl.ds(pl.multiple_of(h * HD, HD), HD)] = part[at]

            @pl.when(h == 0)
            def _(x=x, yh=yh, at=at):
                o_ref[0, x, yh, :, width - HD :] = stats[at]

            @pl.when(h > 0)
            def _(x=x, yh=yh, at=at):
                o_ref[0, x, yh, :, width - HD :] += stats[at]


def attend_body(pieces, first, last, *refs):
    q_ref = refs[0]
    k_refs = refs[1 : 1 + pieces]
    v_refs = refs[1 + pieces : 1 + 2 * pieces]
    at = 1 + 2 * pieces
    if not first:
        m_in, l_in, acc_in = refs[at : at + 3]
        at += 3
    outs = refs[at:]
    q = q_ref[...]
    scores = [
        lax.dot_general(k[...], q, (((1,), (1,)), ((), ())), preferred_element_type=jnp.float32)
        for k in k_refs
    ]
    m = functools.reduce(jnp.maximum, [jnp.max(s, axis=0, keepdims=True) for s in scores])
    if not first:
        m_old = m_in[0]
        m = jnp.maximum(m, m_old)
    den = None
    acc = None
    for s, v in zip(scores, v_refs):
        e = jnp.exp2((s - m) * SCORE_TO_LOG2)
        part = jnp.sum(e, axis=0, keepdims=True)
        den = part if den is None else den + part
        mixed = lax.dot_general(
            v[...],
            e.astype(jnp.bfloat16),
            (((0,), (0,)), ((), ())),
            preferred_element_type=jnp.float32,
        )
        acc = mixed if acc is None else acc + mixed
    if not first:
        factor = jnp.exp2((m_old - m) * SCORE_TO_LOG2)
        den = den + factor * l_in[0]
        acc = acc + factor * acc_in[...]
    if last:
        store_part(outs[0], (acc / den).T.astype(jnp.bfloat16), m * SCORE_TO_LOG2 + jnp.log2(den))
    else:
        m_out, l_out, acc_out = outs
        m_out[0] = m
        l_out[0] = den
        acc_out[...] = acc


def attend(q, pairs, state, last=None, block=512):
    rows, width = q.shape
    heads = width // HD
    ks = vs = pairs
    first = state is None
    if last:
        grid, at = (rows // block, heads), lambda f: lambda j, h: f(h, j)
    else:
        grid, at = (heads, rows // block), lambda f: f
    q_spec = pl.BlockSpec((block, HD), at(lambda h, j: (j, h)))
    k_specs = [pl.BlockSpec((k.shape[0], HD), at(lambda h, j: (0, h))) for k in ks]
    v_specs = [pl.BlockSpec((v.shape[0], HD), at(lambda h, j: (0, heads + h))) for v in vs]
    stat = pl.BlockSpec((1, 1, block), at(lambda h, j: (h, 0, j)))
    acc = pl.BlockSpec((HD, block), at(lambda h, j: (h, j)))
    if last:
        out_specs = [pl.BlockSpec((1, *last[1:]), at(lambda h, j: (j, 0, 0, 0, 0)))]
        out_shape = [jax.ShapeDtypeStruct(last, jnp.bfloat16)]
    else:
        stat_shape = jax.ShapeDtypeStruct((heads, 1, rows), jnp.float32)
        out_specs = [stat, stat, acc]
        out_shape = [stat_shape, stat_shape, jax.ShapeDtypeStruct((width, rows), jnp.float32)]
    keys = sum(k.shape[0] for k in ks)
    return pl.pallas_call(
        functools.partial(attend_body, len(ks), first, bool(last)),
        grid=grid,
        in_specs=[q_spec, *k_specs, *v_specs, *(() if first else (stat, stat, acc))],
        out_specs=out_specs,
        out_shape=out_shape,
        cost_estimate=pl.CostEstimate(
            flops=4 * rows * keys * width,
            transcendentals=rows * keys * heads,
            bytes_accessed=2 * (rows + 2 * keys) * width,
        ),
        compiler_params=pltpu.CompilerParams(vmem_limit_bytes=16 << 20),
    )(q, *ks, *vs, *(() if first else state))


def join_project_body(order, place, part_ref, own_w, *refs):
    mine, mate = refs[:3], refs[3:6]
    own_ref, away_ref, attended, weights, sems = refs[6:]
    i = pl.program_id(0)
    x_size = part_ref.shape[0] // 2
    rows = part_ref.shape[1] // 2
    width = part_ref.shape[2] - HD
    block = weights.shape[2]

    def copies(n):
        at = pl.multiple_of(order[n] * block, block)
        yield pltpu.make_async_copy(
            own_w.at[:, pl.ds(at, block)], weights.at[n, pl.ds(0, width)], sems.at[n, 0]
        )
        for p, piece in enumerate(mine if n < 2 else mate):
            yield pltpu.make_async_copy(
                piece.at[:, pl.ds(n % 2 * block, block)],
                weights.at[n, pl.ds((p + 1) * width, width)],
                sems.at[n, p + 1],
            )

    @pl.when(i == 0)
    def _():
        for n in range(4):
            for copy in copies(n):
                copy.start()
        for side in range(2):
            yh = place[4] if side == 0 else 1 - place[4]
            at = pl.ds(pl.multiple_of(yh * rows, rows), rows)
            for p in range(x_size):
                a = part_ref[place[p], at, :].astype(jnp.float32)
                b = part_ref[x_size + place[p], at, :].astype(jnp.float32)
                for h in range(width // HD):
                    k = width + 3 * h
                    lse_a = a[:, k : k + 1] + a[:, k + 1 : k + 2] + a[:, k + 2 : k + 3]
                    lse_b = b[:, k : k + 1] + b[:, k + 1 : k + 2] + b[:, k + 2 : k + 3]
                    share = 1.0 / (1.0 + jnp.exp2(lse_b - lse_a))
                    cols = slice(h * HD, (h + 1) * HD)
                    joined = b[:, cols] + share * (a[:, cols] - b[:, cols])
                    to = slice(p * width + h * HD, p * width + (h + 1) * HD)
                    attended[side * rows : (side + 1) * rows, to] = joined.astype(jnp.bfloat16)

    for n in range(4):

        @pl.when(i == n)
        def _(n=n):
            for copy in copies(n):
                copy.wait()
            out = jnp.dot(attended[...], weights[n], preferred_element_type=jnp.float32)
            own_ref[...] = out[:rows]
            away_ref[...] = out[rows:].astype(jnp.bfloat16)


def join_project(parts, own_w, mine, mate, order, place):
    n, both, wide = parts.shape
    width, d_model = own_w.shape
    block, rows = d_model // 4, both // 2
    out = pl.BlockSpec((rows, block), lambda i, order, place: (0, order[i]))
    far_spec = pl.BlockSpec(memory_space=pltpu.MemorySpace.HBM)
    return pl.pallas_call(
        join_project_body,
        grid_spec=pltpu.PrefetchScalarGridSpec(
            num_scalar_prefetch=2,
            grid=(4,),
            in_specs=[
                pl.BlockSpec((n, both, wide), lambda i, order, place: (0, 0, 0)),
                *[far_spec] * 7,
            ],
            out_specs=[out, out],
            scratch_shapes=[
                pltpu.VMEM((both, 4 * width), jnp.bfloat16),
                pltpu.VMEM((4, 4 * width, block), jnp.bfloat16),
                pltpu.SemaphoreType.DMA((4, 4)),
            ],
        ),
        out_shape=[
            jax.ShapeDtypeStruct((rows, d_model), jnp.float32),
            jax.ShapeDtypeStruct((rows, d_model), jnp.bfloat16),
        ],
        cost_estimate=pl.CostEstimate(
            flops=8 * both * width * d_model, transcendentals=0, bytes_accessed=8 * width * d_model
        ),
        compiler_params=pltpu.CompilerParams(vmem_limit_bytes=30 << 20),
    )(order, place, parts, own_w, *mine, *mate)


def stream_norm_body(own_ref, other_ref, residual_ref, vectors_ref, stream_ref, normed_ref):
    gate, bias, scale, shift_by = (vectors_ref[i : i + 1, :] for i in range(4))
    proj = own_ref[...] + other_ref[...].astype(jnp.float32)
    stream = residual_ref[...].astype(jnp.float32) + gate * (proj + bias)
    center = jnp.mean(stream, axis=-1, keepdims=True)
    off = stream - center
    spread = jnp.mean(off * off, axis=-1, keepdims=True)
    normed = off * lax.rsqrt(spread + 1e-06) * (1.0 + scale) + shift_by
    stream_ref[...] = stream
    normed_ref[...] = normed.astype(jnp.bfloat16)


def stream_norm(own, other, residual, vectors, block=16):
    rows, d_model = own.shape
    row = pl.BlockSpec((block, d_model), lambda i: (i, 0))
    return pl.pallas_call(
        stream_norm_body,
        grid=(rows // block,),
        in_specs=[row, row, row, pl.BlockSpec(vectors.shape, lambda i: (0, 0))],
        out_specs=[row, row],
        out_shape=[
            jax.ShapeDtypeStruct((rows, d_model), jnp.float32),
            jax.ShapeDtypeStruct((rows, d_model), jnp.bfloat16),
        ],
        cost_estimate=pl.CostEstimate(
            flops=20 * rows * d_model, transcendentals=0, bytes_accessed=14 * rows * d_model
        ),
        compiler_params=pltpu.CompilerParams(vmem_limit_bytes=8 << 20),
    )(own, other, residual, vectors)


def mlp_body(order, x_ref, up_ref, down_ref, bias_ref, bias_far_ref, *refs):
    n = 4
    up_far, down_far, out_ref = refs[:n], refs[n : 2 * n], refs[2 * n]
    near, far, hid_near, hid_far, up_buf, down_buf, sems = refs[2 * n + 1 :]
    i = pl.program_id(0)
    quarter = up_ref.shape[0]

    def copies(j):
        down = j >= n
        a, b = (down_far if down else up_far)[j % n // 2 * 2 : j % n // 2 * 2 + 2]
        to = (down_buf if down else up_buf).at[j % n]

        def part(ref, start, size):
            return ref.at[:, pl.ds(start, size)] if down else ref.at[pl.ds(start, size)]

        if j % 2 == 0:
            yield pltpu.make_async_copy(part(a, 0, quarter), to, sems.at[j, 0])
            return
        rest = a.shape[1 if down else 0] - quarter
        yield pltpu.make_async_copy(part(a, quarter, rest), part(to, 0, rest), sems.at[j, 0])
        yield pltpu.make_async_copy(b, part(to, rest, quarter - rest), sems.at[j, 1])

    @pl.when(i == 0)
    def _():
        for j in range(2 * n):
            for copy in copies(j):
                copy.start()
        near[...] = jnp.broadcast_to(bias_ref[...], near.shape)
        far[...] = jnp.broadcast_to(bias_far_ref[...], far.shape)

    for j in range(2 * n):

        @pl.when(i == j)
        def _(j=j):
            for copy in copies(j):
                copy.wait()

    @pl.when(i < n)
    def _():
        at = pl.multiple_of(order[i] * quarter, quarter)
        x = x_ref[:, pl.ds(at, quarter)]
        near[...] += jnp.dot(x, up_ref[...], preferred_element_type=jnp.float32)
        far[...] += jnp.dot(x, up_buf[i], preferred_element_type=jnp.float32)

    @pl.when(i == n - 1)
    def _():
        hid_near[...] = jax.nn.gelu(near[...], approximate=True).astype(jnp.bfloat16)
        hid_far[...] = jax.nn.gelu(far[...], approximate=True).astype(jnp.bfloat16)

    @pl.when(i >= n)
    def _():
        out_ref[...] = (
            jnp.dot(hid_near[...], down_ref[...], preferred_element_type=jnp.float32)
            + jnp.dot(hid_far[...], down_buf[i - n], preferred_element_type=jnp.float32)
        ).astype(jnp.bfloat16)


def mlp(x, up, down, bias, bias_far, up_far, down_far, order):
    rows, d_model = x.shape
    hidden = up.shape[1]
    n = 4
    quarter = d_model // n
    whole = lambda i, order: (0, 0)
    column = lambda i, order: (0, order[jnp.maximum(i - n, 0)])
    far_spec = pl.BlockSpec(memory_space=pltpu.MemorySpace.HBM)
    return pl.pallas_call(
        mlp_body,
        grid_spec=pltpu.PrefetchScalarGridSpec(
            num_scalar_prefetch=1,
            grid=(2 * n,),
            in_specs=[
                pl.BlockSpec((rows, d_model), whole),
                pl.BlockSpec((quarter, hidden), lambda i, order: (order[jnp.minimum(i, n - 1)], 0)),
                pl.BlockSpec((hidden, quarter), column),
                pl.BlockSpec((1, hidden), whole),
                pl.BlockSpec((1, hidden), whole),
                *[far_spec] * (2 * n),
            ],
            out_specs=pl.BlockSpec((rows, quarter), column),
            scratch_shapes=[
                pltpu.VMEM((rows, hidden), jnp.float32),
                pltpu.VMEM((rows, hidden), jnp.float32),
                pltpu.VMEM((rows, hidden), jnp.bfloat16),
                pltpu.VMEM((rows, hidden), jnp.bfloat16),
                pltpu.VMEM((n, quarter, hidden), jnp.bfloat16),
                pltpu.VMEM((n, hidden, quarter), jnp.bfloat16),
                pltpu.SemaphoreType.DMA((2 * n, 2)),
            ],
        ),
        out_shape=jax.ShapeDtypeStruct((rows, d_model), jnp.bfloat16),
        cost_estimate=pl.CostEstimate(
            flops=8 * rows * d_model * hidden,
            transcendentals=rows * hidden * 2,
            bytes_accessed=8 * d_model * hidden,
        ),
        compiler_params=pltpu.CompilerParams(vmem_limit_bytes=30 << 20),
    )(order, x, up, down, bias.reshape(1, -1), bias_far.reshape(1, -1), *up_far, *down_far)


def shift(array, axis, size, by):
    return lax.ppermute(array, axis, [(i, (i + by) % size) for i in range(size)])


def cross(array):
    return lax.ppermute(array, ("yl", "yh"), [(0, 3), (3, 0), (1, 2), (2, 1)])


def halves_body(core, up, down, out, up_a, up_b, down_a, down_b, out_half, sems):
    n = up_a.shape[0] + up_b.shape[0]
    start = pl.multiple_of(core[0] * n, n)
    copies = (
        (up.at[pl.ds(start, up_a.shape[0])], up_a),
        (up.at[pl.ds(start + up_a.shape[0], up_b.shape[0])], up_b),
        (down.at[:, pl.ds(start, down_a.shape[1])], down_a),
        (down.at[:, pl.ds(start + down_a.shape[1], down_b.shape[1])], down_b),
        (out.at[:, pl.ds(start, n)], out_half),
    )
    copies = [pltpu.make_async_copy(a, b, sems.at[i]) for i, (a, b) in enumerate(copies)]
    for copy in copies:
        copy.start()
    for copy in copies:
        copy.wait()


def halves(core, up, down, out, up_most, down_most):
    d_model, hidden = up.shape
    half = d_model // 2
    hbm = pl.BlockSpec(memory_space=pltpu.MemorySpace.HBM)
    shapes = (
        (up_most, hidden),
        (half - up_most, hidden),
        (hidden, down_most),
        (hidden, half - down_most),
        (out.shape[0], half),
    )
    return pl.pallas_call(
        halves_body,
        grid_spec=pltpu.PrefetchScalarGridSpec(
            num_scalar_prefetch=1,
            grid=(1,),
            in_specs=[hbm] * 3,
            out_specs=[hbm] * 5,
            scratch_shapes=[pltpu.SemaphoreType.DMA((5,))],
        ),
        out_shape=[jax.ShapeDtypeStruct(shape, up.dtype) for shape in shapes],
    )(core.reshape(1), up, down, out)


tie = lax.optimization_barrier


def gather_x(rows):
    n = rows.shape[0] // 2
    left = shift(rows, "x", 4, 1)
    right = shift(rows, "x", 4, 3)
    far = jnp.concatenate([shift(left[:n], "x", 4, 1), shift(right[n:], "x", 4, 3)], axis=0)
    return rows, left, right, far


def shards(
    img_query,
    img_key,
    img_value,
    text_key,
    text_value,
    residual_in,
    mod_shift,
    mod_scale,
    gate_attn,
    gate_mlp,
    out_weight,
    out_bias,
    up_weight,
    up_bias,
    down_weight,
    down_bias,
):
    yl_at, yh_at, core = lax.axis_index("yl"), lax.axis_index("yh"), lax.axis_index("dp")
    rows_own, width = img_query.shape
    row_block, d_model = residual_in.shape

    vectors = jnp.stack([gate_attn, out_bias, mod_scale, mod_shift])
    order = jnp.bitwise_xor(2 * core, jnp.arange(4, dtype=jnp.int32))
    x_at = lax.axis_index("x")
    place = jnp.concatenate(
        [(x_at + jnp.array([0, 3, 1, 2], jnp.int32)) % 4, yh_at.reshape(1).astype(jnp.int32)]
    )
    up_first, up_late, down_first, down_late, out_half = halves(
        core, up_weight, down_weight, out_weight, d_model // 24 * 7, d_model // 8 * 3
    )

    q_other = shift(img_query, "yl", 2, 1)
    own = jnp.concatenate(
        [
            jnp.concatenate([img_key, text_key], axis=0),
            jnp.concatenate([img_value, text_value], axis=0),
        ],
        axis=1,
    )
    cut = -(-own.shape[0] // 32) * 16

    def around(up, down):
        return [shift(up, "z", 8, 1), shift(down, "z", 8, 7)]

    one = around(own, own)
    up_a = cross(up_first)
    out_l = shift(out_half, "x", 4, 1)
    out_r = shift(out_half, "x", 4, 3)
    one, q_other = tie((one, q_other))
    queries = jnp.where(
        yl_at == 0,
        jnp.concatenate([img_query, q_other], axis=0),
        jnp.concatenate([q_other, img_query], axis=0),
    )
    two = around(*one)
    state = attend(queries, [own], None)
    state = attend(queries, one, state)
    two, state, up_a, out_l, out_r, down_first, out_half = tie(
        (two, state, up_a, out_l, out_r, down_first, out_half)
    )
    three = around(*two)
    down_a = cross(down_first)
    out_f = shift(out_half, "x", 4, 2)
    state = attend(queries, two, state)
    three, state = tie((three, state))
    four = around(three[0][:cut], three[1][cut:])
    state = attend(queries, three, state)
    four, state = tie((four, state))
    shape = (2, 4, 2, row_block, width + HD)
    (part,) = attend(queries, four, state, shape)
    out_mine = [out_l, out_r, out_f]
    part, down_a, up_a, out_mine, up_late, down_late = tie(
        (part, down_a, up_a, out_mine, up_late, down_late)
    )
    out_mate = [shift(piece, "dp", 2, 1) for piece in out_mine]
    up_b = cross(up_late)
    down_b = cross(down_late)

    parts = lax.all_to_all(
        part.reshape(8, 2 * row_block, width + HD), ("yl", "x"), split_axis=0, concat_axis=0, tiled=True
    )
    parts, out_mate = tie((parts, out_mate))
    proj_own, proj_away = join_project(parts, out_weight, out_mine, out_mate, order, place)
    proj_away, up_b, down_b = tie((proj_away, up_b, down_b))
    proj_other = shift(proj_away, "yh", 2, 1)
    up_far = [up_a, up_b, shift(up_a, "dp", 2, 1), shift(up_b, "dp", 2, 1)]
    down_far = [down_a, down_b, shift(down_a, "dp", 2, 1), shift(down_b, "dp", 2, 1)]
    bias_far = cross(up_bias)
    proj_other, up_far, down_far = tie((proj_other, up_far, down_far))
    stream, normed = stream_norm(proj_own, proj_other, residual_in, vectors)
    everyone = jnp.concatenate(gather_x(normed), axis=0)
    out = mlp(everyone, up_weight, down_weight, up_bias, bias_far, up_far, down_far, order)
    blocks = out.reshape(4, row_block, d_model)
    total = blocks[0].astype(jnp.float32)
    total = total + shift(blocks[1], "x", 4, 3).astype(jnp.float32)
    total = total + shift(blocks[2], "x", 4, 1).astype(jnp.float32)
    total = total + shift(blocks[3], "x", 4, 2).astype(jnp.float32)
    return (stream + gate_mlp * (total + down_bias)).astype(jnp.bfloat16)


def solution(mesh):
    fine = Mesh(mesh.devices.reshape([n for _, n in FINE]), [name for name, _ in FINE])
    seq, tp = ("yl", "z"), ("yh", "x")
    tokens = P(("dp", *seq), tp)
    rows = P(("dp", *seq, *tp), None)
    in_specs = (
        tokens,
        tokens,
        tokens,
        tokens,
        tokens,
        rows,
        P("dp"),
        P("dp"),
        P("dp"),
        P("dp"),
        P(tp, None),
        P(),
        P(None, tp),
        P(tp),
        P(tp, None),
        P(),
    )
    return jax.shard_map(shards, mesh=fine, in_specs=in_specs, out_specs=rows, check_vma=False)
```

```python
import functools
import math

import jax
import jax.numpy as jnp
from jax import lax
from jax.experimental import pallas as pl
from jax.experimental.pallas import tpu as pltpu
from jax.sharding import Mesh, PartitionSpec as P

HD = 128
LOG2E = math.log2(math.e)
SCORE_TO_LOG2 = LOG2E / math.sqrt(HD)

FINE = (("yl", 2), ("z", 8), ("yh", 2), ("x", 4), ("dp", 2))


def store_part(o_ref, part, lse):
    h = pl.program_id(1)
    terms = []
    rest = lse
    for _ in range(3):
        terms.append(rest.astype(jnp.bfloat16).astype(jnp.float32))
        rest = rest - terms[-1]
    row = lax.broadcasted_iota(jnp.int32, (HD, lse.shape[1]), 0) - 3 * h
    stats = jnp.zeros((HD, lse.shape[1]), jnp.float32)
    for k, term in enumerate(terms):
        stats = jnp.where(row == k, term, stats)
    stats = stats.T.astype(jnp.bfloat16)
    _, x_size, yh_size, rows, width = o_ref.shape
    for x in range(x_size):
        for yh in range(yh_size):
            at = slice((yh * x_size + x) * rows, (yh * x_size + x + 1) * rows)
            o_ref[0, x, yh, :, pl.ds(pl.multiple_of(h * HD, HD), HD)] = part[at]

            @pl.when(h == 0)
            def _(x=x, yh=yh, at=at):
                o_ref[0, x, yh, :, width - HD :] = stats[at]

            @pl.when(h > 0)
            def _(x=x, yh=yh, at=at):
                o_ref[0, x, yh, :, width - HD :] += stats[at]


def attend_body(pieces, first, last, *refs):
    q_ref = refs[0]
    k_refs = refs[1 : 1 + pieces]
    v_refs = refs[1 + pieces : 1 + 2 * pieces]
    at = 1 + 2 * pieces
    if not first:
        m_in, l_in, acc_in = refs[at : at + 3]
        at += 3
    outs = refs[at:]
    q = q_ref[...]
    scores = [
        lax.dot_general(k[...], q, (((1,), (1,)), ((), ())), preferred_element_type=jnp.float32)
        for k in k_refs
    ]
    m = functools.reduce(jnp.maximum, [jnp.max(s, axis=0, keepdims=True) for s in scores])
    if not first:
        m_old = m_in[0]
        m = jnp.maximum(m, m_old)
    den = None
    acc = None
    for s, v in zip(scores, v_refs):
        e = jnp.exp2((s - m) * SCORE_TO_LOG2)
        part = jnp.sum(e, axis=0, keepdims=True)
        den = part if den is None else den + part
        mixed = lax.dot_general(
            v[...],
            e.astype(jnp.bfloat16),
            (((0,), (0,)), ((), ())),
            preferred_element_type=jnp.float32,
        )
        acc = mixed if acc is None else acc + mixed
    if not first:
        factor = jnp.exp2((m_old - m) * SCORE_TO_LOG2)
        den = den + factor * l_in[0]
        acc = acc + factor * acc_in[...]
    if last:
        store_part(outs[0], (acc / den).T.astype(jnp.bfloat16), m * SCORE_TO_LOG2 + jnp.log2(den))
    else:
        m_out, l_out, acc_out = outs
        m_out[0] = m
        l_out[0] = den
        acc_out[...] = acc


def attend(q, pairs, state, last=None, block=512):
    rows, width = q.shape
    heads = width // HD
    ks = vs = pairs
    first = state is None
    if last:
        grid, at = (rows // block, heads), lambda f: lambda j, h: f(h, j)
    else:
        grid, at = (heads, rows // block), lambda f: f
    q_spec = pl.BlockSpec((block, HD), at(lambda h, j: (j, h)))
    k_specs = [pl.BlockSpec((k.shape[0], HD), at(lambda h, j: (0, h))) for k in ks]
    v_specs = [pl.BlockSpec((v.shape[0], HD), at(lambda h, j: (0, heads + h))) for v in vs]
    stat = pl.BlockSpec((1, 1, block), at(lambda h, j: (h, 0, j)))
    acc = pl.BlockSpec((HD, block), at(lambda h, j: (h, j)))
    if last:
        out_specs = [pl.BlockSpec((1, *last[1:]), at(lambda h, j: (j, 0, 0, 0, 0)))]
        out_shape = [jax.ShapeDtypeStruct(last, jnp.bfloat16)]
    else:
        stat_shape = jax.ShapeDtypeStruct((heads, 1, rows), jnp.float32)
        out_specs = [stat, stat, acc]
        out_shape = [stat_shape, stat_shape, jax.ShapeDtypeStruct((width, rows), jnp.float32)]
    keys = sum(k.shape[0] for k in ks)
    return pl.pallas_call(
        functools.partial(attend_body, len(ks), first, bool(last)),
        grid=grid,
        in_specs=[q_spec, *k_specs, *v_specs, *(() if first else (stat, stat, acc))],
        out_specs=out_specs,
        out_shape=out_shape,
        cost_estimate=pl.CostEstimate(
            flops=4 * rows * keys * width,
            transcendentals=rows * keys * heads,
            bytes_accessed=2 * (rows + 2 * keys) * width,
        ),
        compiler_params=pltpu.CompilerParams(vmem_limit_bytes=16 << 20),
    )(q, *ks, *vs, *(() if first else state))


def join_project_body(order, place, part_ref, own_w, *refs):
    mine, mate = refs[:3], refs[3:6]
    own_ref, away_ref, attended, weights, sems = refs[6:]
    i = pl.program_id(0)
    x_size = part_ref.shape[0] // 2
    rows = part_ref.shape[1] // 2
    width = part_ref.shape[2] - HD
    block = weights.shape[2]

    def copies(n):
        at = pl.multiple_of(order[n] * block, block)
        yield pltpu.make_async_copy(
            own_w.at[:, pl.ds(at, block)], weights.at[n, pl.ds(0, width)], sems.at[n, 0]
        )
        for p, piece in enumerate(mine if n < 2 else mate):
            yield pltpu.make_async_copy(
                piece.at[:, pl.ds(n % 2 * block, block)],
                weights.at[n, pl.ds((p + 1) * width, width)],
                sems.at[n, p + 1],
            )

    @pl.when(i == 0)
    def _():
        for n in range(4):
            for copy in copies(n):
                copy.start()
        for side in range(2):
            yh = place[4] if side == 0 else 1 - place[4]
            at = pl.ds(pl.multiple_of(yh * rows, rows), rows)
            for p in range(x_size):
                a = part_ref[place[p], at, :].astype(jnp.float32)
                b = part_ref[x_size + place[p], at, :].astype(jnp.float32)
                for h in range(width // HD):
                    k = width + 3 * h
                    lse_a = a[:, k : k + 1] + a[:, k + 1 : k + 2] + a[:, k + 2 : k + 3]
                    lse_b = b[:, k : k + 1] + b[:, k + 1 : k + 2] + b[:, k + 2 : k + 3]
                    share = 1.0 / (1.0 + jnp.exp2(lse_b - lse_a))
                    cols = slice(h * HD, (h + 1) * HD)
                    joined = b[:, cols] + share * (a[:, cols] - b[:, cols])
                    to = slice(p * width + h * HD, p * width + (h + 1) * HD)
                    attended[side * rows : (side + 1) * rows, to] = joined.astype(jnp.bfloat16)

    for n in range(4):

        @pl.when(i == n)
        def _(n=n):
            for copy in copies(n):
                copy.wait()
            out = jnp.dot(attended[...], weights[n], preferred_element_type=jnp.float32)
            own_ref[...] = out[:rows]
            away_ref[...] = out[rows:].astype(jnp.bfloat16)


def join_project(parts, own_w, mine, mate, order, place):
    n, both, wide = parts.shape
    width, d_model = own_w.shape
    block, rows = d_model // 4, both // 2
    out = pl.BlockSpec((rows, block), lambda i, order, place: (0, order[i]))
    far_spec = pl.BlockSpec(memory_space=pltpu.MemorySpace.HBM)
    return pl.pallas_call(
        join_project_body,
        grid_spec=pltpu.PrefetchScalarGridSpec(
            num_scalar_prefetch=2,
            grid=(4,),
            in_specs=[
                pl.BlockSpec((n, both, wide), lambda i, order, place: (0, 0, 0)),
                *[far_spec] * 7,
            ],
            out_specs=[out, out],
            scratch_shapes=[
                pltpu.VMEM((both, 4 * width), jnp.bfloat16),
                pltpu.VMEM((4, 4 * width, block), jnp.bfloat16),
                pltpu.SemaphoreType.DMA((4, 4)),
            ],
        ),
        out_shape=[
            jax.ShapeDtypeStruct((rows, d_model), jnp.float32),
            jax.ShapeDtypeStruct((rows, d_model), jnp.bfloat16),
        ],
        cost_estimate=pl.CostEstimate(
            flops=8 * both * width * d_model, transcendentals=0, bytes_accessed=8 * width * d_model
        ),
        compiler_params=pltpu.CompilerParams(vmem_limit_bytes=30 << 20),
    )(order, place, parts, own_w, *mine, *mate)


def stream_norm_body(own_ref, other_ref, residual_ref, vectors_ref, stream_ref, normed_ref):
    gate, bias, scale, shift_by = (vectors_ref[i : i + 1, :] for i in range(4))
    proj = own_ref[...] + other_ref[...].astype(jnp.float32)
    stream = residual_ref[...].astype(jnp.float32) + gate * (proj + bias)
    center = jnp.mean(stream, axis=-1, keepdims=True)
    off = stream - center
    spread = jnp.mean(off * off, axis=-1, keepdims=True)
    normed = off * lax.rsqrt(spread + 1e-06) * (1.0 + scale) + shift_by
    stream_ref[...] = stream
    normed_ref[...] = normed.astype(jnp.bfloat16)


def stream_norm(own, other, residual, vectors, block=16):
    rows, d_model = own.shape
    row = pl.BlockSpec((block, d_model), lambda i: (i, 0))
    return pl.pallas_call(
        stream_norm_body,
        grid=(rows // block,),
        in_specs=[row, row, row, pl.BlockSpec(vectors.shape, lambda i: (0, 0))],
        out_specs=[row, row],
        out_shape=[
            jax.ShapeDtypeStruct((rows, d_model), jnp.float32),
            jax.ShapeDtypeStruct((rows, d_model), jnp.bfloat16),
        ],
        cost_estimate=pl.CostEstimate(
            flops=20 * rows * d_model, transcendentals=0, bytes_accessed=14 * rows * d_model
        ),
        compiler_params=pltpu.CompilerParams(vmem_limit_bytes=8 << 20),
    )(own, other, residual, vectors)


def mlp_body(order, x_ref, up_ref, down_ref, bias_ref, bias_far_ref, *refs):
    n = 4
    up_far, down_far, out_ref = refs[:n], refs[n : n + 4], refs[n + 4]
    near, far, hid_near, hid_far, up_buf, down_buf, sems = refs[n + 5 :]
    i = pl.program_id(0)
    quarter = up_ref.shape[0]

    first = down_far[0].shape[1] - quarter

    def copies(j):
        sem = sems.at[j, 0]
        if j < n:
            yield pltpu.make_async_copy(up_far[j], up_buf.at[j], sem)
            return
        a, b = down_far[(j - n) // 2 * 2 : (j - n) // 2 * 2 + 2]
        to = down_buf.at[j - n]
        if j % 2 == 0:
            yield pltpu.make_async_copy(a.at[:, pl.ds(0, quarter)], to, sem)
        else:
            yield pltpu.make_async_copy(a.at[:, pl.ds(quarter, first)], to.at[:, pl.ds(0, first)], sem)
            yield pltpu.make_async_copy(b, to.at[:, pl.ds(first, quarter - first)], sems.at[j, 1])

    @pl.when(i == 0)
    def _():
        for j in range(2 * n):
            for copy in copies(j):
                copy.start()
        near[...] = jnp.broadcast_to(bias_ref[...], near.shape)
        far[...] = jnp.broadcast_to(bias_far_ref[...], far.shape)

    for j in range(2 * n):

        @pl.when(i == j)
        def _(j=j):
            for copy in copies(j):
                copy.wait()

    @pl.when(i < n)
    def _():
        at = pl.multiple_of(i * quarter, quarter)
        near[...] += jnp.dot(
            x_ref[:, pl.ds(at, quarter)], up_ref[...], preferred_element_type=jnp.float32
        )
        at = pl.multiple_of(order[i] * quarter, quarter)
        far[...] += jnp.dot(
            x_ref[:, pl.ds(at, quarter)], up_buf[i], preferred_element_type=jnp.float32
        )

    @pl.when(i == n - 1)
    def _():
        hid_near[...] = jax.nn.gelu(near[...], approximate=True).astype(jnp.bfloat16)
        hid_far[...] = jax.nn.gelu(far[...], approximate=True).astype(jnp.bfloat16)

    @pl.when(i >= n)
    def _():
        out_ref[...] = (
            jnp.dot(hid_near[...], down_ref[...], preferred_element_type=jnp.float32)
            + jnp.dot(hid_far[...], down_buf[i - n], preferred_element_type=jnp.float32)
        ).astype(jnp.bfloat16)


def mlp(x, up, down, bias, bias_far, up_far, down_far, order):
    rows, d_model = x.shape
    hidden = up.shape[1]
    n = len(up_far)
    quarter = d_model // n
    whole = lambda i, order: (0, 0)
    column = lambda i, order: (0, order[jnp.maximum(i, n)])
    far_spec = pl.BlockSpec(memory_space=pltpu.MemorySpace.HBM)
    return pl.pallas_call(
        mlp_body,
        grid_spec=pltpu.PrefetchScalarGridSpec(
            num_scalar_prefetch=1,
            grid=(2 * n,),
            in_specs=[
                pl.BlockSpec((rows, d_model), whole),
                pl.BlockSpec((quarter, hidden), lambda i, order: (jnp.minimum(i, n - 1), 0)),
                pl.BlockSpec((hidden, quarter), column),
                pl.BlockSpec((1, hidden), whole),
                pl.BlockSpec((1, hidden), whole),
                *[far_spec] * (n + 4),
            ],
            out_specs=pl.BlockSpec((rows, quarter), column),
            scratch_shapes=[
                pltpu.VMEM((rows, hidden), jnp.float32),
                pltpu.VMEM((rows, hidden), jnp.float32),
                pltpu.VMEM((rows, hidden), jnp.bfloat16),
                pltpu.VMEM((rows, hidden), jnp.bfloat16),
                pltpu.VMEM((n, quarter, hidden), jnp.bfloat16),
                pltpu.VMEM((n, hidden, quarter), jnp.bfloat16),
                pltpu.SemaphoreType.DMA((2 * n, 2)),
            ],
        ),
        out_shape=jax.ShapeDtypeStruct((rows, d_model), jnp.bfloat16),
        cost_estimate=pl.CostEstimate(
            flops=8 * rows * d_model * hidden,
            transcendentals=rows * hidden * 2,
            bytes_accessed=8 * d_model * hidden,
        ),
        compiler_params=pltpu.CompilerParams(vmem_limit_bytes=30 << 20),
    )(order, x, up, down, bias.reshape(1, -1), bias_far.reshape(1, -1), *up_far, *down_far)


def shift(array, axis, size, by):
    return lax.ppermute(array, axis, [(i, (i + by) % size) for i in range(size)])


def cross(array):
    return lax.ppermute(array, ("yl", "yh"), [(0, 3), (3, 0), (1, 2), (2, 1)])


def pieces_body(place, up, down, out, *refs):
    dests, bufs, sems = refs[:4], refs[4:8], refs[8]
    half = out.shape[1] // 2
    start = pl.multiple_of(place[0] * half, half)
    rows = dests[0].shape[0]
    first = dests[1].shape[1]
    sources = (
        up.at[pl.ds(pl.multiple_of(place[1] * rows, rows), rows)],
        down.at[:, pl.ds(start, first)],
        down.at[:, pl.ds(start + first, half - first)],
        out.at[:, pl.ds(start, half)],
    )
    reads = [pltpu.make_async_copy(a, b, sems.at[0, i]) for i, (a, b) in enumerate(zip(sources, bufs))]
    writes = [pltpu.make_async_copy(a, b, sems.at[1, i]) for i, (a, b) in enumerate(zip(bufs, dests))]
    for copy in reads:
        copy.start()
    for read, write in zip(reads, writes):
        read.wait()
        write.start()
    for copy in writes:
        copy.wait()


def pieces_of(place, up, down, out, down_most):
    d_model, hidden = up.shape
    half = d_model // 2
    hbm = pl.BlockSpec(memory_space=pltpu.MemorySpace.HBM)
    shapes = (
        (d_model // 4, hidden),
        (hidden, down_most),
        (hidden, half - down_most),
        (out.shape[0], half),
    )
    return pl.pallas_call(
        pieces_body,
        grid_spec=pltpu.PrefetchScalarGridSpec(
            num_scalar_prefetch=1,
            grid=(1,),
            in_specs=[hbm] * 3,
            out_specs=[hbm] * 4,
            scratch_shapes=[
                *[pltpu.VMEM(shape, up.dtype) for shape in shapes],
                pltpu.SemaphoreType.DMA((2, 4)),
            ],
        ),
        out_shape=[jax.ShapeDtypeStruct(shape, up.dtype) for shape in shapes],
        compiler_params=pltpu.CompilerParams(vmem_limit_bytes=8 << 20),
    )(place, up, down, out)


tie = lax.optimization_barrier


def gather_x(rows):
    n = rows.shape[0] // 2
    left = shift(rows, "x", 4, 1)
    right = shift(rows, "x", 4, 3)
    far = jnp.concatenate([shift(left[:n], "x", 4, 1), shift(right[n:], "x", 4, 3)], axis=0)
    return rows, left, right, far


def shards(
    img_query,
    img_key,
    img_value,
    text_key,
    text_value,
    residual_in,
    mod_shift,
    mod_scale,
    gate_attn,
    gate_mlp,
    out_weight,
    out_bias,
    up_weight,
    up_bias,
    down_weight,
    down_bias,
):
    yl_at, yh_at, core = lax.axis_index("yl"), lax.axis_index("yh"), lax.axis_index("dp")
    rows_own, width = img_query.shape
    row_block, d_model = residual_in.shape

    vectors = jnp.stack([gate_attn, out_bias, mod_scale, mod_shift])
    order = jnp.bitwise_xor(
        jnp.array([2, 2, 2, 2, 0, 0, 0, 0], jnp.int32) * (1 - yl_at)
        + core * jnp.array([1, 1, 1, 1, 2, 2, 2, 2], jnp.int32),
        jnp.array([0, 2, 1, 3, 0, 1, 2, 3], jnp.int32),
    )
    x_at = lax.axis_index("x")
    place = jnp.concatenate(
        [(x_at + jnp.array([0, 3, 1, 2], jnp.int32)) % 4, yh_at.reshape(1).astype(jnp.int32)]
    )
    up_first, down_first, down_late, out_half = pieces_of(
        jnp.stack([core, 2 * yl_at + core]), up_weight, down_weight, out_weight, d_model // 8 * 3
    )

    q_other = shift(img_query, "yl", 2, 1)
    own = jnp.concatenate(
        [
            jnp.concatenate([img_key, text_key], axis=0),
            jnp.concatenate([img_value, text_value], axis=0),
        ],
        axis=1,
    )
    cut = -(-own.shape[0] // 32) * 16

    def around(up, down):
        return [shift(up, "z", 8, 1), shift(down, "z", 8, 7)]

    one = around(own, own)
    up_a = cross(up_first)
    out_l = shift(out_half, "x", 4, 1)
    out_r = shift(out_half, "x", 4, 3)
    one, q_other = tie((one, q_other))
    queries = jnp.where(
        yl_at == 0,
        jnp.concatenate([img_query, q_other], axis=0),
        jnp.concatenate([q_other, img_query], axis=0),
    )
    two = around(*one)
    state = attend(queries, [own], None)
    state = attend(queries, one, state)
    two, state, up_a, out_l, out_r, down_first, out_half = tie(
        (two, state, up_a, out_l, out_r, down_first, out_half)
    )
    three = around(*two)
    down_a = cross(down_first)
    up_b = shift(up_a, "yl", 2, 1)
    out_f = shift(out_half, "x", 4, 2)
    state = attend(queries, two, state)
    three, state = tie((three, state))
    four = around(three[0][:cut], three[1][cut:])
    state = attend(queries, three, state)
    four, state = tie((four, state))
    shape = (2, 4, 2, row_block, width + HD)
    (part,) = attend(queries, four, state, shape)
    out_mine = [out_l, out_r, out_f]
    part, down_a, up_a, up_b, out_mine, down_late = tie(
        (part, down_a, up_a, up_b, out_mine, down_late)
    )
    out_mate = [shift(piece, "dp", 2, 1) for piece in out_mine]
    down_b = cross(down_late)

    parts = lax.all_to_all(
        part.reshape(8, 2 * row_block, width + HD), ("yl", "x"), split_axis=0, concat_axis=0, tiled=True
    )
    parts, out_mate = tie((parts, out_mate))
    proj_own, proj_away = join_project(parts, out_weight, out_mine, out_mate, order[4:], place)
    proj_away, down_b = tie((proj_away, down_b))
    proj_other = shift(proj_away, "yh", 2, 1)
    up_far = [up_a, up_b, shift(up_a, "dp", 2, 1), shift(up_b, "dp", 2, 1)]
    down_far = [down_a, down_b, shift(down_a, "dp", 2, 1), shift(down_b, "dp", 2, 1)]
    bias_far = cross(up_bias)
    proj_other, up_far, down_far = tie((proj_other, up_far, down_far))
    stream, normed = stream_norm(proj_own, proj_other, residual_in, vectors)
    everyone = jnp.concatenate(gather_x(normed), axis=0)
    out = mlp(everyone, up_weight, down_weight, up_bias, bias_far, up_far, down_far, order)
    blocks = out.reshape(4, row_block, d_model)
    total = blocks[0].astype(jnp.float32)
    total = total + shift(blocks[1], "x", 4, 3).astype(jnp.float32)
    total = total + shift(blocks[2], "x", 4, 1).astype(jnp.float32)
    total = total + shift(blocks[3], "x", 4, 2).astype(jnp.float32)
    return (stream + gate_mlp * (total + down_bias)).astype(jnp.bfloat16)


def solution(mesh):
    fine = Mesh(mesh.devices.reshape([n for _, n in FINE]), [name for name, _ in FINE])
    seq, tp = ("yl", "z"), ("yh", "x")
    tokens = P(("dp", *seq), tp)
    rows = P(("dp", *seq, *tp), None)
    in_specs = (
        tokens,
        tokens,
        tokens,
        tokens,
        tokens,
        rows,
        P("dp"),
        P("dp"),
        P("dp"),
        P("dp"),
        P(tp, None),
        P(),
        P(None, tp),
        P(tp),
        P(tp, None),
        P(),
    )
    return jax.shard_map(shards, mesh=fine, in_specs=in_specs, out_specs=rows, check_vma=False)
```

```python
import functools
import math

import jax
import jax.numpy as jnp
from jax import lax
from jax.experimental import pallas as pl
from jax.experimental.pallas import tpu as pltpu
from jax.sharding import Mesh, PartitionSpec as P

HD = 128
LOG2E = math.log2(math.e)
SCORE_TO_LOG2 = LOG2E / math.sqrt(HD)

FINE = (("yl", 2), ("z", 8), ("yh", 2), ("x", 4), ("dp", 2))


def store_part(o_ref, part, lse):
    h = pl.program_id(1)
    terms = []
    rest = lse
    for _ in range(3):
        terms.append(rest.astype(jnp.bfloat16).astype(jnp.float32))
        rest = rest - terms[-1]
    row = lax.broadcasted_iota(jnp.int32, (HD, lse.shape[1]), 0) - 3 * h
    stats = jnp.zeros((HD, lse.shape[1]), jnp.float32)
    for k, term in enumerate(terms):
        stats = jnp.where(row == k, term, stats)
    stats = stats.T.astype(jnp.bfloat16)
    _, x_size, yh_size, rows, width = o_ref.shape
    for x in range(x_size):
        for yh in range(yh_size):
            at = slice((yh * x_size + x) * rows, (yh * x_size + x + 1) * rows)
            o_ref[0, x, yh, :, pl.ds(pl.multiple_of(h * HD, HD), HD)] = part[at]

            @pl.when(h == 0)
            def _(x=x, yh=yh, at=at):
                o_ref[0, x, yh, :, width - HD :] = stats[at]

            @pl.when(h > 0)
            def _(x=x, yh=yh, at=at):
                o_ref[0, x, yh, :, width - HD :] += stats[at]


def attend_body(pieces, first, last, *refs):
    q_ref = refs[0]
    k_refs = refs[1 : 1 + pieces]
    v_refs = refs[1 + pieces : 1 + 2 * pieces]
    at = 1 + 2 * pieces
    if not first:
        m_in, l_in, acc_in = refs[at : at + 3]
        at += 3
    outs = refs[at:]
    q = q_ref[...]
    scores = [
        lax.dot_general(k[...], q, (((1,), (1,)), ((), ())), preferred_element_type=jnp.float32)
        for k in k_refs
    ]
    m = functools.reduce(jnp.maximum, [jnp.max(s, axis=0, keepdims=True) for s in scores])
    if not first:
        m_old = m_in[0]
        m = jnp.maximum(m, m_old)
    den = None
    acc = None
    for s, v in zip(scores, v_refs):
        e = jnp.exp2((s - m) * SCORE_TO_LOG2)
        part = jnp.sum(e, axis=0, keepdims=True)
        den = part if den is None else den + part
        mixed = lax.dot_general(
            v[...],
            e.astype(jnp.bfloat16),
            (((0,), (0,)), ((), ())),
            preferred_element_type=jnp.float32,
        )
        acc = mixed if acc is None else acc + mixed
    if not first:
        factor = jnp.exp2((m_old - m) * SCORE_TO_LOG2)
        den = den + factor * l_in[0]
        acc = acc + factor * acc_in[...]
    if last:
        store_part(outs[0], (acc / den).T.astype(jnp.bfloat16), m * SCORE_TO_LOG2 + jnp.log2(den))
    else:
        m_out, l_out, acc_out = outs
        m_out[0] = m
        l_out[0] = den
        acc_out[...] = acc


def attend(q, pairs, state, last=None, block=512):
    rows, width = q.shape
    heads = width // HD
    ks = vs = pairs
    first = state is None
    if last:
        grid, at = (rows // block, heads), lambda f: lambda j, h: f(h, j)
    else:
        grid, at = (heads, rows // block), lambda f: f
    q_spec = pl.BlockSpec((block, HD), at(lambda h, j: (j, h)))
    k_specs = [pl.BlockSpec((k.shape[0], HD), at(lambda h, j: (0, h))) for k in ks]
    v_specs = [pl.BlockSpec((v.shape[0], HD), at(lambda h, j: (0, heads + h))) for v in vs]
    stat = pl.BlockSpec((1, 1, block), at(lambda h, j: (h, 0, j)))
    acc = pl.BlockSpec((HD, block), at(lambda h, j: (h, j)))
    if last:
        out_specs = [pl.BlockSpec((1, *last[1:]), at(lambda h, j: (j, 0, 0, 0, 0)))]
        out_shape = [jax.ShapeDtypeStruct(last, jnp.bfloat16)]
    else:
        stat_shape = jax.ShapeDtypeStruct((heads, 1, rows), jnp.float32)
        out_specs = [stat, stat, acc]
        out_shape = [stat_shape, stat_shape, jax.ShapeDtypeStruct((width, rows), jnp.float32)]
    keys = sum(k.shape[0] for k in ks)
    return pl.pallas_call(
        functools.partial(attend_body, len(ks), first, bool(last)),
        grid=grid,
        in_specs=[q_spec, *k_specs, *v_specs, *(() if first else (stat, stat, acc))],
        out_specs=out_specs,
        out_shape=out_shape,
        cost_estimate=pl.CostEstimate(
            flops=4 * rows * keys * width,
            transcendentals=rows * keys * heads,
            bytes_accessed=2 * (rows + 2 * keys) * width,
        ),
        compiler_params=pltpu.CompilerParams(vmem_limit_bytes=16 << 20),
    )(q, *ks, *vs, *(() if first else state))


def join_project_body(order, place, part_ref, own_w, *refs):
    mine, mate = refs[:3], refs[3:6]
    own_ref, away_ref, attended, weights, sems = refs[6:]
    i = pl.program_id(0)
    x_size = part_ref.shape[0] // 2
    rows = part_ref.shape[1] // 2
    width = part_ref.shape[2] - HD
    block = weights.shape[2]

    def copies(n):
        at = pl.multiple_of(order[n] * block, block)
        yield pltpu.make_async_copy(
            own_w.at[:, pl.ds(at, block)], weights.at[n, pl.ds(0, width)], sems.at[n, 0]
        )
        for p, piece in enumerate(mine if n < 2 else mate):
            yield pltpu.make_async_copy(
                piece.at[:, pl.ds(n % 2 * block, block)],
                weights.at[n, pl.ds((p + 1) * width, width)],
                sems.at[n, p + 1],
            )

    @pl.when(i == 0)
    def _():
        for n in range(4):
            for copy in copies(n):
                copy.start()
        for side in range(2):
            yh = place[4] if side == 0 else 1 - place[4]
            at = pl.ds(pl.multiple_of(yh * rows, rows), rows)
            for p in range(x_size):
                a = part_ref[place[p], at, :].astype(jnp.float32)
                b = part_ref[x_size + place[p], at, :].astype(jnp.float32)
                for h in range(width // HD):
                    k = width + 3 * h
                    lse_a = a[:, k : k + 1] + a[:, k + 1 : k + 2] + a[:, k + 2 : k + 3]
                    lse_b = b[:, k : k + 1] + b[:, k + 1 : k + 2] + b[:, k + 2 : k + 3]
                    share = 1.0 / (1.0 + jnp.exp2(lse_b - lse_a))
                    cols = slice(h * HD, (h + 1) * HD)
                    joined = b[:, cols] + share * (a[:, cols] - b[:, cols])
                    to = slice(p * width + h * HD, p * width + (h + 1) * HD)
                    attended[side * rows : (side + 1) * rows, to] = joined.astype(jnp.bfloat16)

    for n in range(4):

        @pl.when(i == n)
        def _(n=n):
            for copy in copies(n):
                copy.wait()
            out = jnp.dot(attended[...], weights[n], preferred_element_type=jnp.float32)
            own_ref[...] = out[:rows]
            away_ref[...] = out[rows:].astype(jnp.bfloat16)


def join_project(parts, own_w, mine, mate, order, place):
    n, both, wide = parts.shape
    width, d_model = own_w.shape
    block, rows = d_model // 4, both // 2
    out = pl.BlockSpec((rows, block), lambda i, order, place: (0, order[i]))
    far_spec = pl.BlockSpec(memory_space=pltpu.MemorySpace.HBM)
    return pl.pallas_call(
        join_project_body,
        grid_spec=pltpu.PrefetchScalarGridSpec(
            num_scalar_prefetch=2,
            grid=(4,),
            in_specs=[
                pl.BlockSpec((n, both, wide), lambda i, order, place: (0, 0, 0)),
                *[far_spec] * 7,
            ],
            out_specs=[out, out],
            scratch_shapes=[
                pltpu.VMEM((both, 4 * width), jnp.bfloat16),
                pltpu.VMEM((4, 4 * width, block), jnp.bfloat16),
                pltpu.SemaphoreType.DMA((4, 4)),
            ],
        ),
        out_shape=[
            jax.ShapeDtypeStruct((rows, d_model), jnp.float32),
            jax.ShapeDtypeStruct((rows, d_model), jnp.bfloat16),
        ],
        cost_estimate=pl.CostEstimate(
            flops=8 * both * width * d_model, transcendentals=0, bytes_accessed=8 * width * d_model
        ),
        compiler_params=pltpu.CompilerParams(vmem_limit_bytes=30 << 20),
    )(order, place, parts, own_w, *mine, *mate)


def stream_norm_body(own_ref, other_ref, residual_ref, vectors_ref, stream_ref, normed_ref):
    gate, bias, scale, shift_by = (vectors_ref[i : i + 1, :] for i in range(4))
    proj = own_ref[...] + other_ref[...].astype(jnp.float32)
    stream = residual_ref[...].astype(jnp.float32) + gate * (proj + bias)
    center = jnp.mean(stream, axis=-1, keepdims=True)
    off = stream - center
    spread = jnp.mean(off * off, axis=-1, keepdims=True)
    normed = off * lax.rsqrt(spread + 1e-06) * (1.0 + scale) + shift_by
    stream_ref[...] = stream
    normed_ref[...] = normed.astype(jnp.bfloat16)


def stream_norm(own, other, residual, vectors, block=16):
    rows, d_model = own.shape
    row = pl.BlockSpec((block, d_model), lambda i: (i, 0))
    return pl.pallas_call(
        stream_norm_body,
        grid=(rows // block,),
        in_specs=[row, row, row, pl.BlockSpec(vectors.shape, lambda i: (0, 0))],
        out_specs=[row, row],
        out_shape=[
            jax.ShapeDtypeStruct((rows, d_model), jnp.float32),
            jax.ShapeDtypeStruct((rows, d_model), jnp.bfloat16),
        ],
        cost_estimate=pl.CostEstimate(
            flops=20 * rows * d_model, transcendentals=0, bytes_accessed=14 * rows * d_model
        ),
        compiler_params=pltpu.CompilerParams(vmem_limit_bytes=8 << 20),
    )(own, other, residual, vectors)


def mlp_body(order, x_ref, up_ref, down_ref, bias_ref, bias_far_ref, *refs):
    n = 4
    up_far, down_far, out_ref = refs[:n], refs[n : n + 4], refs[n + 4]
    near, far, hid_near, hid_far, up_buf, down_buf, sems = refs[n + 5 :]
    i = pl.program_id(0)
    quarter = up_ref.shape[0]

    first = down_far[0].shape[1] - quarter

    def copies(j):
        sem = sems.at[j, 0]
        if j < n:
            yield pltpu.make_async_copy(up_far[j], up_buf.at[j], sem)
            return
        a, b = down_far[(j - n) // 2 * 2 : (j - n) // 2 * 2 + 2]
        to = down_buf.at[j - n]
        if j % 2 == 0:
            yield pltpu.make_async_copy(a.at[:, pl.ds(0, quarter)], to, sem)
        else:
            yield pltpu.make_async_copy(a.at[:, pl.ds(quarter, first)], to.at[:, pl.ds(0, first)], sem)
            yield pltpu.make_async_copy(b, to.at[:, pl.ds(first, quarter - first)], sems.at[j, 1])

    for j in range(2 * n):

        @pl.when(i == max(j - 2, 0))
        def _(j=j):
            for copy in copies(j):
                copy.start()

    @pl.when(i == 0)
    def _():
        near[...] = jnp.broadcast_to(bias_ref[...], near.shape)
        far[...] = jnp.broadcast_to(bias_far_ref[...], far.shape)

    for j in range(2 * n):

        @pl.when(i == j)
        def _(j=j):
            for copy in copies(j):
                copy.wait()

    @pl.when(i < n)
    def _():
        at = pl.multiple_of(i * quarter, quarter)
        near[...] += jnp.dot(
            x_ref[:, pl.ds(at, quarter)], up_ref[...], preferred_element_type=jnp.float32
        )
        at = pl.multiple_of(order[i] * quarter, quarter)
        far[...] += jnp.dot(
            x_ref[:, pl.ds(at, quarter)], up_buf[i], preferred_element_type=jnp.float32
        )

    @pl.when(i == n - 1)
    def _():
        hid_near[...] = jax.nn.gelu(near[...], approximate=True).astype(jnp.bfloat16)
        hid_far[...] = jax.nn.gelu(far[...], approximate=True).astype(jnp.bfloat16)

    @pl.when(i >= n)
    def _():
        out_ref[...] = (
            jnp.dot(hid_near[...], down_ref[...], preferred_element_type=jnp.float32)
            + jnp.dot(hid_far[...], down_buf[i - n], preferred_element_type=jnp.float32)
        ).astype(jnp.bfloat16)


def mlp(x, up, down, bias, bias_far, up_far, down_far, order):
    rows, d_model = x.shape
    hidden = up.shape[1]
    n = len(up_far)
    quarter = d_model // n
    whole = lambda i, order: (0, 0)
    column = lambda i, order: (0, order[jnp.maximum(i, n)])
    far_spec = pl.BlockSpec(memory_space=pltpu.MemorySpace.HBM)
    return pl.pallas_call(
        mlp_body,
        grid_spec=pltpu.PrefetchScalarGridSpec(
            num_scalar_prefetch=1,
            grid=(2 * n,),
            in_specs=[
                pl.BlockSpec((rows, d_model), whole),
                pl.BlockSpec((quarter, hidden), lambda i, order: (jnp.minimum(i, n - 1), 0)),
                pl.BlockSpec((hidden, quarter), column),
                pl.BlockSpec((1, hidden), whole),
                pl.BlockSpec((1, hidden), whole),
                *[far_spec] * (n + 4),
            ],
            out_specs=pl.BlockSpec((rows, quarter), column),
            scratch_shapes=[
                pltpu.VMEM((rows, hidden), jnp.float32),
                pltpu.VMEM((rows, hidden), jnp.float32),
                pltpu.VMEM((rows, hidden), jnp.bfloat16),
                pltpu.VMEM((rows, hidden), jnp.bfloat16),
                pltpu.VMEM((n, quarter, hidden), jnp.bfloat16),
                pltpu.VMEM((n, hidden, quarter), jnp.bfloat16),
                pltpu.SemaphoreType.DMA((2 * n, 2)),
            ],
        ),
        out_shape=jax.ShapeDtypeStruct((rows, d_model), jnp.bfloat16),
        cost_estimate=pl.CostEstimate(
            flops=8 * rows * d_model * hidden,
            transcendentals=rows * hidden * 2,
            bytes_accessed=8 * d_model * hidden,
        ),
        compiler_params=pltpu.CompilerParams(vmem_limit_bytes=46 << 20),
    )(order, x, up, down, bias.reshape(1, -1), bias_far.reshape(1, -1), *up_far, *down_far)


def shift(array, axis, size, by):
    return lax.ppermute(array, axis, [(i, (i + by) % size) for i in range(size)])


def cross(array):
    return lax.ppermute(array, ("yl", "yh"), [(0, 3), (3, 0), (1, 2), (2, 1)])


def part_of(array, parts, index, axis):
    n = array.shape[axis] // parts
    return lax.dynamic_slice_in_dim(array, index * n, n, axis)


def half_of(array, index, axis, start, stop):
    n = array.shape[axis] // 2
    return lax.dynamic_slice_in_dim(array, index * n + start, stop - start, axis)


tie = lax.optimization_barrier


def gather_x(rows):
    n = rows.shape[0] // 2
    left = shift(rows, "x", 4, 1)
    right = shift(rows, "x", 4, 3)
    far = jnp.concatenate([shift(left[:n], "x", 4, 1), shift(right[n:], "x", 4, 3)], axis=0)
    return rows, left, right, far


def shards(
    img_query,
    img_key,
    img_value,
    text_key,
    text_value,
    residual_in,
    mod_shift,
    mod_scale,
    gate_attn,
    gate_mlp,
    out_weight,
    out_bias,
    up_weight,
    up_bias,
    down_weight,
    down_bias,
):
    yl_at, yh_at, core = lax.axis_index("yl"), lax.axis_index("yh"), lax.axis_index("dp")
    rows_own, width = img_query.shape
    row_block, d_model = residual_in.shape

    vectors = jnp.stack([gate_attn, out_bias, mod_scale, mod_shift])
    order = jnp.bitwise_xor(
        jnp.array([2, 2, 2, 2, 0, 0, 0, 0], jnp.int32) * (1 - yl_at)
        + core * jnp.array([1, 1, 1, 1, 2, 2, 2, 2], jnp.int32),
        jnp.array([0, 2, 1, 3, 0, 1, 2, 3], jnp.int32),
    )
    x_at = lax.axis_index("x")
    place = jnp.concatenate(
        [(x_at + jnp.array([0, 3, 1, 2], jnp.int32)) % 4, yh_at.reshape(1).astype(jnp.int32)]
    )
    down_most = d_model // 8 * 3
    out_half = part_of(out_weight, 2, core, 1)

    q_other = shift(img_query, "yl", 2, 1)
    own = jnp.concatenate(
        [
            jnp.concatenate([img_key, text_key], axis=0),
            jnp.concatenate([img_value, text_value], axis=0),
        ],
        axis=1,
    )
    cut = -(-own.shape[0] // 32) * 16

    def around(up, down):
        return [shift(up, "z", 8, 1), shift(down, "z", 8, 7)]

    one = around(own, own)
    up_a = cross(part_of(up_weight, 4, 2 * yl_at + core, 0))
    out_l = shift(out_half, "x", 4, 1)
    out_r = shift(out_half, "x", 4, 3)
    down_first = half_of(down_weight, core, 1, 0, down_most)
    down_late = half_of(down_weight, core, 1, down_most, d_model // 2)
    one, q_other, down_first, down_late = tie((one, q_other, down_first, down_late))
    queries = jnp.where(
        yl_at == 0,
        jnp.concatenate([img_query, q_other], axis=0),
        jnp.concatenate([q_other, img_query], axis=0),
    )
    two = around(*one)
    state = attend(queries, [own], None)
    state = attend(queries, one, state)
    two, state, up_a, out_l, out_r, down_first, out_half = tie(
        (two, state, up_a, out_l, out_r, down_first, out_half)
    )
    three = around(*two)
    down_a = cross(down_first)
    up_b = shift(up_a, "yl", 2, 1)
    out_f = shift(out_half, "x", 4, 2)
    state = attend(queries, two, state)
    three, state = tie((three, state))
    four = around(three[0][:cut], three[1][cut:])
    state = attend(queries, three, state)
    four, state = tie((four, state))
    shape = (2, 4, 2, row_block, width + HD)
    (part,) = attend(queries, four, state, shape)
    out_mine = [out_l, out_r, out_f]
    part, down_a, up_a, up_b, out_mine, down_late = tie(
        (part, down_a, up_a, up_b, out_mine, down_late)
    )
    out_mate = [shift(piece, "dp", 2, 1) for piece in out_mine]
    down_b = cross(down_late)

    parts = lax.all_to_all(
        part.reshape(8, 2 * row_block, width + HD), ("yl", "x"), split_axis=0, concat_axis=0, tiled=True
    )
    parts, out_mate = tie((parts, out_mate))
    proj_own, proj_away = join_project(parts, out_weight, out_mine, out_mate, order[4:], place)
    proj_away, down_b = tie((proj_away, down_b))
    proj_other = shift(proj_away, "yh", 2, 1)
    up_far = [up_a, up_b, shift(up_a, "dp", 2, 1), shift(up_b, "dp", 2, 1)]
    down_far = [down_a, down_b, shift(down_a, "dp", 2, 1), shift(down_b, "dp", 2, 1)]
    bias_far = cross(up_bias)
    proj_other, up_far, down_far = tie((proj_other, up_far, down_far))
    stream, normed = stream_norm(proj_own, proj_other, residual_in, vectors)
    everyone = jnp.concatenate(gather_x(normed), axis=0)
    out = mlp(everyone, up_weight, down_weight, up_bias, bias_far, up_far, down_far, order)
    blocks = out.reshape(4, row_block, d_model)
    total = blocks[0].astype(jnp.float32)
    total = total + shift(blocks[1], "x", 4, 3).astype(jnp.float32)
    total = total + shift(blocks[2], "x", 4, 1).astype(jnp.float32)
    total = total + shift(blocks[3], "x", 4, 2).astype(jnp.float32)
    return (stream + gate_mlp * (total + down_bias)).astype(jnp.bfloat16)


def solution(mesh):
    fine = Mesh(mesh.devices.reshape([n for _, n in FINE]), [name for name, _ in FINE])
    seq, tp = ("yl", "z"), ("yh", "x")
    tokens = P(("dp", *seq), tp)
    rows = P(("dp", *seq, *tp), None)
    in_specs = (
        tokens,
        tokens,
        tokens,
        tokens,
        tokens,
        rows,
        P("dp"),
        P("dp"),
        P("dp"),
        P("dp"),
        P(tp, None),
        P(),
        P(None, tp),
        P(tp),
        P(tp, None),
        P(),
    )
    return jax.shard_map(shards, mesh=fine, in_specs=in_specs, out_specs=rows, check_vma=False)
```

```python
import functools
import math

import jax
import jax.numpy as jnp
from jax import lax
from jax.experimental import pallas as pl
from jax.experimental.pallas import tpu as pltpu
from jax.sharding import Mesh, PartitionSpec as P

HD = 128
LOG2E = math.log2(math.e)
SCORE_TO_LOG2 = LOG2E / math.sqrt(HD)

FINE = (("yl", 2), ("z", 8), ("yh", 2), ("x", 4), ("dp", 2))


def store_part(o_ref, part, lse):
    h = pl.program_id(1)
    terms = []
    rest = lse
    for _ in range(3):
        terms.append(rest.astype(jnp.bfloat16).astype(jnp.float32))
        rest = rest - terms[-1]
    row = lax.broadcasted_iota(jnp.int32, (HD, lse.shape[1]), 0) - 3 * h
    stats = jnp.zeros((HD, lse.shape[1]), jnp.float32)
    for k, term in enumerate(terms):
        stats = jnp.where(row == k, term, stats)
    stats = stats.T.astype(jnp.bfloat16)
    _, x_size, yh_size, rows, width = o_ref.shape
    for x in range(x_size):
        for yh in range(yh_size):
            at = slice((yh * x_size + x) * rows, (yh * x_size + x + 1) * rows)
            o_ref[0, x, yh, :, pl.ds(pl.multiple_of(h * HD, HD), HD)] = part[at]

            @pl.when(h == 0)
            def _(x=x, yh=yh, at=at):
                o_ref[0, x, yh, :, width - HD :] = stats[at]

            @pl.when(h > 0)
            def _(x=x, yh=yh, at=at):
                o_ref[0, x, yh, :, width - HD :] += stats[at]


def attend_body(pieces, first, last, *refs):
    q_ref = refs[0]
    k_refs = refs[1 : 1 + pieces]
    v_refs = refs[1 + pieces : 1 + 2 * pieces]
    at = 1 + 2 * pieces
    if not first:
        m_in, l_in, acc_in = refs[at : at + 3]
        at += 3
    outs = refs[at:]
    q = q_ref[...]
    scores = [
        lax.dot_general(k[...], q, (((1,), (1,)), ((), ())), preferred_element_type=jnp.float32)
        for k in k_refs
    ]
    m = functools.reduce(jnp.maximum, [jnp.max(s, axis=0, keepdims=True) for s in scores])
    if not first:
        m_old = m_in[0]
        m = jnp.maximum(m, m_old)
    den = None
    acc = None
    for s, v in zip(scores, v_refs):
        e = jnp.exp2((s - m) * SCORE_TO_LOG2)
        part = jnp.sum(e, axis=0, keepdims=True)
        den = part if den is None else den + part
        mixed = lax.dot_general(
            v[...],
            e.astype(jnp.bfloat16),
            (((0,), (0,)), ((), ())),
            preferred_element_type=jnp.float32,
        )
        acc = mixed if acc is None else acc + mixed
    if not first:
        factor = jnp.exp2((m_old - m) * SCORE_TO_LOG2)
        den = den + factor * l_in[0]
        acc = acc + factor * acc_in[...]
    if last:
        store_part(outs[0], (acc / den).T.astype(jnp.bfloat16), m * SCORE_TO_LOG2 + jnp.log2(den))
    else:
        m_out, l_out, acc_out = outs
        m_out[0] = m
        l_out[0] = den
        acc_out[...] = acc


def attend(q, pairs, state, last=None, block=512):
    rows, width = q.shape
    heads = width // HD
    ks = vs = pairs
    first = state is None
    if last:
        grid, at = (rows // block, heads), lambda f: lambda j, h: f(h, j)
    else:
        grid, at = (heads, rows // block), lambda f: f
    q_spec = pl.BlockSpec((block, HD), at(lambda h, j: (j, h)))
    k_specs = [pl.BlockSpec((k.shape[0], HD), at(lambda h, j: (0, h))) for k in ks]
    v_specs = [pl.BlockSpec((v.shape[0], HD), at(lambda h, j: (0, heads + h))) for v in vs]
    stat = pl.BlockSpec((1, 1, block), at(lambda h, j: (h, 0, j)))
    acc = pl.BlockSpec((HD, block), at(lambda h, j: (h, j)))
    if last:
        out_specs = [pl.BlockSpec((1, *last[1:]), at(lambda h, j: (j, 0, 0, 0, 0)))]
        out_shape = [jax.ShapeDtypeStruct(last, jnp.bfloat16)]
    else:
        stat_shape = jax.ShapeDtypeStruct((heads, 1, rows), jnp.float32)
        out_specs = [stat, stat, acc]
        out_shape = [stat_shape, stat_shape, jax.ShapeDtypeStruct((width, rows), jnp.float32)]
    keys = sum(k.shape[0] for k in ks)
    return pl.pallas_call(
        functools.partial(attend_body, len(ks), first, bool(last)),
        grid=grid,
        in_specs=[q_spec, *k_specs, *v_specs, *(() if first else (stat, stat, acc))],
        out_specs=out_specs,
        out_shape=out_shape,
        cost_estimate=pl.CostEstimate(
            flops=4 * rows * keys * width,
            transcendentals=rows * keys * heads,
            bytes_accessed=2 * (rows + 2 * keys) * width,
        ),
        compiler_params=pltpu.CompilerParams(vmem_limit_bytes=16 << 20),
    )(q, *ks, *vs, *(() if first else state))


def join_project_body(order, place, part_ref, own_w, *refs):
    mine, mate = refs[:3], refs[3:6]
    own_ref, away_ref, attended, weights, sems = refs[6:]
    i = pl.program_id(0)
    x_size = part_ref.shape[0] // 2
    rows = part_ref.shape[1] // 2
    width = part_ref.shape[2] - HD
    block = weights.shape[2]

    def copies(n):
        at = pl.multiple_of(order[n] * block, block)
        yield pltpu.make_async_copy(
            own_w.at[:, pl.ds(at, block)], weights.at[n, pl.ds(0, width)], sems.at[n, 0]
        )
        for p, piece in enumerate(mine if n < 2 else mate):
            yield pltpu.make_async_copy(
                piece.at[:, pl.ds(n % 2 * block, block)],
                weights.at[n, pl.ds((p + 1) * width, width)],
                sems.at[n, p + 1],
            )

    @pl.when(i == 0)
    def _():
        for n in range(4):
            for copy in copies(n):
                copy.start()
        for side in range(2):
            yh = place[4] if side == 0 else 1 - place[4]
            at = pl.ds(pl.multiple_of(yh * rows, rows), rows)
            for p in range(x_size):
                a = part_ref[place[p], at, :].astype(jnp.float32)
                b = part_ref[x_size + place[p], at, :].astype(jnp.float32)
                for h in range(width // HD):
                    k = width + 3 * h
                    lse_a = a[:, k : k + 1] + a[:, k + 1 : k + 2] + a[:, k + 2 : k + 3]
                    lse_b = b[:, k : k + 1] + b[:, k + 1 : k + 2] + b[:, k + 2 : k + 3]
                    share = 1.0 / (1.0 + jnp.exp2(lse_b - lse_a))
                    cols = slice(h * HD, (h + 1) * HD)
                    joined = b[:, cols] + share * (a[:, cols] - b[:, cols])
                    to = slice(p * width + h * HD, p * width + (h + 1) * HD)
                    attended[side * rows : (side + 1) * rows, to] = joined.astype(jnp.bfloat16)

    for n in range(4):

        @pl.when(i == n)
        def _(n=n):
            for copy in copies(n):
                copy.wait()
            out = jnp.dot(attended[...], weights[n], preferred_element_type=jnp.float32)
            own_ref[...] = out[:rows]
            away_ref[...] = out[rows:].astype(jnp.bfloat16)


def join_project(parts, own_w, mine, mate, order, place):
    n, both, wide = parts.shape
    width, d_model = own_w.shape
    block, rows = d_model // 4, both // 2
    out = pl.BlockSpec((rows, block), lambda i, order, place: (0, order[i]))
    far_spec = pl.BlockSpec(memory_space=pltpu.MemorySpace.HBM)
    return pl.pallas_call(
        join_project_body,
        grid_spec=pltpu.PrefetchScalarGridSpec(
            num_scalar_prefetch=2,
            grid=(4,),
            in_specs=[
                pl.BlockSpec((n, both, wide), lambda i, order, place: (0, 0, 0)),
                *[far_spec] * 7,
            ],
            out_specs=[out, out],
            scratch_shapes=[
                pltpu.VMEM((both, 4 * width), jnp.bfloat16),
                pltpu.VMEM((4, 4 * width, block), jnp.bfloat16),
                pltpu.SemaphoreType.DMA((4, 4)),
            ],
        ),
        out_shape=[
            jax.ShapeDtypeStruct((rows, d_model), jnp.float32),
            jax.ShapeDtypeStruct((rows, d_model), jnp.bfloat16),
        ],
        cost_estimate=pl.CostEstimate(
            flops=8 * both * width * d_model, transcendentals=0, bytes_accessed=8 * width * d_model
        ),
        compiler_params=pltpu.CompilerParams(vmem_limit_bytes=30 << 20),
    )(order, place, parts, own_w, *mine, *mate)


def stream_norm_body(own_ref, other_ref, residual_ref, vectors_ref, stream_ref, normed_ref):
    gate, bias, scale, shift_by = (vectors_ref[i : i + 1, :] for i in range(4))
    proj = own_ref[...] + other_ref[...].astype(jnp.float32)
    stream = residual_ref[...].astype(jnp.float32) + gate * (proj + bias)
    center = jnp.mean(stream, axis=-1, keepdims=True)
    off = stream - center
    spread = jnp.mean(off * off, axis=-1, keepdims=True)
    normed = off * lax.rsqrt(spread + 1e-06) * (1.0 + scale) + shift_by
    stream_ref[...] = stream
    normed_ref[...] = normed.astype(jnp.bfloat16)


def stream_norm(own, other, residual, vectors, block=16):
    rows, d_model = own.shape
    row = pl.BlockSpec((block, d_model), lambda i: (i, 0))
    return pl.pallas_call(
        stream_norm_body,
        grid=(rows // block,),
        in_specs=[row, row, row, pl.BlockSpec(vectors.shape, lambda i: (0, 0))],
        out_specs=[row, row],
        out_shape=[
            jax.ShapeDtypeStruct((rows, d_model), jnp.float32),
            jax.ShapeDtypeStruct((rows, d_model), jnp.bfloat16),
        ],
        cost_estimate=pl.CostEstimate(
            flops=20 * rows * d_model, transcendentals=0, bytes_accessed=14 * rows * d_model
        ),
        compiler_params=pltpu.CompilerParams(vmem_limit_bytes=8 << 20),
    )(own, other, residual, vectors)


def start_ahead(i, copies, n):
    for j in range(n):

        @pl.when(i == max(j - 2, 0))
        def _(j=j):
            for copy in copies(j):
                copy.start()

    for j in range(n):

        @pl.when(i == j)
        def _(j=j):
            for copy in copies(j):
                copy.wait()


def up_body(n_rows, order, up_ref, bias_ref, bias_far_ref, *refs):
    n = 4
    row_refs, up_far, out_ref = refs[:n_rows], refs[n_rows : n_rows + n], refs[n_rows + n]
    x, near, far, up_buf, sems = refs[n_rows + n + 1 :]
    i = pl.program_id(0)
    quarter, hidden = up_ref.shape

    start_ahead(i, lambda j: [pltpu.make_async_copy(up_far[j], up_buf.at[j], sems.at[j])], n)

    @pl.when(i == 0)
    def _():
        at = 0
        for ref in row_refs:
            x[at : at + ref.shape[0]] = ref[...]
            at += ref.shape[0]
        near[...] = jnp.broadcast_to(bias_ref[...], near.shape)
        far[...] = jnp.broadcast_to(bias_far_ref[...], far.shape)

    at = pl.multiple_of(i * quarter, quarter)
    near[...] += jnp.dot(x[:, pl.ds(at, quarter)], up_ref[...], preferred_element_type=jnp.float32)
    at = pl.multiple_of(order[i] * quarter, quarter)
    far[...] += jnp.dot(x[:, pl.ds(at, quarter)], up_buf[i], preferred_element_type=jnp.float32)

    @pl.when(i == n - 1)
    def _():
        out_ref[:, :hidden] = jax.nn.gelu(near[...], approximate=True).astype(jnp.bfloat16)
        out_ref[:, hidden:] = jax.nn.gelu(far[...], approximate=True).astype(jnp.bfloat16)


def up_project(row_pieces, up, bias, bias_far, up_far, order):
    d_model, hidden = up.shape
    n = 4
    quarter = d_model // n
    rows = sum(piece.shape[0] for piece in row_pieces)
    whole = lambda i, order: (0, 0)
    return pl.pallas_call(
        functools.partial(up_body, len(row_pieces)),
        grid_spec=pltpu.PrefetchScalarGridSpec(
            num_scalar_prefetch=1,
            grid=(n,),
            in_specs=[
                pl.BlockSpec((quarter, hidden), lambda i, order: (i, 0)),
                pl.BlockSpec((1, hidden), whole),
                pl.BlockSpec((1, hidden), whole),
                *[pl.BlockSpec(piece.shape, whole) for piece in row_pieces],
                *[pl.BlockSpec(memory_space=pltpu.MemorySpace.HBM)] * n,
            ],
            out_specs=pl.BlockSpec((rows, 2 * hidden), whole),
            scratch_shapes=[
                pltpu.VMEM((rows, d_model), jnp.bfloat16),
                pltpu.VMEM((rows, hidden), jnp.float32),
                pltpu.VMEM((rows, hidden), jnp.float32),
                pltpu.VMEM((n, quarter, hidden), jnp.bfloat16),
                pltpu.SemaphoreType.DMA((n,)),
            ],
        ),
        out_shape=jax.ShapeDtypeStruct((rows, 2 * hidden), jnp.bfloat16),
        cost_estimate=pl.CostEstimate(
            flops=4 * rows * d_model * hidden,
            transcendentals=rows * hidden * 2,
            bytes_accessed=4 * d_model * hidden,
        ),
        compiler_params=pltpu.CompilerParams(vmem_limit_bytes=40 << 20),
    )(order, up, bias.reshape(1, -1), bias_far.reshape(1, -1), *row_pieces, *up_far)


def down_body(n_rows, order, down_ref, *refs):
    n = 4
    row_refs, down_far, out_ref = refs[:n_rows], refs[n_rows : n_rows + n], refs[n_rows + n]
    x, down_buf, sems = refs[n_rows + n + 1 :]
    i = pl.program_id(0)
    hidden, quarter = down_ref.shape
    first = down_far[0].shape[1] - quarter

    def copies(j):
        a, b = down_far[j // 2 * 2 : j // 2 * 2 + 2]
        to = down_buf.at[j]
        if j % 2 == 0:
            return [pltpu.make_async_copy(a.at[:, pl.ds(0, quarter)], to, sems.at[j, 0])]
        return [
            pltpu.make_async_copy(a.at[:, pl.ds(quarter, first)], to.at[:, pl.ds(0, first)], sems.at[j, 0]),
            pltpu.make_async_copy(b, to.at[:, pl.ds(first, quarter - first)], sems.at[j, 1]),
        ]

    start_ahead(i, copies, n)

    @pl.when(i == 0)
    def _():
        at = 0
        for ref in row_refs:
            x[at : at + ref.shape[0]] = ref[...]
            at += ref.shape[0]

    out_ref[...] = (
        jnp.dot(x[:, :hidden], down_ref[...], preferred_element_type=jnp.float32)
        + jnp.dot(x[:, hidden:], down_buf[i], preferred_element_type=jnp.float32)
    ).astype(jnp.bfloat16)


def down_project(row_pieces, down, down_far, order):
    hidden, d_model = down.shape
    n = 4
    quarter = d_model // n
    rows = sum(piece.shape[0] for piece in row_pieces)
    whole = lambda i, order: (0, 0)
    column = lambda i, order: (0, order[i])
    return pl.pallas_call(
        functools.partial(down_body, len(row_pieces)),
        grid_spec=pltpu.PrefetchScalarGridSpec(
            num_scalar_prefetch=1,
            grid=(n,),
            in_specs=[
                pl.BlockSpec((hidden, quarter), column),
                *[pl.BlockSpec(piece.shape, whole) for piece in row_pieces],
                *[pl.BlockSpec(memory_space=pltpu.MemorySpace.HBM)] * n,
            ],
            out_specs=pl.BlockSpec((rows, quarter), column),
            scratch_shapes=[
                pltpu.VMEM((rows, 2 * hidden), jnp.bfloat16),
                pltpu.VMEM((n, hidden, quarter), jnp.bfloat16),
                pltpu.SemaphoreType.DMA((n, 2)),
            ],
        ),
        out_shape=jax.ShapeDtypeStruct((rows, d_model), jnp.bfloat16),
        cost_estimate=pl.CostEstimate(
            flops=4 * rows * d_model * hidden, transcendentals=0, bytes_accessed=4 * d_model * hidden
        ),
        compiler_params=pltpu.CompilerParams(vmem_limit_bytes=40 << 20),
    )(order, down, *row_pieces, *down_far)


def shift(array, axis, size, by):
    return lax.ppermute(array, axis, [(i, (i + by) % size) for i in range(size)])


def cross(array):
    return lax.ppermute(array, ("yl", "yh"), [(0, 3), (3, 0), (1, 2), (2, 1)])


def part_of(array, parts, index, axis):
    n = array.shape[axis] // parts
    return lax.dynamic_slice_in_dim(array, index * n, n, axis)


def half_of(array, index, axis, start, stop):
    n = array.shape[axis] // 2
    return lax.dynamic_slice_in_dim(array, index * n + start, stop - start, axis)


tie = lax.optimization_barrier


def gather_x(rows):
    n = rows.shape[0] // 2
    left = shift(rows, "x", 4, 1)
    right = shift(rows, "x", 4, 3)
    far = [shift(left[:n], "x", 4, 1), shift(right[n:], "x", 4, 3)]
    return [rows, left, right], far


def shards(
    img_query,
    img_key,
    img_value,
    text_key,
    text_value,
    residual_in,
    mod_shift,
    mod_scale,
    gate_attn,
    gate_mlp,
    out_weight,
    out_bias,
    up_weight,
    up_bias,
    down_weight,
    down_bias,
):
    yl_at, yh_at, core = lax.axis_index("yl"), lax.axis_index("yh"), lax.axis_index("dp")
    rows_own, width = img_query.shape
    row_block, d_model = residual_in.shape

    vectors = jnp.stack([gate_attn, out_bias, mod_scale, mod_shift])
    order = jnp.bitwise_xor(
        jnp.array([2, 2, 2, 2, 0, 0, 0, 0], jnp.int32) * (1 - yl_at)
        + core * jnp.array([1, 1, 1, 1, 2, 2, 2, 2], jnp.int32),
        jnp.array([0, 2, 1, 3, 0, 1, 2, 3], jnp.int32),
    )
    x_at = lax.axis_index("x")
    place = jnp.concatenate(
        [(x_at + jnp.array([0, 3, 1, 2], jnp.int32)) % 4, yh_at.reshape(1).astype(jnp.int32)]
    )
    down_most = d_model // 8 * 3
    out_half = part_of(out_weight, 2, core, 1)

    q_other = shift(img_query, "yl", 2, 1)
    own = jnp.concatenate(
        [
            jnp.concatenate([img_key, text_key], axis=0),
            jnp.concatenate([img_value, text_value], axis=0),
        ],
        axis=1,
    )
    cut = -(-own.shape[0] // 32) * 16

    def around(up, down):
        return [shift(up, "z", 8, 1), shift(down, "z", 8, 7)]

    one = around(own, own)
    up_a = cross(part_of(up_weight, 4, 2 * yl_at + core, 0))
    out_l = shift(out_half, "x", 4, 1)
    out_r = shift(out_half, "x", 4, 3)
    down_first = half_of(down_weight, core, 1, 0, down_most)
    down_late = half_of(down_weight, core, 1, down_most, d_model // 2)
    one, q_other, down_first, down_late = tie((one, q_other, down_first, down_late))
    queries = jnp.where(
        yl_at == 0,
        jnp.concatenate([img_query, q_other], axis=0),
        jnp.concatenate([q_other, img_query], axis=0),
    )
    two = around(*one)
    state = attend(queries, [own], None)
    state = attend(queries, one, state)
    two, state = tie((two, state))
    three = around(*two)
    state, up_a, out_l, out_r, down_first, out_half = tie(
        (state, up_a, out_l, out_r, down_first, out_half)
    )
    down_a = cross(down_first)
    up_b = shift(up_a, "yl", 2, 1)
    out_f = shift(out_half, "x", 4, 2)
    state = attend(queries, two, state)
    three, state = tie((three, state))
    four = around(three[0][:cut], three[1][cut:])
    state = attend(queries, three, state)
    four, state = tie((four, state))
    shape = (2, 4, 2, row_block, width + HD)
    (part,) = attend(queries, four, state, shape)
    out_mine = [out_l, out_r, out_f]
    part, down_a, up_a, up_b, out_mine, down_late = tie(
        (part, down_a, up_a, up_b, out_mine, down_late)
    )
    out_mate = [shift(piece, "dp", 2, 1) for piece in out_mine]
    down_b = cross(down_late)

    parts = lax.all_to_all(
        part.reshape(8, 2 * row_block, width + HD), ("yl", "x"), split_axis=0, concat_axis=0, tiled=True
    )
    parts, out_mate, bias_far = tie((parts, out_mate, cross(up_bias)))
    proj_own, proj_away = join_project(parts, out_weight, out_mine, out_mate, order[4:], place)
    proj_away, down_b = tie((proj_away, down_b))
    proj_other = shift(proj_away, "yh", 2, 1)
    up_far = [up_a, up_b, shift(up_a, "dp", 2, 1), shift(up_b, "dp", 2, 1)]
    down_far = [down_a, down_b, shift(down_a, "dp", 2, 1), shift(down_b, "dp", 2, 1)]
    proj_other, up_far, down_far = tie((proj_other, up_far, down_far))
    stream, normed = stream_norm(proj_own, proj_other, residual_in, vectors)
    near_rows, far_rows = gather_x(normed)
    units = [
        up_project(part, up_weight, up_bias, bias_far, up_far, order[:4])
        for part in (near_rows, far_rows)
    ]
    out = down_project(units, down_weight, down_far, order[4:])
    blocks = out.reshape(4, row_block, d_model)
    total = blocks[0].astype(jnp.float32)
    total = total + shift(blocks[1], "x", 4, 3).astype(jnp.float32)
    total = total + shift(blocks[2], "x", 4, 1).astype(jnp.float32)
    total = total + shift(blocks[3], "x", 4, 2).astype(jnp.float32)
    return (stream + gate_mlp * (total + down_bias)).astype(jnp.bfloat16)


def solution(mesh):
    fine = Mesh(mesh.devices.reshape([n for _, n in FINE]), [name for name, _ in FINE])
    seq, tp = ("yl", "z"), ("yh", "x")
    tokens = P(("dp", *seq), tp)
    rows = P(("dp", *seq, *tp), None)
    in_specs = (
        tokens,
        tokens,
        tokens,
        tokens,
        tokens,
        rows,
        P("dp"),
        P("dp"),
        P("dp"),
        P("dp"),
        P(tp, None),
        P(),
        P(None, tp),
        P(tp),
        P(tp, None),
        P(),
    )
    return jax.shard_map(shards, mesh=fine, in_specs=in_specs, out_specs=rows, check_vma=False)
```

```python
import functools
import math

import jax
import jax.numpy as jnp
from jax import lax
from jax.experimental import pallas as pl
from jax.experimental.pallas import tpu as pltpu
from jax.sharding import Mesh, PartitionSpec as P

HD = 128
LOG2E = math.log2(math.e)
SCORE_TO_LOG2 = LOG2E / math.sqrt(HD)

FINE = (("yl", 2), ("z", 8), ("yh", 2), ("x", 4), ("dp", 2))


def split_three(value):
    terms = []
    for _ in range(3):
        terms.append(value.astype(jnp.bfloat16).astype(jnp.float32))
        value = value - terms[-1]
    return terms


def attend_body(pieces, block, first, last, *refs):
    q_ref = refs[0]
    kv_refs = refs[1 : 1 + pieces]
    at = 1 + pieces
    if not first:
        m_in, l_in, acc_in = refs[at : at + 3]
        at += 3
    outs = refs[at:]
    rows, width = q_ref.shape
    for j in range(rows // block):
        qs = slice(j * block, (j + 1) * block)
        stats = jnp.zeros((HD, block), jnp.float32)
        for h in range(width // HD):
            cols = slice(h * HD, (h + 1) * HD)
            v_cols = slice(width + h * HD, width + (h + 1) * HD)
            q = q_ref[qs, cols]
            scores = [
                lax.dot_general(
                    kv[:, cols], q, (((1,), (1,)), ((), ())), preferred_element_type=jnp.float32
                )
                for kv in kv_refs
            ]
            m = functools.reduce(jnp.maximum, [jnp.max(s, axis=0, keepdims=True) for s in scores])
            if not first:
                m_old = m_in[h, :, qs]
                m = jnp.maximum(m, m_old)
            den = None
            acc = None
            for s, kv in zip(scores, kv_refs):
                e = jnp.exp2((s - m) * SCORE_TO_LOG2)
                part = jnp.sum(e, axis=0, keepdims=True)
                den = part if den is None else den + part
                mixed = lax.dot_general(
                    kv[:, v_cols],
                    e.astype(jnp.bfloat16),
                    (((0,), (0,)), ((), ())),
                    preferred_element_type=jnp.float32,
                )
                acc = mixed if acc is None else acc + mixed
            if not first:
                factor = jnp.exp2((m_old - m) * SCORE_TO_LOG2)
                den = den + factor * l_in[h, :, qs]
                acc = acc + factor * acc_in[cols, qs]
            if not last:
                m_out, l_out, acc_out = outs
                m_out[h, :, qs] = m
                l_out[h, :, qs] = den
                acc_out[cols, qs] = acc
                continue
            store_part(outs[0], j, cols, (acc / den).T.astype(jnp.bfloat16))
            row = lax.broadcasted_iota(jnp.int32, (HD, block), 0)
            for k, term in enumerate(split_three(m * SCORE_TO_LOG2 + jnp.log2(den))):
                stats = jnp.where(row == 3 * h + k, term, stats)
        if last:
            store_part(outs[0], j, slice(width, width + HD), stats.T.astype(jnp.bfloat16))


def store_part(o_ref, j, cols, part):
    _, x_size, yh_size, rows, _ = o_ref.shape
    for x in range(x_size):
        for yh in range(yh_size):
            at = (yh * x_size + x) * rows
            o_ref[j, x, yh, :, cols] = part[at : at + rows]


def attend(q, pairs, state, last=None):
    rows, width = q.shape
    heads = width // HD
    first = state is None
    block = rows // last[0] if last else rows
    if last:
        out_shape = [jax.ShapeDtypeStruct(last, jnp.bfloat16)]
    else:
        stat_shape = jax.ShapeDtypeStruct((heads, 1, rows), jnp.float32)
        out_shape = [stat_shape, stat_shape, jax.ShapeDtypeStruct((width, rows), jnp.float32)]
    keys = sum(pair.shape[0] for pair in pairs)
    return pl.pallas_call(
        functools.partial(attend_body, len(pairs), block, first, bool(last)),
        out_shape=out_shape,
        cost_estimate=pl.CostEstimate(
            flops=4 * rows * keys * width,
            transcendentals=rows * keys * heads,
            bytes_accessed=2 * (rows + 2 * keys) * width,
        ),
        compiler_params=pltpu.CompilerParams(vmem_limit_bytes=24 << 20),
    )(q, *pairs, *(() if first else state))


def join_project_body(order, place, part_ref, own_w, *refs):
    mine, mate = refs[:3], refs[3:6]
    own_ref, away_ref, attended, weights, sems = refs[6:]
    i = pl.program_id(0)
    x_size = part_ref.shape[0] // 2
    rows = part_ref.shape[1] // 2
    width = part_ref.shape[2] - HD
    block = weights.shape[2]

    def copies(n):
        at = pl.multiple_of(order[n] * block, block)
        yield pltpu.make_async_copy(
            own_w.at[:, pl.ds(at, block)], weights.at[n, pl.ds(0, width)], sems.at[n, 0]
        )
        for p, piece in enumerate(mine if n < 2 else mate):
            yield pltpu.make_async_copy(
                piece.at[:, pl.ds(n % 2 * block, block)],
                weights.at[n, pl.ds((p + 1) * width, width)],
                sems.at[n, p + 1],
            )

    @pl.when(i == 0)
    def _():
        for n in range(4):
            for copy in copies(n):
                copy.start()
        for side in range(2):
            yh = place[4] if side == 0 else 1 - place[4]
            at = pl.ds(pl.multiple_of(yh * rows, rows), rows)
            for p in range(x_size):
                a = part_ref[place[p], at, :].astype(jnp.float32)
                b = part_ref[x_size + place[p], at, :].astype(jnp.float32)
                for h in range(width // HD):
                    k = width + 3 * h
                    lse_a = a[:, k : k + 1] + a[:, k + 1 : k + 2] + a[:, k + 2 : k + 3]
                    lse_b = b[:, k : k + 1] + b[:, k + 1 : k + 2] + b[:, k + 2 : k + 3]
                    share = 1.0 / (1.0 + jnp.exp2(lse_b - lse_a))
                    cols = slice(h * HD, (h + 1) * HD)
                    joined = b[:, cols] + share * (a[:, cols] - b[:, cols])
                    to = slice(p * width + h * HD, p * width + (h + 1) * HD)
                    attended[side * rows : (side + 1) * rows, to] = joined.astype(jnp.bfloat16)

    for n in range(4):

        @pl.when(i == n)
        def _(n=n):
            for copy in copies(n):
                copy.wait()
            out = jnp.dot(attended[...], weights[n], preferred_element_type=jnp.float32)
            own_ref[...] = out[:rows]
            away_ref[...] = out[rows:].astype(jnp.bfloat16)


def join_project(parts, own_w, mine, mate, order, place):
    n, both, wide = parts.shape
    width, d_model = own_w.shape
    block, rows = d_model // 4, both // 2
    out = pl.BlockSpec((rows, block), lambda i, order, place: (0, order[i]))
    far_spec = pl.BlockSpec(memory_space=pltpu.MemorySpace.HBM)
    return pl.pallas_call(
        join_project_body,
        grid_spec=pltpu.PrefetchScalarGridSpec(
            num_scalar_prefetch=2,
            grid=(4,),
            in_specs=[
                pl.BlockSpec((n, both, wide), lambda i, order, place: (0, 0, 0)),
                *[far_spec] * 7,
            ],
            out_specs=[out, out],
            scratch_shapes=[
                pltpu.VMEM((both, 4 * width), jnp.bfloat16),
                pltpu.VMEM((4, 4 * width, block), jnp.bfloat16),
                pltpu.SemaphoreType.DMA((4, 4)),
            ],
        ),
        out_shape=[
            jax.ShapeDtypeStruct((rows, d_model), jnp.float32),
            jax.ShapeDtypeStruct((rows, d_model), jnp.bfloat16),
        ],
        cost_estimate=pl.CostEstimate(
            flops=8 * both * width * d_model, transcendentals=0, bytes_accessed=8 * width * d_model
        ),
        compiler_params=pltpu.CompilerParams(vmem_limit_bytes=30 << 20),
    )(order, place, parts, own_w, *mine, *mate)


def stream_norm_body(own_ref, other_ref, residual_ref, vectors_ref, stream_ref, normed_ref):
    gate, bias, scale, shift_by = (vectors_ref[i : i + 1, :] for i in range(4))
    proj = own_ref[...] + other_ref[...].astype(jnp.float32)
    stream = residual_ref[...].astype(jnp.float32) + gate * (proj + bias)
    center = jnp.mean(stream, axis=-1, keepdims=True)
    off = stream - center
    spread = jnp.mean(off * off, axis=-1, keepdims=True)
    normed = off * lax.rsqrt(spread + 1e-06) * (1.0 + scale) + shift_by
    stream_ref[...] = stream
    normed_ref[...] = normed.astype(jnp.bfloat16)


def stream_norm(own, other, residual, vectors, block=16):
    rows, d_model = own.shape
    row = pl.BlockSpec((block, d_model), lambda i: (i, 0))
    return pl.pallas_call(
        stream_norm_body,
        grid=(rows // block,),
        in_specs=[row, row, row, pl.BlockSpec(vectors.shape, lambda i: (0, 0))],
        out_specs=[row, row],
        out_shape=[
            jax.ShapeDtypeStruct((rows, d_model), jnp.float32),
            jax.ShapeDtypeStruct((rows, d_model), jnp.bfloat16),
        ],
        cost_estimate=pl.CostEstimate(
            flops=20 * rows * d_model, transcendentals=0, bytes_accessed=14 * rows * d_model
        ),
        compiler_params=pltpu.CompilerParams(vmem_limit_bytes=8 << 20),
    )(own, other, residual, vectors)


def start_ahead(i, copies, n):
    for j in range(n):

        @pl.when(i == max(j - 2, 0))
        def _(j=j):
            for copy in copies(j):
                copy.start()

    for j in range(n):

        @pl.when(i == j)
        def _(j=j):
            for copy in copies(j):
                copy.wait()


def up_body(n_rows, order, up_ref, bias_ref, bias_far_ref, *refs):
    n = 4
    row_refs, up_far, out_ref = refs[:n_rows], refs[n_rows : n_rows + n], refs[n_rows + n]
    x, near, far, up_buf, sems = refs[n_rows + n + 1 :]
    i = pl.program_id(0)
    quarter, hidden = up_ref.shape

    start_ahead(i, lambda j: [pltpu.make_async_copy(up_far[j], up_buf.at[j], sems.at[j])], n)

    @pl.when(i == 0)
    def _():
        at = 0
        for ref in row_refs:
            x[at : at + ref.shape[0]] = ref[...]
            at += ref.shape[0]
        near[...] = jnp.broadcast_to(bias_ref[...], near.shape)
        far[...] = jnp.broadcast_to(bias_far_ref[...], far.shape)

    at = pl.multiple_of(i * quarter, quarter)
    near[...] += jnp.dot(x[:, pl.ds(at, quarter)], up_ref[...], preferred_element_type=jnp.float32)
    at = pl.multiple_of(order[i] * quarter, quarter)
    far[...] += jnp.dot(x[:, pl.ds(at, quarter)], up_buf[i], preferred_element_type=jnp.float32)

    @pl.when(i == n - 1)
    def _():
        out_ref[:, :hidden] = jax.nn.gelu(near[...], approximate=True).astype(jnp.bfloat16)
        out_ref[:, hidden:] = jax.nn.gelu(far[...], approximate=True).astype(jnp.bfloat16)


def up_project(row_pieces, up, bias, bias_far, up_far, order):
    d_model, hidden = up.shape
    n = 4
    quarter = d_model // n
    rows = sum(piece.shape[0] for piece in row_pieces)
    whole = lambda i, order: (0, 0)
    return pl.pallas_call(
        functools.partial(up_body, len(row_pieces)),
        grid_spec=pltpu.PrefetchScalarGridSpec(
            num_scalar_prefetch=1,
            grid=(n,),
            in_specs=[
                pl.BlockSpec((quarter, hidden), lambda i, order: (i, 0)),
                pl.BlockSpec((1, hidden), whole),
                pl.BlockSpec((1, hidden), whole),
                *[pl.BlockSpec(piece.shape, whole) for piece in row_pieces],
                *[pl.BlockSpec(memory_space=pltpu.MemorySpace.HBM)] * n,
            ],
            out_specs=pl.BlockSpec((rows, 2 * hidden), whole),
            scratch_shapes=[
                pltpu.VMEM((rows, d_model), jnp.bfloat16),
                pltpu.VMEM((rows, hidden), jnp.float32),
                pltpu.VMEM((rows, hidden), jnp.float32),
                pltpu.VMEM((n, quarter, hidden), jnp.bfloat16),
                pltpu.SemaphoreType.DMA((n,)),
            ],
        ),
        out_shape=jax.ShapeDtypeStruct((rows, 2 * hidden), jnp.bfloat16),
        cost_estimate=pl.CostEstimate(
            flops=4 * rows * d_model * hidden,
            transcendentals=rows * hidden * 2,
            bytes_accessed=4 * d_model * hidden,
        ),
        compiler_params=pltpu.CompilerParams(vmem_limit_bytes=40 << 20),
    )(order, up, bias.reshape(1, -1), bias_far.reshape(1, -1), *row_pieces, *up_far)


def down_body(n_rows, order, down_ref, *refs):
    n = 4
    row_refs, down_far, out_ref = refs[:n_rows], refs[n_rows : n_rows + n], refs[n_rows + n]
    x, down_buf, sems = refs[n_rows + n + 1 :]
    i = pl.program_id(0)
    hidden, quarter = down_ref.shape
    first = down_far[0].shape[1] - quarter

    def copies(j):
        a, b = down_far[j // 2 * 2 : j // 2 * 2 + 2]
        to = down_buf.at[j]
        if j % 2 == 0:
            return [pltpu.make_async_copy(a.at[:, pl.ds(0, quarter)], to, sems.at[j, 0])]
        return [
            pltpu.make_async_copy(a.at[:, pl.ds(quarter, first)], to.at[:, pl.ds(0, first)], sems.at[j, 0]),
            pltpu.make_async_copy(b, to.at[:, pl.ds(first, quarter - first)], sems.at[j, 1]),
        ]

    start_ahead(i, copies, n)

    @pl.when(i == 0)
    def _():
        at = 0
        for ref in row_refs:
            x[at : at + ref.shape[0]] = ref[...]
            at += ref.shape[0]

    out_ref[...] = (
        jnp.dot(x[:, :hidden], down_ref[...], preferred_element_type=jnp.float32)
        + jnp.dot(x[:, hidden:], down_buf[i], preferred_element_type=jnp.float32)
    ).astype(jnp.bfloat16)


def down_project(row_pieces, down, down_far, order):
    hidden, d_model = down.shape
    n = 4
    quarter = d_model // n
    rows = sum(piece.shape[0] for piece in row_pieces)
    whole = lambda i, order: (0, 0)
    column = lambda i, order: (0, order[i])
    return pl.pallas_call(
        functools.partial(down_body, len(row_pieces)),
        grid_spec=pltpu.PrefetchScalarGridSpec(
            num_scalar_prefetch=1,
            grid=(n,),
            in_specs=[
                pl.BlockSpec((hidden, quarter), column),
                *[pl.BlockSpec(piece.shape, whole) for piece in row_pieces],
                *[pl.BlockSpec(memory_space=pltpu.MemorySpace.HBM)] * n,
            ],
            out_specs=pl.BlockSpec((rows, quarter), column),
            scratch_shapes=[
                pltpu.VMEM((rows, 2 * hidden), jnp.bfloat16),
                pltpu.VMEM((n, hidden, quarter), jnp.bfloat16),
                pltpu.SemaphoreType.DMA((n, 2)),
            ],
        ),
        out_shape=jax.ShapeDtypeStruct((rows, d_model), jnp.bfloat16),
        cost_estimate=pl.CostEstimate(
            flops=4 * rows * d_model * hidden, transcendentals=0, bytes_accessed=4 * d_model * hidden
        ),
        compiler_params=pltpu.CompilerParams(vmem_limit_bytes=40 << 20),
    )(order, down, *row_pieces, *down_far)


def shift(array, axis, size, by):
    return lax.ppermute(array, axis, [(i, (i + by) % size) for i in range(size)])


def cross(array):
    return lax.ppermute(array, ("yl", "yh"), [(0, 3), (3, 0), (1, 2), (2, 1)])


def part_of(array, parts, index, axis):
    n = array.shape[axis] // parts
    return lax.dynamic_slice_in_dim(array, index * n, n, axis)


def half_of(array, index, axis, start, stop):
    n = array.shape[axis] // 2
    return lax.dynamic_slice_in_dim(array, index * n + start, stop - start, axis)


tie = lax.optimization_barrier


def gather_x(rows):
    n = rows.shape[0] // 2
    left = shift(rows, "x", 4, 1)
    right = shift(rows, "x", 4, 3)
    far = [shift(left[:n], "x", 4, 1), shift(right[n:], "x", 4, 3)]
    return [rows, left, right], far


def shards(
    img_query,
    img_key,
    img_value,
    text_key,
    text_value,
    residual_in,
    mod_shift,
    mod_scale,
    gate_attn,
    gate_mlp,
    out_weight,
    out_bias,
    up_weight,
    up_bias,
    down_weight,
    down_bias,
):
    yl_at, yh_at, core = lax.axis_index("yl"), lax.axis_index("yh"), lax.axis_index("dp")
    rows_own, width = img_query.shape
    row_block, d_model = residual_in.shape

    vectors = jnp.stack([gate_attn, out_bias, mod_scale, mod_shift])
    order = jnp.bitwise_xor(
        jnp.array([2, 2, 2, 2, 0, 0, 0, 0], jnp.int32) * (1 - yl_at)
        + core * jnp.array([1, 1, 1, 1, 2, 2, 2, 2], jnp.int32),
        jnp.array([0, 2, 1, 3, 0, 1, 2, 3], jnp.int32),
    )
    x_at = lax.axis_index("x")
    place = jnp.concatenate(
        [(x_at + jnp.array([0, 3, 1, 2], jnp.int32)) % 4, yh_at.reshape(1).astype(jnp.int32)]
    )
    down_most = d_model // 8 * 3
    out_half = part_of(out_weight, 2, core, 1)

    q_other = shift(img_query, "yl", 2, 1)
    own = jnp.concatenate(
        [
            jnp.concatenate([img_key, text_key], axis=0),
            jnp.concatenate([img_value, text_value], axis=0),
        ],
        axis=1,
    )
    cut = -(-own.shape[0] // 32) * 16

    def around(up, down):
        return [shift(up, "z", 8, 1), shift(down, "z", 8, 7)]

    one = around(own, own)
    up_a = cross(part_of(up_weight, 4, 2 * yl_at + core, 0))
    out_l = shift(out_half, "x", 4, 1)
    out_r = shift(out_half, "x", 4, 3)
    down_first = half_of(down_weight, core, 1, 0, down_most)
    down_late = half_of(down_weight, core, 1, down_most, d_model // 2)
    one, q_other, down_first, down_late = tie((one, q_other, down_first, down_late))
    queries = jnp.where(
        yl_at == 0,
        jnp.concatenate([img_query, q_other], axis=0),
        jnp.concatenate([q_other, img_query], axis=0),
    )
    two = around(*one)
    state = attend(queries, [own], None)
    state = attend(queries, one, state)
    two, state = tie((two, state))
    three = around(*two)
    state, up_a, out_l, out_r, down_first, out_half = tie(
        (state, up_a, out_l, out_r, down_first, out_half)
    )
    down_a = cross(down_first)
    up_b = shift(up_a, "yl", 2, 1)
    out_f = shift(out_half, "x", 4, 2)
    state = attend(queries, two, state)
    three, state = tie((three, state))
    four = around(three[0][:cut], three[1][cut:])
    state = attend(queries, three, state)
    four, state = tie((four, state))
    shape = (2, 4, 2, row_block, width + HD)
    (part,) = attend(queries, four, state, shape)
    out_mine = [out_l, out_r, out_f]
    part, down_a, up_a, up_b, out_mine, down_late = tie(
        (part, down_a, up_a, up_b, out_mine, down_late)
    )
    out_mate = [shift(piece, "dp", 2, 1) for piece in out_mine]
    down_b = cross(down_late)

    parts = lax.all_to_all(
        part.reshape(8, 2 * row_block, width + HD), ("yl", "x"), split_axis=0, concat_axis=0, tiled=True
    )
    parts, out_mate, bias_far = tie((parts, out_mate, cross(up_bias)))
    proj_own, proj_away = join_project(parts, out_weight, out_mine, out_mate, order[4:], place)
    proj_away, down_b = tie((proj_away, down_b))
    proj_other = shift(proj_away, "yh", 2, 1)
    up_far = [up_a, up_b, shift(up_a, "dp", 2, 1), shift(up_b, "dp", 2, 1)]
    down_far = [down_a, down_b, shift(down_a, "dp", 2, 1), shift(down_b, "dp", 2, 1)]
    proj_other, up_far, down_far = tie((proj_other, up_far, down_far))
    stream, normed = stream_norm(proj_own, proj_other, residual_in, vectors)
    near_rows, far_rows = gather_x(normed)
    units = [
        up_project(part, up_weight, up_bias, bias_far, up_far, order[:4])
        for part in (near_rows, far_rows)
    ]
    out = down_project(units, down_weight, down_far, order[4:])
    blocks = out.reshape(4, row_block, d_model)
    total = blocks[0].astype(jnp.float32)
    total = total + shift(blocks[1], "x", 4, 3).astype(jnp.float32)
    total = total + shift(blocks[2], "x", 4, 1).astype(jnp.float32)
    total = total + shift(blocks[3], "x", 4, 2).astype(jnp.float32)
    return (stream + gate_mlp * (total + down_bias)).astype(jnp.bfloat16)


def solution(mesh):
    fine = Mesh(mesh.devices.reshape([n for _, n in FINE]), [name for name, _ in FINE])
    seq, tp = ("yl", "z"), ("yh", "x")
    tokens = P(("dp", *seq), tp)
    rows = P(("dp", *seq, *tp), None)
    in_specs = (
        tokens,
        tokens,
        tokens,
        tokens,
        tokens,
        rows,
        P("dp"),
        P("dp"),
        P("dp"),
        P("dp"),
        P(tp, None),
        P(),
        P(None, tp),
        P(tp),
        P(tp, None),
        P(),
    )
    return jax.shard_map(shards, mesh=fine, in_specs=in_specs, out_specs=rows, check_vma=False)
```

```python
import functools
import math

import jax
import jax.numpy as jnp
from jax import lax
from jax.experimental import pallas as pl
from jax.experimental.pallas import tpu as pltpu
from jax.sharding import Mesh, PartitionSpec as P

HD = 128
LOG2E = math.log2(math.e)
SCORE_TO_LOG2 = LOG2E / math.sqrt(HD)

FINE = (("yl", 2), ("z", 8), ("yh", 2), ("x", 4), ("dp", 2))


def split_three(value):
    terms = []
    for _ in range(3):
        terms.append(value.astype(jnp.bfloat16).astype(jnp.float32))
        value = value - terms[-1]
    return terms


def attend_body(pieces, block, first, last, *refs):
    q_ref = refs[0]
    kv_refs = refs[1 : 1 + pieces]
    at = 1 + pieces
    if not first:
        m_in, l_in, acc_in = refs[at : at + 3]
        at += 3
    outs = refs[at:]
    rows, width = q_ref.shape
    for j in range(rows // block):
        qs = slice(j * block, (j + 1) * block)
        stats = jnp.zeros((HD, block), jnp.float32)
        for h in range(width // HD):
            cols = slice(h * HD, (h + 1) * HD)
            v_cols = slice(width + h * HD, width + (h + 1) * HD)
            q = q_ref[qs, cols]
            scores = [
                lax.dot_general(
                    kv[:, cols], q, (((1,), (1,)), ((), ())), preferred_element_type=jnp.float32
                )
                for kv in kv_refs
            ]
            m = functools.reduce(jnp.maximum, [jnp.max(s, axis=0, keepdims=True) for s in scores])
            if not first:
                m_old = m_in[h, :, qs]
                m = jnp.maximum(m, m_old)
            den = None
            acc = None
            for s, kv in zip(scores, kv_refs):
                e = jnp.exp2((s - m) * SCORE_TO_LOG2)
                part = jnp.sum(e, axis=0, keepdims=True)
                den = part if den is None else den + part
                mixed = lax.dot_general(
                    kv[:, v_cols],
                    e.astype(jnp.bfloat16),
                    (((0,), (0,)), ((), ())),
                    preferred_element_type=jnp.float32,
                )
                acc = mixed if acc is None else acc + mixed
            if not first:
                factor = jnp.exp2((m_old - m) * SCORE_TO_LOG2)
                den = den + factor * l_in[h, :, qs]
                acc = acc + factor * acc_in[cols, qs]
            if not last:
                m_out, l_out, acc_out = outs
                m_out[h, :, qs] = m
                l_out[h, :, qs] = den
                acc_out[cols, qs] = acc
                continue
            store_part(outs[0], j, cols, (acc / den).T.astype(jnp.bfloat16))
            row = lax.broadcasted_iota(jnp.int32, (HD, block), 0)
            for k, term in enumerate(split_three(m * SCORE_TO_LOG2 + jnp.log2(den))):
                stats = jnp.where(row == 3 * h + k, term, stats)
        if last:
            store_part(outs[0], j, slice(width, width + HD), stats.T.astype(jnp.bfloat16))


def store_part(o_ref, j, cols, part):
    _, x_size, yh_size, rows, _ = o_ref.shape
    for x in range(x_size):
        for yh in range(yh_size):
            at = (yh * x_size + x) * rows
            o_ref[j, x, yh, :, cols] = part[at : at + rows]


def attend(q, pairs, state, last=None):
    rows, width = q.shape
    heads = width // HD
    first = state is None
    block = rows // last[0] if last else rows
    if last:
        out_shape = [jax.ShapeDtypeStruct(last, jnp.bfloat16)]
    else:
        stat_shape = jax.ShapeDtypeStruct((heads, 1, rows), jnp.float32)
        out_shape = [stat_shape, stat_shape, jax.ShapeDtypeStruct((width, rows), jnp.float32)]
    keys = sum(pair.shape[0] for pair in pairs)
    return pl.pallas_call(
        functools.partial(attend_body, len(pairs), block, first, bool(last)),
        out_shape=out_shape,
        cost_estimate=pl.CostEstimate(
            flops=4 * rows * keys * width,
            transcendentals=rows * keys * heads,
            bytes_accessed=2 * (rows + 2 * keys) * width,
        ),
        compiler_params=pltpu.CompilerParams(vmem_limit_bytes=24 << 20),
    )(q, *pairs, *(() if first else state))


def join_project_body(order, place, part_ref, own_w, *refs):
    mine, mate = refs[:3], refs[3:6]
    own_ref, away_ref, attended, weights, sems = refs[6:]
    i = pl.program_id(0)
    x_size = part_ref.shape[0] // 2
    rows = part_ref.shape[1] // 2
    width = part_ref.shape[2] - HD
    block = weights.shape[2]

    def copies(n):
        at = pl.multiple_of(order[n] * block, block)
        yield pltpu.make_async_copy(
            own_w.at[:, pl.ds(at, block)], weights.at[n, pl.ds(0, width)], sems.at[n, 0]
        )
        for p, piece in enumerate(mine if n < 2 else mate):
            yield pltpu.make_async_copy(
                piece.at[:, pl.ds(n % 2 * block, block)],
                weights.at[n, pl.ds((p + 1) * width, width)],
                sems.at[n, p + 1],
            )

    @pl.when(i == 0)
    def _():
        for n in range(4):
            for copy in copies(n):
                copy.start()
        for side in range(2):
            yh = place[4] if side == 0 else 1 - place[4]
            at = pl.ds(pl.multiple_of(yh * rows, rows), rows)
            for p in range(x_size):
                a = part_ref[place[p], at, :].astype(jnp.float32)
                b = part_ref[x_size + place[p], at, :].astype(jnp.float32)
                for h in range(width // HD):
                    k = width + 3 * h
                    lse_a = a[:, k : k + 1] + a[:, k + 1 : k + 2] + a[:, k + 2 : k + 3]
                    lse_b = b[:, k : k + 1] + b[:, k + 1 : k + 2] + b[:, k + 2 : k + 3]
                    share = 1.0 / (1.0 + jnp.exp2(lse_b - lse_a))
                    cols = slice(h * HD, (h + 1) * HD)
                    joined = b[:, cols] + share * (a[:, cols] - b[:, cols])
                    to = slice(p * width + h * HD, p * width + (h + 1) * HD)
                    attended[side * rows : (side + 1) * rows, to] = joined.astype(jnp.bfloat16)

    for n in range(4):

        @pl.when(i == n)
        def _(n=n):
            for copy in copies(n):
                copy.wait()
            out = jnp.dot(attended[...], weights[n], preferred_element_type=jnp.float32)
            own_ref[...] = out[:rows]
            away_ref[...] = out[rows:].astype(jnp.bfloat16)


def join_project(parts, own_w, mine, mate, order, place):
    n, both, wide = parts.shape
    width, d_model = own_w.shape
    block, rows = d_model // 4, both // 2
    out = pl.BlockSpec((rows, block), lambda i, order, place: (0, order[i]))
    far_spec = pl.BlockSpec(memory_space=pltpu.MemorySpace.HBM)
    return pl.pallas_call(
        join_project_body,
        grid_spec=pltpu.PrefetchScalarGridSpec(
            num_scalar_prefetch=2,
            grid=(4,),
            in_specs=[
                pl.BlockSpec((n, both, wide), lambda i, order, place: (0, 0, 0)),
                *[far_spec] * 7,
            ],
            out_specs=[out, out],
            scratch_shapes=[
                pltpu.VMEM((both, 4 * width), jnp.bfloat16),
                pltpu.VMEM((4, 4 * width, block), jnp.bfloat16),
                pltpu.SemaphoreType.DMA((4, 4)),
            ],
        ),
        out_shape=[
            jax.ShapeDtypeStruct((rows, d_model), jnp.float32),
            jax.ShapeDtypeStruct((rows, d_model), jnp.bfloat16),
        ],
        cost_estimate=pl.CostEstimate(
            flops=8 * both * width * d_model, transcendentals=0, bytes_accessed=8 * width * d_model
        ),
        compiler_params=pltpu.CompilerParams(vmem_limit_bytes=30 << 20),
    )(order, place, parts, own_w, *mine, *mate)


def stream_norm_body(own_ref, other_ref, residual_ref, vectors_ref, stream_ref, normed_ref):
    gate, bias, scale, shift_by = (vectors_ref[i : i + 1, :] for i in range(4))
    proj = own_ref[...] + other_ref[...].astype(jnp.float32)
    stream = residual_ref[...].astype(jnp.float32) + gate * (proj + bias)
    center = jnp.mean(stream, axis=-1, keepdims=True)
    off = stream - center
    spread = jnp.mean(off * off, axis=-1, keepdims=True)
    normed = off * lax.rsqrt(spread + 1e-06) * (1.0 + scale) + shift_by
    stream_ref[...] = stream
    normed_ref[...] = normed.astype(jnp.bfloat16)


def stream_norm(own, other, residual, vectors, block=16):
    rows, d_model = own.shape
    row = pl.BlockSpec((block, d_model), lambda i: (i, 0))
    return pl.pallas_call(
        stream_norm_body,
        grid=(rows // block,),
        in_specs=[row, row, row, pl.BlockSpec(vectors.shape, lambda i: (0, 0))],
        out_specs=[row, row],
        out_shape=[
            jax.ShapeDtypeStruct((rows, d_model), jnp.float32),
            jax.ShapeDtypeStruct((rows, d_model), jnp.bfloat16),
        ],
        cost_estimate=pl.CostEstimate(
            flops=20 * rows * d_model, transcendentals=0, bytes_accessed=14 * rows * d_model
        ),
        compiler_params=pltpu.CompilerParams(vmem_limit_bytes=8 << 20),
    )(own, other, residual, vectors)


def start_ahead(i, copies, n):
    for j in range(n):

        @pl.when(i == max(j - 2, 0))
        def _(j=j):
            for copy in copies(j):
                copy.start()

    for j in range(n):

        @pl.when(i == j)
        def _(j=j):
            for copy in copies(j):
                copy.wait()


def up_body(n_rows, order, up_ref, bias_ref, bias_far_ref, *refs):
    n = 4
    row_refs, up_far, out_ref = refs[:n_rows], refs[n_rows : n_rows + n], refs[n_rows + n]
    x, near, far, up_buf, sems = refs[n_rows + n + 1 :]
    i = pl.program_id(0)
    quarter, hidden = up_ref.shape

    start_ahead(i, lambda j: [pltpu.make_async_copy(up_far[j], up_buf.at[j], sems.at[j])], n)

    @pl.when(i == 0)
    def _():
        at = 0
        for ref in row_refs:
            x[at : at + ref.shape[0]] = ref[...]
            at += ref.shape[0]
        near[...] = jnp.broadcast_to(bias_ref[...], near.shape)
        far[...] = jnp.broadcast_to(bias_far_ref[...], far.shape)

    at = pl.multiple_of(i * quarter, quarter)
    near[...] += jnp.dot(x[:, pl.ds(at, quarter)], up_ref[...], preferred_element_type=jnp.float32)
    at = pl.multiple_of(order[i] * quarter, quarter)
    far[...] += jnp.dot(x[:, pl.ds(at, quarter)], up_buf[i], preferred_element_type=jnp.float32)

    @pl.when(i == n - 1)
    def _():
        out_ref[:, :hidden] = jax.nn.gelu(near[...], approximate=True).astype(jnp.bfloat16)
        out_ref[:, hidden:] = jax.nn.gelu(far[...], approximate=True).astype(jnp.bfloat16)


def up_project(row_pieces, up, bias, bias_far, up_far, order):
    d_model, hidden = up.shape
    n = 4
    quarter = d_model // n
    rows = sum(piece.shape[0] for piece in row_pieces)
    whole = lambda i, order: (0, 0)
    return pl.pallas_call(
        functools.partial(up_body, len(row_pieces)),
        grid_spec=pltpu.PrefetchScalarGridSpec(
            num_scalar_prefetch=1,
            grid=(n,),
            in_specs=[
                pl.BlockSpec((quarter, hidden), lambda i, order: (i, 0)),
                pl.BlockSpec((1, hidden), whole),
                pl.BlockSpec((1, hidden), whole),
                *[pl.BlockSpec(piece.shape, whole) for piece in row_pieces],
                *[pl.BlockSpec(memory_space=pltpu.MemorySpace.HBM)] * n,
            ],
            out_specs=pl.BlockSpec((rows, 2 * hidden), whole),
            scratch_shapes=[
                pltpu.VMEM((rows, d_model), jnp.bfloat16),
                pltpu.VMEM((rows, hidden), jnp.float32),
                pltpu.VMEM((rows, hidden), jnp.float32),
                pltpu.VMEM((n, quarter, hidden), jnp.bfloat16),
                pltpu.SemaphoreType.DMA((n,)),
            ],
        ),
        out_shape=jax.ShapeDtypeStruct((rows, 2 * hidden), jnp.bfloat16),
        cost_estimate=pl.CostEstimate(
            flops=4 * rows * d_model * hidden,
            transcendentals=rows * hidden * 2,
            bytes_accessed=4 * d_model * hidden,
        ),
        compiler_params=pltpu.CompilerParams(vmem_limit_bytes=40 << 20),
    )(order, up, bias.reshape(1, -1), bias_far.reshape(1, -1), *row_pieces, *up_far)


def down_body(n_rows, order, down_ref, *refs):
    n = 4
    row_refs, down_far, out_ref = refs[:n_rows], refs[n_rows : n_rows + n], refs[n_rows + n]
    x, down_buf, sems = refs[n_rows + n + 1 :]
    i = pl.program_id(0)
    hidden, quarter = down_ref.shape
    first = down_far[0].shape[1] - quarter

    def copies(j):
        a, b = down_far[j // 2 * 2 : j // 2 * 2 + 2]
        to = down_buf.at[j]
        if j % 2 == 0:
            return [pltpu.make_async_copy(a.at[:, pl.ds(0, quarter)], to, sems.at[j, 0])]
        return [
            pltpu.make_async_copy(a.at[:, pl.ds(quarter, first)], to.at[:, pl.ds(0, first)], sems.at[j, 0]),
            pltpu.make_async_copy(b, to.at[:, pl.ds(first, quarter - first)], sems.at[j, 1]),
        ]

    start_ahead(i, copies, n)

    @pl.when(i == 0)
    def _():
        at = 0
        for ref in row_refs:
            x[at : at + ref.shape[0]] = ref[...]
            at += ref.shape[0]

    out_ref[...] = (
        jnp.dot(x[:, :hidden], down_ref[...], preferred_element_type=jnp.float32)
        + jnp.dot(x[:, hidden:], down_buf[i], preferred_element_type=jnp.float32)
    ).astype(jnp.bfloat16)


def down_project(row_pieces, down, down_far, order):
    hidden, d_model = down.shape
    n = 4
    quarter = d_model // n
    rows = sum(piece.shape[0] for piece in row_pieces)
    whole = lambda i, order: (0, 0)
    column = lambda i, order: (0, order[i])
    return pl.pallas_call(
        functools.partial(down_body, len(row_pieces)),
        grid_spec=pltpu.PrefetchScalarGridSpec(
            num_scalar_prefetch=1,
            grid=(n,),
            in_specs=[
                pl.BlockSpec((hidden, quarter), column),
                *[pl.BlockSpec(piece.shape, whole) for piece in row_pieces],
                *[pl.BlockSpec(memory_space=pltpu.MemorySpace.HBM)] * n,
            ],
            out_specs=pl.BlockSpec((rows, quarter), column),
            scratch_shapes=[
                pltpu.VMEM((rows, 2 * hidden), jnp.bfloat16),
                pltpu.VMEM((n, hidden, quarter), jnp.bfloat16),
                pltpu.SemaphoreType.DMA((n, 2)),
            ],
        ),
        out_shape=jax.ShapeDtypeStruct((rows, d_model), jnp.bfloat16),
        cost_estimate=pl.CostEstimate(
            flops=4 * rows * d_model * hidden, transcendentals=0, bytes_accessed=4 * d_model * hidden
        ),
        compiler_params=pltpu.CompilerParams(vmem_limit_bytes=40 << 20),
    )(order, down, *row_pieces, *down_far)


def shift(array, axis, size, by):
    return lax.ppermute(array, axis, [(i, (i + by) % size) for i in range(size)])


def cross(array):
    return lax.ppermute(array, ("yl", "yh"), [(0, 3), (3, 0), (1, 2), (2, 1)])


def part_of(array, parts, index, axis):
    n = array.shape[axis] // parts
    return lax.dynamic_slice_in_dim(array, index * n, n, axis)


def half_of(array, index, axis, start, stop):
    n = array.shape[axis] // 2
    return lax.dynamic_slice_in_dim(array, index * n + start, stop - start, axis)


tie = lax.optimization_barrier


def gather_x(rows, beside):
    n = rows.shape[0] // 2
    left = shift(rows, "x", 4, 1)
    right = shift(rows, "x", 4, 3)
    left, right, beside = tie((left, right, beside))
    far = [shift(left[:n], "x", 4, 1), shift(right[n:], "x", 4, 3)]
    return [rows, left, right], far, beside


def shards(
    img_query,
    img_key,
    img_value,
    text_key,
    text_value,
    residual_in,
    mod_shift,
    mod_scale,
    gate_attn,
    gate_mlp,
    out_weight,
    out_bias,
    up_weight,
    up_bias,
    down_weight,
    down_bias,
):
    yl_at, yh_at, core = lax.axis_index("yl"), lax.axis_index("yh"), lax.axis_index("dp")
    rows_own, width = img_query.shape
    row_block, d_model = residual_in.shape

    vectors = jnp.stack([gate_attn, out_bias, mod_scale, mod_shift])
    order = jnp.bitwise_xor(
        jnp.array([2, 2, 2, 2, 0, 0, 0, 0], jnp.int32) * (1 - yl_at)
        + core * jnp.array([1, 1, 1, 1, 2, 2, 2, 2], jnp.int32),
        jnp.array([0, 2, 1, 3, 0, 1, 2, 3], jnp.int32),
    )
    x_at = lax.axis_index("x")
    place = jnp.concatenate(
        [(x_at + jnp.array([0, 3, 1, 2], jnp.int32)) % 4, yh_at.reshape(1).astype(jnp.int32)]
    )
    down_most = d_model // 3
    out_half = part_of(out_weight, 2, core, 1)

    q_other = shift(img_query, "yl", 2, 1)
    own = jnp.concatenate(
        [
            jnp.concatenate([img_key, text_key], axis=0),
            jnp.concatenate([img_value, text_value], axis=0),
        ],
        axis=1,
    )
    cut = -(-own.shape[0] // 32) * 16

    def around(up, down):
        return [shift(up, "z", 8, 1), shift(down, "z", 8, 7)]

    one = around(own, own)
    up_a = cross(part_of(up_weight, 4, 2 * yl_at + core, 0))
    out_l = shift(out_half, "x", 4, 1)
    out_r = shift(out_half, "x", 4, 3)
    down_first = half_of(down_weight, core, 1, 0, down_most)
    down_late = half_of(down_weight, core, 1, down_most, d_model // 2)
    one, q_other, down_first, down_late = tie((one, q_other, down_first, down_late))
    queries = jnp.where(
        yl_at == 0,
        jnp.concatenate([img_query, q_other], axis=0),
        jnp.concatenate([q_other, img_query], axis=0),
    )
    two = around(*one)
    state = attend(queries, [own], None)
    state = attend(queries, one, state)
    two, state = tie((two, state))
    three = around(*two)
    state, up_a, out_l, out_r, down_first, out_half = tie(
        (state, up_a, out_l, out_r, down_first, out_half)
    )
    down_a = cross(down_first)
    up_b = shift(up_a, "yl", 2, 1)
    out_f = shift(out_half, "x", 4, 2)
    state = attend(queries, two, state)
    three, state = tie((three, state))
    four = around(three[0][:cut], three[1][cut:])
    state = attend(queries, three, state)
    four, state = tie((four, state))
    shape = (2, 4, 2, row_block, width + HD)
    (part,) = attend(queries, four, state, shape)
    out_mine = [out_l, out_r, out_f]
    part, down_a, up_a, up_b, out_mine, down_late = tie(
        (part, down_a, up_a, up_b, out_mine, down_late)
    )
    out_mate = [shift(piece, "dp", 2, 1) for piece in out_mine]
    down_b = cross(down_late)

    parts = lax.all_to_all(
        part.reshape(8, 2 * row_block, width + HD), ("yl", "x"), split_axis=0, concat_axis=0, tiled=True
    )
    parts, out_mate = tie((parts, out_mate))
    proj_own, proj_away = join_project(parts, out_weight, out_mine, out_mate, order[4:], place)
    proj_away, down_b = tie((proj_away, down_b))
    proj_other = shift(proj_away, "yh", 2, 1)
    up_far = [up_a, up_b, shift(up_a, "dp", 2, 1), shift(up_b, "dp", 2, 1)]
    down_far = [down_a, down_b, shift(down_a, "dp", 2, 1), shift(down_b, "dp", 2, 1)]
    proj_other, up_far, down_far = tie((proj_other, up_far, down_far))
    stream, normed = stream_norm(proj_own, proj_other, residual_in, vectors)
    near_rows, far_rows, bias_far = gather_x(normed, cross(up_bias))
    units = [
        up_project(part, up_weight, up_bias, bias_far, up_far, order[:4])
        for part in (near_rows, far_rows)
    ]
    out = down_project(units, down_weight, down_far, order[4:])
    blocks = out.reshape(4, row_block, d_model)
    total = blocks[0].astype(jnp.float32)
    total = total + shift(blocks[1], "x", 4, 3).astype(jnp.float32)
    total = total + shift(blocks[2], "x", 4, 1).astype(jnp.float32)
    total = total + shift(blocks[3], "x", 4, 2).astype(jnp.float32)
    return (stream + gate_mlp * (total + down_bias)).astype(jnp.bfloat16)


def solution(mesh):
    fine = Mesh(mesh.devices.reshape([n for _, n in FINE]), [name for name, _ in FINE])
    seq, tp = ("yl", "z"), ("yh", "x")
    tokens = P(("dp", *seq), tp)
    rows = P(("dp", *seq, *tp), None)
    in_specs = (
        tokens,
        tokens,
        tokens,
        tokens,
        tokens,
        rows,
        P("dp"),
        P("dp"),
        P("dp"),
        P("dp"),
        P(tp, None),
        P(),
        P(None, tp),
        P(tp),
        P(tp, None),
        P(),
    )
    return jax.shard_map(shards, mesh=fine, in_specs=in_specs, out_specs=rows, check_vma=False)
```
